256 devices in a mesh: ctx: 64 (over z, x_hi, y), tp: 4 (over x_lo, core).
Axes of the slice: x: 4 (x_hi: 2, x_lo: 2; x = x_hi * 2 + x_lo), y: 4, z: 8, core: 2. Of those that a mesh axis runs over, the one named last changes fastest.
Arguments:
- queries: bfloat16 [9216, 3072], P('ctx', 'tp'), may hold values from -8 to 8
- keys: bfloat16 [9216, 3072], P('ctx', 'tp'), may hold values from -8 to 8
- values: bfloat16 [9216, 3072], P('ctx', 'tp'), may hold values from -6 to 6
- positions: int32 [9216], P('ctx'), may hold values from 0 to 9215, as said below
- lambda_vecs: float32 [4, 12, 128], P(None, 'tp'), may hold values from -0.6 to 0.6
- head_gain: float32 [3072], P('tp'), may hold values from 0.5 to 1.5
- out_weight: bfloat16 [3072, 5120], P('tp'), may hold values from -0.109375 to 0.109375
- residual: bfloat16 [9216, 5120], P('ctx', 'tp'), may hold values from -3 to 3
Outputs:
- mixed: bfloat16 [9216, 5120], P('ctx', 'tp')
The draws below stay inside these ranges and needn't reach their ends.
Inputs may be any that keep to these rules, and one draw needn't show every extreme that they name: Each aligned run of 72 rows holds 72 consecutive positions in increasing order; the runs' first positions are the multiples of 72, each once.
All inputs are finite; a program needn't handle non-finite values.
Results may differ from the reference program's by a relative error of at most 0.012.
Values may be sent and summed in bfloat16 or wider, within the bound.
No kernel may reach another device: no remote copies, remote signals or barrier semaphores. Data moves between devices by JAX's collectives and lax.ppermute only.
A program may use at most 192 MiB of HBM per device.

```python
import math
import jax
import jax.numpy as jnp
from jax import lax

D = 5120
HEAD_DIM = 128
HEADS = 12
TOKENS = 9216
BLOCK = 72


def drawn_rows(key, salt):
    width = HEADS * 2 * HEAD_DIM
    local_key = jax.random.fold_in(key, salt)
    return jnp.clip(jax.random.normal(local_key, (TOKENS, width), jnp.float32), -6.0, 6.0)


def draw_queries(key, part):
    result = drawn_rows(key, 3)
    return result.astype(jnp.bfloat16)


def draw_keys(key, part):
    result = drawn_rows(key, 5)
    return result.astype(jnp.bfloat16)


def draw_positions(key, part):
    block_count = TOKENS // BLOCK
    order = jax.random.permutation(jax.random.fold_in(key, 23), block_count).astype(jnp.int32)
    row_index = jnp.arange(TOKENS, dtype=jnp.int32)
    return (order[row_index // BLOCK] * BLOCK + row_index % BLOCK).astype(jnp.int32)


def level_of(stream_key, dims, shards, least, high):
    def one(dim, shards_of):
        draws = jax.random.uniform(jax.random.fold_in(jax.random.fold_in(stream_key, 6), dim), (shards_of,), jnp.float32, least / len(shards), high / len(shards))
        return jnp.repeat(jnp.exp(draws), dims[dim] // shards_of).reshape((-1,) + (1,) * (len(dims) - dim - 1))

    factor_of = one(*shards[0])
    for cut in shards[1:]:
        factor_of = factor_of * one(*cut)
    return factor_of


def bell_draw(stream_key, extent, scale, limit, cuts=(), kind=jnp.bfloat16):
    level = level_of(stream_key, extent, cuts, -0.22, 0.18) if cuts else 1.0
    values = jax.random.normal(stream_key, extent, jnp.float32) * scale * level
    return jnp.minimum(jnp.maximum(values, -limit), limit).astype(kind)


def setup_inputs(seed: int = 0) -> dict:
    splits = jax.random.split(jax.random.key(seed), 9)
    queries = draw_queries(jax.random.fold_in(splits[8], 71), 0)
    keys = draw_keys(jax.random.fold_in(splits[8], 71), 0)
    values = bell_draw(splits[2], (TOKENS, HEADS * 2 * HEAD_DIM), 1.0, 6.0, ((0, 64), (1, 4)))
    positions = draw_positions(jax.random.fold_in(splits[8], 71), 0)
    lambda_vecs = bell_draw(splits[4], (4, HEADS, HEAD_DIM), 0.15, 0.6, ((1, 4),), jnp.float32)
    head_gain = jnp.clip(1.0 + 0.1 * jax.random.normal(splits[5], (HEADS * 2 * HEAD_DIM,), jnp.float32), 0.5, 1.5)
    out_weight = bell_draw(splits[6], (HEADS * 2 * HEAD_DIM, D), (HEADS * 2 * HEAD_DIM) ** -0.5, 0.109375, ((0, 4),))
    residual = bell_draw(splits[7], (TOKENS, D), 0.5, 3.0, ((0, 64), (1, 4)))
    return {"queries": queries, "keys": keys, "values": values, "positions": positions, "lambda_vecs": lambda_vecs, "head_gain": head_gain, "out_weight": out_weight, "residual": residual}


lambda_init = 0.2
out_factor = 0.8
norm_eps = 1e-05

def reference(queries, keys, values, positions, lambda_vecs, head_gain, out_weight, residual):
    score_scale = 1.0 / math.sqrt(HEAD_DIM)
    lambda_head = jnp.exp(lax.optimization_barrier(jnp.sum(lambda_vecs[0] * lambda_vecs[1], -1))) - jnp.exp(lax.optimization_barrier(jnp.sum(lambda_vecs[2] * lambda_vecs[3], -1))) + lambda_init
    key_heads = keys.reshape(TOKENS, HEADS, 2, HEAD_DIM).astype(jnp.float32)
    value_heads = values.reshape(TOKENS, HEADS, 2 * HEAD_DIM).astype(jnp.float32)
    gain_heads = head_gain.reshape(HEADS, 1, 2 * HEAD_DIM)
    query_block = math.gcd(TOKENS, 256)

    def one_block(block_index):
        start = (block_index * query_block).astype(jnp.int32)
        query_rows = lax.dynamic_slice_in_dim(queries, start, query_block, 0)
        query_rows = query_rows.reshape(query_block, HEADS, 2, HEAD_DIM).astype(jnp.float32)
        row_positions = lax.dynamic_slice_in_dim(positions, start, query_block, 0)
        allowed = positions[None, :] <= row_positions[:, None]
        scores = jnp.einsum('ihad,jhad->ahij', query_rows, key_heads) * score_scale
        scores = jnp.where(allowed, scores, -jnp.inf)
        highest = lax.optimization_barrier(jnp.max(scores, -1, keepdims=True))
        expo = jnp.where(allowed, jnp.exp(scores - highest), 0.0)
        total = lax.optimization_barrier(jnp.sum(expo, -1))
        weights = expo.astype(jnp.bfloat16).astype(jnp.float32)
        attn = jnp.einsum('ahij,jhe->ahie', weights, value_heads) / total[..., None]
        diff = attn[0] - lambda_head[:, None, None] * attn[1]
        mean_square = lax.optimization_barrier(jnp.mean(diff * diff, -1, keepdims=True))
        normed = out_factor * diff / jnp.sqrt(mean_square + norm_eps) * gain_heads
        return jnp.transpose(normed, (1, 0, 2)).reshape(query_block, HEADS * 2 * HEAD_DIM).astype(jnp.bfloat16)
    normed_all = lax.map(one_block, jnp.arange(TOKENS // query_block, dtype=jnp.int32))
    normed_all = normed_all.reshape(TOKENS, HEADS * 2 * HEAD_DIM)
    projected = jnp.dot(normed_all, out_weight, preferred_element_type=jnp.float32)
    return (projected + residual.astype(jnp.float32)).astype(jnp.bfloat16)
```

```python
import math

import jax
import jax.numpy as jnp
from jax import lax
from jax.experimental import pallas as pl
from jax.experimental.pallas import tpu as pltpu
from jax.sharding import Mesh, PartitionSpec as P

lambda_init = 0.2
out_factor = 0.8
norm_eps = 1e-05

HD = 128
RUN = 72
NEG = -1e30
FLOOR = -1e29
f32 = jnp.float32
bf16 = jnp.bfloat16


def shift(x, axis, size, step):
    return lax.ppermute(x, axis, [(i, (i + step) % size) for i in range(size)])


def attend_kernel(rows, slots, qb, kb, *refs):
    nq = slots // 2
    q_refs = refs[:nq]
    kv_ref = refs[nq]
    o_refs = refs[nq + 1 : 2 * nq + 1]
    lse_ref = refs[2 * nq + 1]
    q_s, k_s, v_s, lse_s = refs[2 * nq + 2 :]
    head = pl.program_id(0)
    keys = kv_ref.shape[0] * rows
    tile = 2 * rows
    for z in range(kv_ref.shape[0]):
        k_s[z * rows : (z + 1) * rows, :] = kv_ref[z, :rows, :]
        v_s[z * rows : (z + 1) * rows, :] = kv_ref[z, rows : 2 * rows, :]
    for i in range(nq):
        for d in range(2):
            q_s[(2 * i + d) * rows : (2 * i + d + 1) * rows, :] = q_refs[i][d, :rows, :]
    col = lax.broadcasted_iota(jnp.int32, (1, keys), 1)
    kpos = lax.rem(col, RUN)
    for b in range(keys // RUN):
        kpos = kpos + jnp.where(lax.div(col, RUN) == b, kb[b] * RUN, 0)
    row = lax.broadcasted_iota(jnp.int32, (tile, 1), 0)
    lane = lax.broadcasted_iota(jnp.int32, (tile, HD), 1)
    scale = math.log2(math.e) / math.sqrt(HD)

    @pl.when(head == 0)
    def _():
        lse_s[...] = jnp.zeros_like(lse_s)

    for t in range(nq):
        qpos = lax.rem(row, RUN)
        for b in range(tile // RUN):
            qpos = qpos + jnp.where(lax.div(row, RUN) == b, qb[t * (tile // RUN) + b] * RUN, 0)
        allowed = kpos <= qpos
        stats = lse_s[t * tile : (t + 1) * tile, :]
        for a in range(2):
            s = lax.dot_general(
                q_s[t * tile : (t + 1) * tile, a * HD : (a + 1) * HD],
                k_s[:, a * HD : (a + 1) * HD],
                (((1,), (1,)), ((), ())),
                preferred_element_type=f32,
            )
            s = jnp.where(allowed, s, NEG)
            m = jnp.maximum(jnp.max(s, -1, keepdims=True), FLOOR) * scale
            p = jnp.exp2(s * scale - m)
            total = jnp.sum(p, -1, keepdims=True)
            num = jnp.dot(p.astype(bf16), v_s[...], preferred_element_type=f32)
            some = total > 0.0
            safe = jnp.where(some, total, 1.0)
            o_refs[t][:, a * 2 * HD : (a + 1) * 2 * HD] = num * (1.0 / safe)
            lse = jnp.where(some, m + jnp.log2(safe), NEG)
            stats = jnp.where(lane == head * 2 + a, lse, stats)
        lse_s[t * tile : (t + 1) * tile, :] = stats

    @pl.when(head == pl.num_programs(0) - 1)
    def _():
        lse_ref[...] = jnp.transpose(lse_s[...])[: lse_ref.shape[0], :]


def attend(q_parts, kv, qb, kb, rows, heads):
    nq = len(q_parts)
    slots = 2 * nq
    zs = kv.shape[0]
    pad = q_parts[0].shape[1]
    return pl.pallas_call(
        lambda *r: attend_kernel(rows, slots, *r),
        out_shape=[jax.ShapeDtypeStruct((2 * rows, heads * 4 * HD), f32)] * nq
        + [jax.ShapeDtypeStruct((8, slots * rows), f32)],
        grid_spec=pltpu.PrefetchScalarGridSpec(
            num_scalar_prefetch=2,
            grid=(heads,),
            in_specs=[pl.BlockSpec((2, pad, 2 * HD), lambda h, *_: (0, 0, h))] * nq
            + [pl.BlockSpec((zs, kv.shape[1], 2 * HD), lambda h, *_: (0, 0, h))],
            out_specs=[pl.BlockSpec((2 * rows, 4 * HD), lambda h, *_: (0, h))] * nq
            + [pl.BlockSpec((8, slots * rows), lambda h, *_: (0, 0))],
            scratch_shapes=[
                pltpu.VMEM((slots * rows, 2 * HD), bf16),
                pltpu.VMEM((zs * rows, 2 * HD), bf16),
                pltpu.VMEM((zs * rows, 2 * HD), bf16),
                pltpu.VMEM((slots * rows, HD), f32),
            ],
        ),
        compiler_params=pltpu.CompilerParams(vmem_limit_bytes=56 << 20),
        name="attend",
    )(qb, kb, *q_parts, kv)


def weigh_kernel(heads, lam_ref, lse_ref, all_ref, *refs):
    nq = len(refs) // 2
    tile = refs[0].shape[0]
    w = jnp.exp2(lse_ref[...] - all_ref[...])
    w = jnp.concatenate([w, jnp.zeros((HD - w.shape[0], w.shape[1]), f32)], 0)
    w = jnp.transpose(w)
    for i in range(nq):
        for h in range(heads):
            w1 = w[i * tile : (i + 1) * tile, 2 * h : 2 * h + 1]
            w2 = w[i * tile : (i + 1) * tile, 2 * h + 1 : 2 * h + 2] * lam_ref[h]
            o1 = refs[i][:, h * 4 * HD : h * 4 * HD + 2 * HD]
            o2 = refs[i][:, h * 4 * HD + 2 * HD : (h + 1) * 4 * HD]
            refs[nq + i][:, h * 2 * HD : (h + 1) * 2 * HD] = (w1 * o1 - w2 * o2).astype(bf16)


def weigh(lam, lse, lse_all, outs, heads):
    nq = len(outs)
    vm = pl.BlockSpec(memory_space=pltpu.VMEM)
    return pl.pallas_call(
        lambda *r: weigh_kernel(heads, *r),
        out_shape=[jax.ShapeDtypeStruct((outs[0].shape[0], heads * 2 * HD), bf16)] * nq,
        in_specs=[pl.BlockSpec(memory_space=pltpu.SMEM), vm, vm] + [vm] * nq,
        out_specs=[vm] * nq,
        compiler_params=pltpu.CompilerParams(vmem_limit_bytes=48 << 20),
        name="weigh",
    )(lam, lse, lse_all, *outs)


def logsum(parts):
    top = parts[0]
    for p in parts[1:]:
        top = jnp.maximum(top, p)
    top = jnp.maximum(top, FLOOR)
    total = 0.0
    for p in parts:
        total = total + jnp.exp2(p - top)
    return jnp.where(total > 0.0, top + jnp.log2(jnp.maximum(total, 1e-37)), NEG)


def per_device(sizes, queries, keys, values, positions, lambda_vecs, head_gain, out_weight, residual):
    nz, nh, ny, nl, nc = sizes
    rows, width = queries.shape
    heads = lambda_vecs.shape[1]
    block = (positions[::RUN] // RUN).astype(bf16)
    ids = jnp.broadcast_to(jnp.pad(block, (0, width - block.shape[0]))[None, :], (16, width))

    kv = lax.all_gather(jnp.concatenate([keys, values, ids], 0), "z", axis=0, tiled=False)
    kb = kv[:, 2 * rows, : rows // RUN].astype(jnp.int32).reshape(-1)

    q_mine = jnp.concatenate([queries, ids], 0)
    q_pair = jnp.stack([q_mine, shift(q_mine, "h", nh, 1)], 0)
    q_parts = [q_pair] + [shift(q_pair, "y", ny, d) for d in range(1, ny)]
    qb = jnp.stack([q[:, rows, : rows // RUN] for q in q_parts], 0).astype(jnp.int32).reshape(-1)

    *outs, lse = attend(q_parts, kv, qb, kb, rows, heads)

    tile = 2 * rows
    own = [lse[:, i * tile : (i + 1) * tile] for i in range(ny)]
    back = [own[0]] + [shift(own[i], "y", ny, -i) for i in range(1, ny)]
    mine = logsum(back)
    swapped = jnp.concatenate([mine[:, rows:], mine[:, :rows]], 1)
    other = shift(swapped, "h", nh, 1)
    mine = logsum([mine, other])
    everyone = jnp.concatenate([mine] + [shift(mine, "y", ny, i) for i in range(1, ny)], 1)

    lam = (
        jnp.exp(jnp.sum(lambda_vecs[0] * lambda_vecs[1], -1))
        - jnp.exp(jnp.sum(lambda_vecs[2] * lambda_vecs[3], -1))
        + lambda_init
    )
    parts = weigh(lam, lse, everyone, outs, heads)

    got = [shift(parts[i], "y", ny, -i) for i in range(1, ny)]
    total = parts[0].astype(f32)
    for g in got:
        total = total + g.astype(f32)
    away = shift(total[rows:].astype(bf16), "h", nh, 1)
    diff = (total[:rows] + away.astype(f32)).reshape(rows, heads, 2 * HD)
    mean_square = jnp.mean(diff * diff, -1, keepdims=True)
    normed = out_factor * diff / jnp.sqrt(mean_square + norm_eps) * head_gain.reshape(1, heads, 2 * HD)
    normed = normed.reshape(rows, width).astype(bf16)

    share = jnp.dot(normed, out_weight, preferred_element_type=f32).astype(bf16)
    share = share.reshape(rows, nl, nc, -1)
    l, c = lax.axis_index("l"), lax.axis_index("c")
    keep = lax.dynamic_index_in_dim(share, c, 2, False)
    send = lax.dynamic_index_in_dim(share, 1 - c, 2, False)
    both = keep.astype(f32) + shift(send, "c", nc, 1).astype(f32)
    keep = lax.dynamic_index_in_dim(both, l, 1, False)
    send = lax.dynamic_index_in_dim(both, 1 - l, 1, False).astype(bf16)
    projected = keep + shift(send, "l", nl, 1).astype(f32)
    return (projected + residual.astype(f32)).astype(bf16)


def solution(mesh):
    sizes = (8, 2, 4, 2, 2)
    fine = Mesh(mesh.devices.reshape(sizes), ("z", "h", "y", "l", "c"))
    ctx, tp = ("z", "h", "y"), ("l", "c")
    placed = (
        P(ctx, tp),
        P(ctx, tp),
        P(ctx, tp),
        P(ctx),
        P(None, tp, None),
        P(tp),
        P(tp, None),
        P(ctx, tp),
    )
    return jax.shard_map(
        lambda *a: per_device(sizes, *a), mesh=fine, in_specs=placed, out_specs=P(ctx, tp), check_vma=False
    )
```

```python
import math

import jax
import jax.numpy as jnp
from jax import lax
from jax.experimental import pallas as pl
from jax.experimental.pallas import tpu as pltpu
from jax.sharding import Mesh, PartitionSpec as P

lambda_init = 0.2
out_factor = 0.8
norm_eps = 1e-05

HD = 128
RUN = 72
TILE = 4
NEG = -1e30
FLOOR = -1e29
f32 = jnp.float32
bf16 = jnp.bfloat16


def attend_kernel(rows, qb, kb, *refs):
    q_refs, (kv_ref, o_ref, lse_ref) = refs[:-11], refs[-11:-8]
    q3, k3, v3, q_s, k_s, v_s, lse_s, order = refs[-8:]
    head = pl.program_id(0)
    blocks = q3.shape[0]
    per = rows // RUN
    tile = TILE * RUN
    tiles = blocks // TILE
    scale = math.log2(math.e) / math.sqrt(HD)

    @pl.when(head == 0)
    def _():
        lse_s[...] = jnp.zeros_like(lse_s)
        for i in range(blocks):
            rk = jnp.int32(0)
            rq = jnp.int32(0)
            for j in range(blocks):
                rk = rk + (kb[j] < kb[i]).astype(jnp.int32)
                rq = rq + (qb[j] < qb[i]).astype(jnp.int32)
            order[0, i] = rk
            order[1, rk] = kb[i]
            order[2, i] = rq
            order[3, rq] = i
            order[4, rq] = qb[i]
        for t in range(tiles):
            last = order[4, t * TILE + TILE - 1]
            need = jnp.int32(0)
            for j in range(blocks):
                need = need + (kb[j] <= last).astype(jnp.int32)
            order[5, t] = lax.div(need + (TILE - 1), TILE)

    for i in range(blocks):
        z, d = i // per, i % per
        r = order[0, i]
        k3[r] = kv_ref[z, d * RUN : (d + 1) * RUN, :]
        v3[r] = kv_ref[z, rows + d * RUN : rows + (d + 1) * RUN, :]
        p, e = z // 2, z % 2
        q3[order[2, i]] = q_refs[p][e, d * RUN : (d + 1) * RUN, :]
    for i in range(blocks):
        q_s[i * RUN : (i + 1) * RUN, :] = q3[i]
        k_s[i * RUN : (i + 1) * RUN, :] = k3[i]
        v_s[i * RUN : (i + 1) * RUN, :] = v3[i]

    col = lax.broadcasted_iota(jnp.int32, (1, blocks * RUN), 1)
    kpos = lax.rem(col, RUN)
    for i in range(blocks):
        kpos = kpos + jnp.where(lax.div(col, RUN) == i, order[1, i] * RUN, 0)
    row = lax.broadcasted_iota(jnp.int32, (tile, 1), 0)
    lane = lax.broadcasted_iota(jnp.int32, (RUN, HD), 1)

    def one_tile(t, carry):
        need = order[5, t]
        start = pl.multiple_of(t * tile, tile)
        qpos = lax.rem(row, RUN)
        for i in range(TILE):
            qpos = qpos + jnp.where(lax.div(row, RUN) == i, order[4, t * TILE + i] * RUN, 0)

        def put(a, num, lse):
            for i in range(TILE):
                g = order[3, t * TILE + i]
                o_ref[g, :, a * 2 * HD : (a + 1) * 2 * HD] = num[i * RUN : (i + 1) * RUN]
                lse_s[g] = jnp.where(lane == head * 2 + a, lse[i * RUN : (i + 1) * RUN], lse_s[g])

        for n in range(1, tiles + 1):

            @pl.when(need == n)
            def _(n=n):
                allowed = kpos[:, : n * tile] <= qpos
                for a in range(2):
                    s = lax.dot_general(
                        q_s[pl.ds(start, tile), a * HD : (a + 1) * HD],
                        k_s[: n * tile, a * HD : (a + 1) * HD],
                        (((1,), (1,)), ((), ())),
                        preferred_element_type=f32,
                    )
                    s = jnp.where(allowed, s, NEG)
                    m = jnp.maximum(jnp.max(s, -1, keepdims=True), FLOOR) * scale
                    p = jnp.exp2(s * scale - m)
                    total = jnp.sum(p, -1, keepdims=True)
                    num = jnp.dot(p.astype(bf16), v_s[: n * tile, :], preferred_element_type=f32)
                    some = total > 0.0
                    safe = jnp.where(some, total, 1.0)
                    put(a, num * (1.0 / safe), jnp.where(some, m + jnp.log2(safe), NEG))

        @pl.when(need == 0)
        def _():
            for a in range(2):
                put(a, jnp.zeros((tile, 2 * HD), f32), jnp.full((tile, 1), NEG, f32))

        return carry

    lax.fori_loop(0, tiles, one_tile, 0)

    @pl.when(head == pl.num_programs(0) - 1)
    def _():
        lse_ref[...] = jnp.transpose(lse_s[...].reshape(blocks * RUN, HD))[: lse_ref.shape[0], :]


def attend(q_parts, kv, qb, kb, rows, heads):
    nq = len(q_parts)
    blocks = 2 * nq * rows // RUN
    zs = kv.shape[0]
    pad = q_parts[0].shape[1]
    return pl.pallas_call(
        lambda *r: attend_kernel(rows, *r),
        out_shape=[
            jax.ShapeDtypeStruct((blocks, RUN, heads * 4 * HD), f32),
            jax.ShapeDtypeStruct((8, blocks * RUN), f32),
        ],
        grid_spec=pltpu.PrefetchScalarGridSpec(
            num_scalar_prefetch=2,
            grid=(heads,),
            in_specs=[pl.BlockSpec((2, pad, 2 * HD), lambda h, *_: (0, 0, h))] * nq
            + [pl.BlockSpec((zs, kv.shape[1], 2 * HD), lambda h, *_: (0, 0, h))],
            out_specs=[
                pl.BlockSpec((blocks, RUN, 4 * HD), lambda h, *_: (0, 0, h)),
                pl.BlockSpec((8, blocks * RUN), lambda h, *_: (0, 0)),
            ],
            scratch_shapes=[pltpu.VMEM((blocks, RUN, 2 * HD), bf16)] * 3
            + [pltpu.VMEM((blocks * RUN, 2 * HD), bf16)] * 3
            + [pltpu.VMEM((blocks, RUN, HD), f32), pltpu.SMEM((6, 128), jnp.int32)],
        ),
        compiler_params=pltpu.CompilerParams(vmem_limit_bytes=40 << 20),
        name="attend",
    )(qb, kb, *q_parts, kv)


def weigh_kernel(heads, place, lam, lse_ref, all_ref, o_ref, out_ref, w_s):
    s = pl.program_id(0)
    rows = out_ref.shape[1]

    @pl.when(s == 0)
    def _():
        w = jnp.exp2(lse_ref[...] - all_ref[...])
        w = jnp.concatenate([w, jnp.zeros((HD - w.shape[0], w.shape[1]), f32)], 0)
        w_s[...] = jnp.transpose(w)

    w = w_s[pl.ds(pl.multiple_of(s * rows, rows), rows), :]
    for h in range(heads):
        w1 = w[:, 2 * h : 2 * h + 1]
        w2 = w[:, 2 * h + 1 : 2 * h + 2] * lam[h]
        o1 = o_ref[:, :, h * 4 * HD : h * 4 * HD + 2 * HD].reshape(rows, 2 * HD)
        o2 = o_ref[:, :, h * 4 * HD + 2 * HD : (h + 1) * 4 * HD].reshape(rows, 2 * HD)
        out_ref[0, :, h * 2 * HD : (h + 1) * 2 * HD] = (w1 * o1 - w2 * o2).astype(bf16)


def weigh(place, lam, lse, lse_all, o, rows, heads):
    slots = lse.shape[1] // rows
    return pl.pallas_call(
        lambda *r: weigh_kernel(heads, *r),
        out_shape=jax.ShapeDtypeStruct((slots, rows, heads * 2 * HD), bf16),
        grid_spec=pltpu.PrefetchScalarGridSpec(
            num_scalar_prefetch=2,
            grid=(slots,),
            in_specs=[pl.BlockSpec(lse.shape, lambda s, *_: (0, 0))] * 2
            + [pl.BlockSpec((rows // RUN, RUN, heads * 4 * HD), lambda s, *_: (s, 0, 0))],
            out_specs=pl.BlockSpec((1, rows, heads * 2 * HD), lambda s, place, lam: (place[s], 0, 0)),
            scratch_shapes=[pltpu.VMEM((slots * rows, HD), f32)],
        ),
        compiler_params=pltpu.CompilerParams(vmem_limit_bytes=16 << 20),
        name="weigh",
    )(place, lam, lse, lse_all, o)


def logsum(a, b):
    top = jnp.maximum(a, b)
    return top + jnp.log2(jnp.exp2(a - top) + jnp.exp2(b - top))


def reorder(x, rows, mask):
    slots = x.shape[1] // rows
    return jnp.concatenate([x[:, (s ^ mask) * rows : ((s ^ mask) + 1) * rows] for s in range(slots)], 1)


def swap(x, axis, size, mask):
    return lax.ppermute(x, axis, [(i, i ^ mask) for i in range(size)])


def per_device(sizes, queries, keys, values, positions, lambda_vecs, head_gain, out_weight, residual):
    nz, nh, ny, nl, nc = sizes
    rows, width = queries.shape
    heads = lambda_vecs.shape[1]
    lane = lax.broadcasted_iota(jnp.int32, (16, width), 1)
    ids = jnp.where(lane == 0, positions[0] // RUN, positions[RUN] // RUN).astype(bf16)

    kv = lax.all_gather(jnp.concatenate([keys, values, ids], 0), "z", axis=0, tiled=False)
    kb = kv[:, 2 * rows, : rows // RUN].astype(jnp.int32).reshape(-1)

    q_mine = jnp.concatenate([queries, ids], 0)
    q_pair = jnp.stack([q_mine, swap(q_mine, "h", nh, 1)], 0)
    q_parts = [q_pair] + [swap(q_pair, "y", ny, d) for d in range(1, ny)]
    qb = jnp.stack([q[:, rows, : rows // RUN] for q in q_parts], 0).astype(jnp.int32).reshape(-1)

    l, c = lax.axis_index("l"), lax.axis_index("c")
    w4 = out_weight.reshape(width, nl, nc, -1)
    w_keep = lax.dynamic_index_in_dim(w4, c, 2, False)
    w_away = swap(lax.dynamic_index_in_dim(w4, 1 - c, 2, False), "c", nc, 1)
    w_both = jnp.concatenate([w_keep, w_away], 0)
    w_mine = lax.dynamic_index_in_dim(w_both, l, 1, False)
    w_other = lax.dynamic_index_in_dim(w_both, 1 - l, 1, False)

    o, lse = attend(q_parts, kv, qb, kb, rows, heads)

    whole = lse
    for axis, size, mask, slot in (("h", nh, 1, 1), ("y", ny, 1, 2), ("y", ny, 3, 6)):
        whole = logsum(whole, reorder(swap(whole, axis, size, mask), rows, slot))

    lam = (
        jnp.exp(jnp.sum(lambda_vecs[0] * lambda_vecs[1], -1))
        - jnp.exp(jnp.sum(lambda_vecs[2] * lambda_vecs[3], -1))
        + lambda_init
    )
    slot = jnp.arange(nh * ny, dtype=jnp.int32)
    place = (lax.axis_index("h") ^ (slot & 1)) * ny + (lax.axis_index("y") ^ (slot >> 1))
    parts = weigh(place, lam, lse, whole, o, rows, heads)

    got = lax.all_to_all(parts, ("h", "y"), 0, 0, tiled=False)
    diff = jnp.sum(got.astype(f32), 0).reshape(rows, heads, 2 * HD)
    mean_square = jnp.mean(diff * diff, -1, keepdims=True)
    normed = out_factor * diff / jnp.sqrt(mean_square + norm_eps) * head_gain.reshape(1, heads, 2 * HD)
    normed = normed.reshape(rows, width).astype(bf16)

    normed = jnp.concatenate([normed, swap(normed, "c", nc, 1)], 1)
    send = jnp.dot(normed, w_other, preferred_element_type=f32).astype(bf16)
    away = swap(send, "l", nl, 1)
    keep = jnp.dot(normed, w_mine, preferred_element_type=f32)
    return (keep + away.astype(f32) + residual.astype(f32)).astype(bf16)


def solution(mesh):
    sizes = (8, 2, 4, 2, 2)
    fine = Mesh(mesh.devices.reshape(sizes), ("z", "h", "y", "l", "c"))
    ctx, tp = ("z", "h", "y"), ("l", "c")
    placed = (
        P(ctx, tp),
        P(ctx, tp),
        P(ctx, tp),
        P(ctx),
        P(None, tp, None),
        P(tp),
        P(tp, None),
        P(ctx, tp),
    )
    return jax.shard_map(
        lambda *a: per_device(sizes, *a), mesh=fine, in_specs=placed, out_specs=P(ctx, tp), check_vma=False
    )
```

```python
import math

import jax
import jax.numpy as jnp
from jax import lax
from jax.experimental import pallas as pl
from jax.experimental.pallas import tpu as pltpu
from jax.sharding import Mesh, PartitionSpec as P

lambda_init = 0.2
out_factor = 0.8
norm_eps = 1e-05

HD = 128
RUN = 72
TILE = 4
NEG = -1e30
FLOOR = -1e29
f32 = jnp.float32
bf16 = jnp.bfloat16


def attend_kernel(rows, qb, kb, *refs):
    slots = (len(refs) - 11) // 2
    q_refs, kv_refs, (o_ref, lse_ref) = refs[:slots], refs[slots:-10], refs[-10:-8]
    q3, k3, v3, q_s, k_s, v_s, lse_s, order = refs[-8:]
    head = pl.program_id(0)
    blocks = q3.shape[0]
    per = rows // RUN
    tile = TILE * RUN
    tiles = blocks // TILE
    scale = math.log2(math.e) / math.sqrt(HD)

    @pl.when(head == 0)
    def _():
        lse_s[...] = jnp.zeros_like(lse_s)
        for i in range(blocks):
            rk = jnp.int32(0)
            rq = jnp.int32(0)
            for j in range(blocks):
                rk = rk + (kb[j] < kb[i]).astype(jnp.int32)
                rq = rq + (qb[j] < qb[i]).astype(jnp.int32)
            order[0, i] = rk
            order[1, rk] = kb[i]
            order[2, i] = rq
            order[3, rq] = i
            order[4, rq] = qb[i]
        for t in range(tiles):
            last = order[4, t * TILE + TILE - 1]
            need = jnp.int32(0)
            for j in range(blocks):
                need = need + (kb[j] <= last).astype(jnp.int32)
            order[5, t] = lax.div(need + (TILE - 1), TILE)

    for i in range(blocks):
        z, d = i // per, i % per
        r = order[0, i]
        v_off = rows if z < slots - 1 else 0
        k3[r] = kv_refs[z][d * RUN : (d + 1) * RUN, :]
        v3[r] = kv_refs[min(z, slots - 1) + (z == slots - 1)][v_off + d * RUN : v_off + (d + 1) * RUN, :]
        q3[order[2, i]] = q_refs[z][d * RUN : (d + 1) * RUN, :]
    for i in range(blocks):
        q_s[i * RUN : (i + 1) * RUN, :] = q3[i]
        k_s[i * RUN : (i + 1) * RUN, :] = k3[i]
        v_s[i * RUN : (i + 1) * RUN, :] = v3[i]

    col = lax.broadcasted_iota(jnp.int32, (1, blocks * RUN), 1)
    kpos = lax.rem(col, RUN)
    for i in range(blocks):
        kpos = kpos + jnp.where(lax.div(col, RUN) == i, order[1, i] * RUN, 0)
    row = lax.broadcasted_iota(jnp.int32, (tile, 1), 0)
    lane = lax.broadcasted_iota(jnp.int32, (RUN, HD), 1)

    def one_tile(t, carry):
        need = order[5, t]
        start = pl.multiple_of(t * tile, tile)
        qpos = lax.rem(row, RUN)
        for i in range(TILE):
            qpos = qpos + jnp.where(lax.div(row, RUN) == i, order[4, t * TILE + i] * RUN, 0)

        def put(a, num, lse):
            for i in range(TILE):
                g = order[3, t * TILE + i]
                o_ref[g, :, a * 2 * HD : (a + 1) * 2 * HD] = num[i * RUN : (i + 1) * RUN].astype(bf16)
                lse_s[g] = jnp.where(lane == head * 2 + a, lse[i * RUN : (i + 1) * RUN], lse_s[g])

        for n in range(1, tiles + 1):

            @pl.when(need == n)
            def _(n=n):
                allowed = kpos[:, : n * tile] <= qpos
                for a in range(2):
                    s = lax.dot_general(
                        q_s[pl.ds(start, tile), a * HD : (a + 1) * HD],
                        k_s[: n * tile, a * HD : (a + 1) * HD],
                        (((1,), (1,)), ((), ())),
                        preferred_element_type=f32,
                    )
                    s = jnp.where(allowed, s, NEG)
                    m = jnp.maximum(jnp.max(s, -1, keepdims=True), FLOOR) * scale
                    p = jnp.exp2(s * scale - m)
                    total = jnp.sum(p, -1, keepdims=True)
                    num = jnp.dot(p.astype(bf16), v_s[: n * tile, :], preferred_element_type=f32)
                    some = total > 0.0
                    safe = jnp.where(some, total, 1.0)
                    put(a, num * (1.0 / safe), jnp.where(some, m + jnp.log2(safe), NEG))

        @pl.when(need == 0)
        def _():
            for a in range(2):
                put(a, jnp.zeros((tile, 2 * HD), f32), jnp.full((tile, 1), NEG, f32))

        return carry

    lax.fori_loop(0, tiles, one_tile, 0)

    @pl.when(head == pl.num_programs(0) - 1)
    def _():
        lse_ref[...] = jnp.transpose(lse_s[...].reshape(blocks * RUN, HD))[: lse_ref.shape[0], :]


def attend(q_parts, kv_parts, qb, kb, rows, heads):
    blocks = len(q_parts) * rows // RUN
    return pl.pallas_call(
        lambda *r: attend_kernel(rows, *r),
        out_shape=[
            jax.ShapeDtypeStruct((blocks, RUN, heads * 4 * HD), bf16),
            jax.ShapeDtypeStruct((8, blocks * RUN), f32),
        ],
        grid_spec=pltpu.PrefetchScalarGridSpec(
            num_scalar_prefetch=2,
            grid=(heads,),
            in_specs=[pl.BlockSpec((x.shape[0], 2 * HD), lambda h, *_: (0, h)) for x in q_parts + kv_parts],
            out_specs=[
                pl.BlockSpec((blocks, RUN, 4 * HD), lambda h, *_: (0, 0, h)),
                pl.BlockSpec((8, blocks * RUN), lambda h, *_: (0, 0)),
            ],
            scratch_shapes=[pltpu.VMEM((blocks, RUN, 2 * HD), bf16)] * 3
            + [pltpu.VMEM((blocks * RUN, 2 * HD), bf16)] * 3
            + [pltpu.VMEM((blocks, RUN, HD), f32), pltpu.SMEM((6, 128), jnp.int32)],
        ),
        compiler_params=pltpu.CompilerParams(vmem_limit_bytes=32 << 20),
        name="attend",
    )(qb, kb, *[pltpu.with_memory_space_constraint(x, pltpu.HBM) for x in q_parts + kv_parts])


def weigh_kernel(heads, place, lam, lse_ref, all_ref, o_ref, out_ref, w_s):
    s = pl.program_id(0)
    rows = out_ref.shape[1]

    @pl.when(s == 0)
    def _():
        w = jnp.exp2(lse_ref[...] - all_ref[...])
        w = jnp.concatenate([w, jnp.zeros((HD - w.shape[0], w.shape[1]), f32)], 0)
        w_s[...] = jnp.transpose(w)

    w = w_s[pl.ds(pl.multiple_of(s * rows, rows), rows), :]
    for h in range(heads):
        w1 = w[:, 2 * h : 2 * h + 1]
        w2 = w[:, 2 * h + 1 : 2 * h + 2] * lam[h]
        o1 = o_ref[:, :, h * 4 * HD : h * 4 * HD + 2 * HD].reshape(rows, 2 * HD).astype(f32)
        o2 = o_ref[:, :, h * 4 * HD + 2 * HD : (h + 1) * 4 * HD].reshape(rows, 2 * HD).astype(f32)
        out_ref[0, :, h * 2 * HD : (h + 1) * 2 * HD] = (w1 * o1 - w2 * o2).astype(bf16)


def weigh(place, lam, lse, lse_all, o, rows, heads):
    slots = lse.shape[1] // rows
    return pl.pallas_call(
        lambda *r: weigh_kernel(heads, *r),
        out_shape=jax.ShapeDtypeStruct((slots, rows, heads * 2 * HD), bf16),
        grid_spec=pltpu.PrefetchScalarGridSpec(
            num_scalar_prefetch=2,
            grid=(slots,),
            in_specs=[pl.BlockSpec(lse.shape, lambda s, *_: (0, 0))] * 2
            + [pl.BlockSpec((rows // RUN, RUN, heads * 4 * HD), lambda s, *_: (s, 0, 0))],
            out_specs=pl.BlockSpec((1, rows, heads * 2 * HD), lambda s, place, lam: (place[s], 0, 0)),
            scratch_shapes=[pltpu.VMEM((slots * rows, HD), f32)],
        ),
        compiler_params=pltpu.CompilerParams(vmem_limit_bytes=16 << 20),
        name="weigh",
    )(place, lam, lse, lse_all, o)


def project_kernel(heads, cols, got_ref, gain_ref, w_ref, send_ref, keep_ref, n_s):
    total = got_ref[0].astype(f32)
    for i in range(1, got_ref.shape[0]):
        total = total + got_ref[i].astype(f32)
    for h in range(heads):
        d = total[:, h * 2 * HD : (h + 1) * 2 * HD]
        mean_square = jnp.mean(d * d, -1, keepdims=True)
        g = gain_ref[0:1, h * 2 * HD : (h + 1) * 2 * HD]
        n_s[:, h * 2 * HD : (h + 1) * 2 * HD] = (out_factor * d / jnp.sqrt(mean_square + norm_eps) * g).astype(bf16)
    n = n_s[...]
    width = keep_ref.shape[2]
    for i in range(4):
        w = w_ref[:, pl.ds(pl.multiple_of(cols[i] * width, HD), width)]
        share = jnp.dot(n, w, preferred_element_type=f32)
        if i < 2:
            send_ref[i] = share.astype(bf16)
        else:
            keep_ref[i - 2] = share


def project(cols, got, gain, weight, heads):
    rows = got.shape[1]
    width = weight.shape[1] // 4
    vm = pl.BlockSpec(memory_space=pltpu.VMEM)
    return pl.pallas_call(
        lambda *r: project_kernel(heads, *r),
        out_shape=[
            jax.ShapeDtypeStruct((2, rows, width), bf16),
            jax.ShapeDtypeStruct((2, rows, width), f32),
        ],
        in_specs=[pl.BlockSpec(memory_space=pltpu.SMEM), vm, vm, vm],
        out_specs=[vm, vm],
        scratch_shapes=[pltpu.VMEM((rows, got.shape[2]), bf16)],
        compiler_params=pltpu.CompilerParams(vmem_limit_bytes=16 << 20),
        name="project",
    )(cols, got, gain, weight)


def shift(x, axis, size, step):
    return lax.ppermute(x, axis, [(i, (i + step) % size) for i in range(size)])


def logsum(a, b):
    top = jnp.maximum(a, b)
    return top + jnp.log2(jnp.exp2(a - top) + jnp.exp2(b - top))


def reorder(x, rows, mask):
    slots = x.shape[1] // rows
    return jnp.concatenate([x[:, (s ^ mask) * rows : ((s ^ mask) + 1) * rows] for s in range(slots)], 1)


def swap(x, axis, size, mask):
    return lax.ppermute(x, axis, [(i, i ^ mask) for i in range(size)])


def per_device(sizes, queries, keys, values, positions, lambda_vecs, head_gain, out_weight, residual):
    nz, nh, ny, nl, nc = sizes
    rows, width = queries.shape
    heads = lambda_vecs.shape[1]
    block = ((positions[::RUN].astype(f32) + 0.5) * (1.0 / RUN)).astype(jnp.int32).astype(bf16)
    ids = jnp.broadcast_to(jnp.pad(block, (0, width - block.shape[0]))[None, :], (16, width))

    q_mine = jnp.concatenate([queries, ids], 0)
    kv_mine = jnp.concatenate([keys, values, ids], 0)
    q_pair = swap(q_mine, "h", nh, 1)
    up, down = shift(kv_mine, "z", nz, 1), shift(kv_mine, "z", nz, -1)
    q_near = [swap(q_mine, "y", ny, d) for d in range(1, ny)]
    kv_parts = [kv_mine, up, down]
    up, down, q_pair = lax.optimization_barrier((up, down, q_pair))
    up, down = shift(up, "z", nz, 1), shift(down, "z", nz, -1)
    q_far = [swap(q_pair, "y", ny, d) for d in range(1, ny)]
    kv_parts += [up, down]
    up, down, q_near = lax.optimization_barrier((up, down, q_near))
    up, down = shift(up, "z", nz, 1), shift(down, "z", nz, -1)
    kv_parts += [up, down]
    up, down, q_far = lax.optimization_barrier((up, down, q_far))
    kv_parts += [shift(up[:rows], "z", nz, 1), shift(down[rows:], "z", nz, -1)]
    q_parts = [q_mine, q_pair]
    for d in range(ny - 1):
        q_parts += [q_near[d], q_far[d]]

    def numbers(parts):
        spots = [p[p.shape[0] - 16 : p.shape[0] - 15, : rows // RUN] for p in parts]
        return jnp.concatenate(spots, 0).astype(jnp.int32).reshape(-1)

    qb = numbers(q_parts)
    kb = numbers(kv_parts[: nz - 1] + kv_parts[nz:])

    o, lse = attend(q_parts, kv_parts, qb, kb, rows, heads)

    whole = lse
    for axis, size, mask, slot in (("h", nh, 1, 1), ("y", ny, 1, 2), ("y", ny, 3, 6)):
        whole = logsum(whole, reorder(swap(whole, axis, size, mask), rows, slot))

    lam = (
        jnp.exp(jnp.sum(lambda_vecs[0] * lambda_vecs[1], -1))
        - jnp.exp(jnp.sum(lambda_vecs[2] * lambda_vecs[3], -1))
        + lambda_init
    )
    slot = jnp.arange(nh * ny, dtype=jnp.int32)
    place = (lax.axis_index("h") ^ (slot & 1)) * ny + (lax.axis_index("y") ^ (slot >> 1))
    parts = weigh(place, lam, lse, whole, o, rows, heads)

    got = lax.all_to_all(parts, ("h", "y"), 0, 0, tiled=False)
    l, c = lax.axis_index("l"), lax.axis_index("c")
    cols = jnp.stack([l * nc + 1 - c, (1 - l) * nc + 1 - c, l * nc + c, (1 - l) * nc + c]).astype(jnp.int32)
    send, keep = project(cols, got, head_gain.reshape(1, width), out_weight, heads)
    near = swap(send, "c", nc, 1)
    far = swap((keep[1] + near[1].astype(f32)).astype(bf16), "l", nl, 1)
    return (keep[0] + near[0].astype(f32) + far.astype(f32) + residual.astype(f32)).astype(bf16)


def solution(mesh):
    sizes = (8, 2, 4, 2, 2)
    fine = Mesh(mesh.devices.reshape(sizes), ("z", "h", "y", "l", "c"))
    ctx, tp = ("z", "h", "y"), ("l", "c")
    placed = (
        P(ctx, tp),
        P(ctx, tp),
        P(ctx, tp),
        P(ctx),
        P(None, tp, None),
        P(tp),
        P(tp, None),
        P(ctx, tp),
    )
    return jax.shard_map(
        lambda *a: per_device(sizes, *a), mesh=fine, in_specs=placed, out_specs=P(ctx, tp), check_vma=False
    )
```

```python
import math

import jax
import jax.numpy as jnp
from jax import lax
from jax.experimental import pallas as pl
from jax.experimental.pallas import tpu as pltpu
from jax.sharding import Mesh, PartitionSpec as P

lambda_init = 0.2
out_factor = 0.8
norm_eps = 1e-05

HD = 128
RUN = 72
TILE = 4
NEG = -1e30
FLOOR = -1e29
f32 = jnp.float32
bf16 = jnp.bfloat16


def attend_kernel(rows, *refs):
    slots = (len(refs) - 11) // 2
    q_refs, kv_refs, (o_ref, lse_ref) = refs[:slots], refs[slots:-10], refs[-10:-8]
    q3, k3, v3, q_s, k_s, v_s, lse_s, order = refs[-8:]
    head = pl.program_id(0)
    blocks = q3.shape[0]
    per = rows // RUN
    tile = TILE * RUN
    tiles = blocks // TILE
    scale = math.log2(math.e) / math.sqrt(HD)

    @pl.when(head == 0)
    def _():
        lse_s[...] = jnp.zeros_like(lse_s)
        first = lax.broadcasted_iota(jnp.int32, (16, HD), 0) == 0
        lanes = lax.broadcasted_iota(jnp.int32, (16, HD), 1)

        def numbers(part):
            tail = part[part.shape[0] - 16 :, :HD].astype(f32)
            return [jnp.sum(jnp.where(first & (lanes == d), tail, 0.0)).astype(jnp.int32) for d in range(per)]

        kb = [v for p in [*kv_refs[: slots - 1], kv_refs[slots]] for v in numbers(p)]
        qb = [v for p in q_refs for v in numbers(p)]
        for i in range(blocks):
            rk = jnp.int32(0)
            rq = jnp.int32(0)
            for j in range(blocks):
                rk = rk + (kb[j] < kb[i]).astype(jnp.int32)
                rq = rq + (qb[j] < qb[i]).astype(jnp.int32)
            order[0, i] = rk
            order[1, rk] = kb[i]
            order[2, i] = rq
            order[3, rq] = i
            order[4, rq] = qb[i]
        for t in range(tiles):
            last = order[4, t * TILE + TILE - 1]
            need = jnp.int32(0)
            for j in range(blocks):
                need = need + (order[1, j] <= last).astype(jnp.int32)
            order[5, t] = lax.div(need + (TILE - 1), TILE)

    for i in range(blocks):
        z, d = i // per, i % per
        r = order[0, i]
        v_off = rows if z < slots - 1 else 0
        k3[r] = kv_refs[z][d * RUN : (d + 1) * RUN, :]
        v3[r] = kv_refs[min(z, slots - 1) + (z == slots - 1)][v_off + d * RUN : v_off + (d + 1) * RUN, :]
        q3[order[2, i]] = q_refs[z][d * RUN : (d + 1) * RUN, :]
    for i in range(blocks):
        q_s[i * RUN : (i + 1) * RUN, :] = q3[i]
        k_s[i * RUN : (i + 1) * RUN, :] = k3[i]
        v_s[i * RUN : (i + 1) * RUN, :] = v3[i]

    col = lax.broadcasted_iota(jnp.int32, (1, blocks * RUN), 1)
    kpos = lax.rem(col, RUN)
    for i in range(blocks):
        kpos = kpos + jnp.where(lax.div(col, RUN) == i, order[1, i] * RUN, 0)
    row = lax.broadcasted_iota(jnp.int32, (tile, 1), 0)
    lane = lax.broadcasted_iota(jnp.int32, (RUN, HD), 1)

    def one_tile(t, carry):
        need = order[5, t]
        start = pl.multiple_of(t * tile, tile)
        qpos = lax.rem(row, RUN)
        for i in range(TILE):
            qpos = qpos + jnp.where(lax.div(row, RUN) == i, order[4, t * TILE + i] * RUN, 0)

        def put(a, num, lse):
            for i in range(TILE):
                g = order[3, t * TILE + i]
                o_ref[g, :, a * 2 * HD : (a + 1) * 2 * HD] = num[i * RUN : (i + 1) * RUN].astype(bf16)
                lse_s[g] = jnp.where(lane == head * 2 + a, lse[i * RUN : (i + 1) * RUN], lse_s[g])

        for n in range(1, tiles + 1):

            @pl.when(need == n)
            def _(n=n):
                allowed = kpos[:, : n * tile] <= qpos
                for a in range(2):
                    s = lax.dot_general(
                        q_s[pl.ds(start, tile), a * HD : (a + 1) * HD],
                        k_s[: n * tile, a * HD : (a + 1) * HD],
                        (((1,), (1,)), ((), ())),
                        preferred_element_type=f32,
                    )
                    s = jnp.where(allowed, s, NEG)
                    m = jnp.maximum(jnp.max(s, -1, keepdims=True), FLOOR) * scale
                    p = jnp.exp2(s * scale - m)
                    total = jnp.sum(p, -1, keepdims=True)
                    num = jnp.dot(p.astype(bf16), v_s[: n * tile, :], preferred_element_type=f32)
                    some = total > 0.0
                    safe = jnp.where(some, total, 1.0)
                    put(a, num * (1.0 / safe), jnp.where(some, m + jnp.log2(safe), NEG))

        @pl.when(need == 0)
        def _():
            for a in range(2):
                put(a, jnp.zeros((tile, 2 * HD), f32), jnp.full((tile, 1), NEG, f32))

        return carry

    lax.fori_loop(0, tiles, one_tile, 0)

    @pl.when(head == pl.num_programs(0) - 1)
    def _():
        lse_ref[...] = jnp.transpose(lse_s[...].reshape(blocks * RUN, HD))[: lse_ref.shape[0], :]


def attend(q_parts, kv_parts, rows, heads):
    blocks = len(q_parts) * rows // RUN
    return pl.pallas_call(
        lambda *r: attend_kernel(rows, *r),
        out_shape=[
            jax.ShapeDtypeStruct((blocks, RUN, heads * 4 * HD), bf16),
            jax.ShapeDtypeStruct((8, blocks * RUN), f32),
        ],
        grid_spec=pltpu.PrefetchScalarGridSpec(
            num_scalar_prefetch=0,
            grid=(heads,),
            in_specs=[pl.BlockSpec((x.shape[0], 2 * HD), lambda h, *_: (0, h)) for x in q_parts + kv_parts],
            out_specs=[
                pl.BlockSpec((blocks, RUN, 4 * HD), lambda h, *_: (0, 0, h)),
                pl.BlockSpec((8, blocks * RUN), lambda h, *_: (0, 0)),
            ],
            scratch_shapes=[pltpu.VMEM((blocks, RUN, 2 * HD), bf16)] * 3
            + [pltpu.VMEM((blocks * RUN, 2 * HD), bf16)] * 3
            + [pltpu.VMEM((blocks, RUN, HD), f32), pltpu.SMEM((6, 128), jnp.int32)],
        ),
        compiler_params=pltpu.CompilerParams(vmem_limit_bytes=32 << 20),
        name="attend",
    )(*[pltpu.with_memory_space_constraint(x, pltpu.HBM) for x in q_parts + kv_parts])


def logsum(parts):
    top = parts[0]
    for p in parts[1:]:
        top = jnp.maximum(top, p)
    total = jnp.exp2(parts[0] - top)
    for p in parts[1:]:
        total = total + jnp.exp2(p - top)
    return top + jnp.log2(total)


def reorder(x, rows, mask):
    slots = x.shape[1] // rows
    return jnp.concatenate([x[:, (s ^ mask) * rows : ((s ^ mask) + 1) * rows] for s in range(slots)], 1)


def merge_kernel(rows, a_ref, b_ref, o_ref):
    o_ref[...] = logsum([a_ref[...], reorder(b_ref[...], rows, 1)])


def merge(a, b, rows):
    vm = pl.BlockSpec(memory_space=pltpu.VMEM)
    return pl.pallas_call(
        lambda *r: merge_kernel(rows, *r),
        out_shape=jax.ShapeDtypeStruct(a.shape, a.dtype),
        in_specs=[vm, vm],
        out_specs=vm,
        compiler_params=pltpu.CompilerParams(vmem_limit_bytes=4 << 20),
        name="merge",
    )(a, b)


def weigh_kernel(heads, place, lam, lse_ref, *refs):
    all_refs, o_ref, out_ref, w_s = refs[:-3], refs[-3], refs[-2], refs[-1]
    s = pl.program_id(0)
    rows = out_ref.shape[1]

    @pl.when(s == 0)
    def _():
        whole = logsum([reorder(r[...], rows, 2 * i) for i, r in enumerate(all_refs)])
        w = jnp.exp2(lse_ref[...] - whole)
        w = jnp.concatenate([w, jnp.zeros((HD - w.shape[0], w.shape[1]), f32)], 0)
        w_s[...] = jnp.transpose(w)

    w = w_s[pl.ds(pl.multiple_of(s * rows, rows), rows), :]
    for h in range(heads):
        w1 = w[:, 2 * h : 2 * h + 1]
        w2 = w[:, 2 * h + 1 : 2 * h + 2] * lam[h]
        o1 = o_ref[:, :, h * 4 * HD : h * 4 * HD + 2 * HD].reshape(rows, 2 * HD).astype(f32)
        o2 = o_ref[:, :, h * 4 * HD + 2 * HD : (h + 1) * 4 * HD].reshape(rows, 2 * HD).astype(f32)
        out_ref[0, :, h * 2 * HD : (h + 1) * 2 * HD] = (w1 * o1 - w2 * o2).astype(bf16)


def weigh(place, lam, lse, lses, o, rows, heads):
    slots = lse.shape[1] // rows
    return pl.pallas_call(
        lambda *r: weigh_kernel(heads, *r),
        out_shape=jax.ShapeDtypeStruct((slots, rows, heads * 2 * HD), bf16),
        grid_spec=pltpu.PrefetchScalarGridSpec(
            num_scalar_prefetch=2,
            grid=(slots,),
            in_specs=[pl.BlockSpec(lse.shape, lambda s, *_: (0, 0))] * (1 + len(lses))
            + [pl.BlockSpec((rows // RUN, RUN, heads * 4 * HD), lambda s, *_: (s, 0, 0))],
            out_specs=pl.BlockSpec((1, rows, heads * 2 * HD), lambda s, place, lam: (place[s], 0, 0)),
            scratch_shapes=[pltpu.VMEM((slots * rows, HD), f32)],
        ),
        compiler_params=pltpu.CompilerParams(vmem_limit_bytes=16 << 20),
        name="weigh",
    )(place, lam, lse, *lses, o)


def project_kernel(heads, cols, got_ref, gain_ref, w_ref, send_ref, keep_ref, n_s):
    i = pl.program_id(0)

    @pl.when(i == 0)
    def _():
        total = got_ref[0].astype(f32)
        for j in range(1, got_ref.shape[0]):
            total = total + got_ref[j].astype(f32)
        for h in range(heads):
            d = total[:, h * 2 * HD : (h + 1) * 2 * HD]
            mean_square = jnp.mean(d * d, -1, keepdims=True)
            g = gain_ref[0:1, h * 2 * HD : (h + 1) * 2 * HD]
            n_s[:, h * 2 * HD : (h + 1) * 2 * HD] = (out_factor * d / jnp.sqrt(mean_square + norm_eps) * g).astype(bf16)

    share = jnp.dot(n_s[...], w_ref[...], preferred_element_type=f32)

    @pl.when(i < 2)
    def _():
        send_ref[0] = share.astype(bf16)

    @pl.when(i >= 2)
    def _():
        keep_ref[0] = share


def project(cols, got, gain, weight, heads):
    rows = got.shape[1]
    width = weight.shape[1] // 4
    return pl.pallas_call(
        lambda *r: project_kernel(heads, *r),
        out_shape=[
            jax.ShapeDtypeStruct((2, rows, width), bf16),
            jax.ShapeDtypeStruct((2, rows, width), f32),
        ],
        grid_spec=pltpu.PrefetchScalarGridSpec(
            num_scalar_prefetch=1,
            grid=(4,),
            in_specs=[
                pl.BlockSpec(got.shape, lambda i, cols: (0, 0, 0)),
                pl.BlockSpec(gain.shape, lambda i, cols: (0, 0)),
                pl.BlockSpec((weight.shape[0], width), lambda i, cols: (0, cols[i])),
            ],
            out_specs=[
                pl.BlockSpec((1, rows, width), lambda i, cols: (jnp.minimum(i, 1), 0, 0)),
                pl.BlockSpec((1, rows, width), lambda i, cols: (jnp.maximum(i, 2) - 2, 0, 0)),
            ],
            scratch_shapes=[pltpu.VMEM((rows, got.shape[2]), bf16)],
        ),
        compiler_params=pltpu.CompilerParams(vmem_limit_bytes=24 << 20),
        name="project",
    )(cols, got, gain, pltpu.with_memory_space_constraint(weight, pltpu.HBM))


def shift(x, axis, size, step):
    return lax.ppermute(x, axis, [(i, (i + step) % size) for i in range(size)])


def swap(x, axis, size, mask):
    return lax.ppermute(x, axis, [(i, i ^ mask) for i in range(size)])


def per_device(sizes, queries, keys, values, positions, lambda_vecs, head_gain, out_weight, residual):
    nz, nh, ny, nl, nc = sizes
    rows, width = queries.shape
    heads = lambda_vecs.shape[1]
    block = ((positions[::RUN].astype(f32) + 0.5) * (1.0 / RUN)).astype(jnp.int32).astype(bf16)
    ids = jnp.broadcast_to(jnp.pad(block, (0, width - block.shape[0]))[None, :], (16, width))
    slot = jnp.arange(nh * ny, dtype=jnp.int32)
    place = (lax.axis_index("h") ^ (slot & 1)) * ny + (lax.axis_index("y") ^ (slot >> 1))

    q_mine = jnp.concatenate([queries, ids], 0)
    kv_mine = jnp.concatenate([keys, values, ids], 0)
    up, down = shift(kv_mine, "z", nz, 1), shift(kv_mine, "z", nz, -1)
    q_pair = swap(q_mine, "h", nh, 1)
    q_near = [swap(q_mine, "y", ny, d) for d in range(1, ny)]
    kv_parts = [kv_mine, up, down]
    up, down, q_pair, q_near = lax.optimization_barrier((up, down, q_pair, q_near))
    up, down = shift(up, "z", nz, 1), shift(down, "z", nz, -1)
    q_far = [swap(q_pair, "y", ny, d) for d in range(1, ny)]
    kv_parts += [up, down]
    up, down, q_far = lax.optimization_barrier((up, down, q_far))
    up, down = shift(up, "z", nz, 1), shift(down, "z", nz, -1)
    kv_parts += [up, down]
    kv_parts += [shift(up[:rows], "z", nz, 1), shift(down[rows:], "z", nz, -1)]
    q_parts = [q_mine, q_pair]
    for d in range(ny - 1):
        q_parts += [q_near[d], q_far[d]]

    o, lse = attend(q_parts, kv_parts, rows, heads)

    pair = merge(lse, swap(lse, "h", nh, 1), rows)
    others = [swap(pair, "y", ny, d) for d in range(1, ny)]

    lam = (
        jnp.exp(jnp.sum(lambda_vecs[0] * lambda_vecs[1], -1))
        - jnp.exp(jnp.sum(lambda_vecs[2] * lambda_vecs[3], -1))
        + lambda_init
    )
    parts = weigh(place, lam, lse, [pair] + others, o, rows, heads)

    got = lax.all_to_all(parts, ("h", "y"), 0, 0, tiled=False)
    l, c = lax.axis_index("l"), lax.axis_index("c")
    cols = jnp.stack([l * nc + 1 - c, (1 - l) * nc + 1 - c, l * nc + c, (1 - l) * nc + c]).astype(jnp.int32)
    send, keep = project(cols, got, head_gain.reshape(1, width), out_weight, heads)
    near = swap(send, "c", nc, 1)
    far = swap((keep[1] + near[1].astype(f32)).astype(bf16), "l", nl, 1)
    return (keep[0] + near[0].astype(f32) + far.astype(f32) + residual.astype(f32)).astype(bf16)


def solution(mesh):
    sizes = (8, 2, 4, 2, 2)
    fine = Mesh(mesh.devices.reshape(sizes), ("z", "h", "y", "l", "c"))
    ctx, tp = ("z", "h", "y"), ("l", "c")
    placed = (
        P(ctx, tp),
        P(ctx, tp),
        P(ctx, tp),
        P(ctx),
        P(None, tp, None),
        P(tp),
        P(tp, None),
        P(ctx, tp),
    )
    return jax.shard_map(
        lambda *a: per_device(sizes, *a), mesh=fine, in_specs=placed, out_specs=P(ctx, tp), check_vma=False
    )
```

```python
import math

import jax
import jax.numpy as jnp
from jax import lax
from jax.experimental import pallas as pl
from jax.experimental.pallas import tpu as pltpu
from jax.sharding import Mesh, PartitionSpec as P

lambda_init = 0.2
out_factor = 0.8
norm_eps = 1e-05

HD = 128
RUN = 72
TILE = 4
NEG = -1e30
FLOOR = -1e29
f32 = jnp.float32
bf16 = jnp.bfloat16


def attend_kernel(rows, spans, slots, spots, prev, *refs):
    q_refs, refs = refs[:slots], refs[slots:]
    count = len(refs) - 10 - 2 * prev
    kv_refs, refs = refs[:count], refs[count:]
    if prev:
        prev_o, prev_lse = refs[:2]
        refs = refs[2:]
    o_ref, lse_ref, q3, k3, v3, q_s, k_s, v_s, lse_s, order = refs
    head = pl.program_id(0)
    per = rows // RUN
    blocks = slots * per
    keys = len(spots) * per
    tile = TILE * RUN
    tiles = blocks // TILE
    scale = math.log2(math.e) / math.sqrt(HD)

    @pl.when(head == 0)
    def _():
        lse_s[...] = jnp.zeros_like(lse_s)
        first = lax.broadcasted_iota(jnp.int32, (16, HD), 0) == 0
        lanes = lax.broadcasted_iota(jnp.int32, (16, HD), 1)

        def numbers(part):
            tail = part[part.shape[0] - 16 :, :HD].astype(f32)
            return [jnp.sum(jnp.where(first & (lanes == d), tail, 0.0)).astype(jnp.int32) for d in range(per)]

        kb = [v for k, kr, v, vr in spots for v in numbers(kv_refs[v])]
        qb = [v for p in q_refs for v in numbers(p)]
        for numbered, row in ((kb, 0), (qb, 2)):
            for i in range(len(numbered)):
                rank = jnp.int32(0)
                for j in range(len(numbered)):
                    rank = rank + (numbered[j] < numbered[i]).astype(jnp.int32)
                order[row, i] = rank
                if row == 0:
                    order[1, rank] = numbered[i]
                else:
                    order[3, rank] = i
                    order[4, rank] = numbered[i]
        for t in range(tiles):
            last = order[4, t * TILE + TILE - 1]
            need = jnp.int32(0)
            for j in range(keys):
                need = need + (kb[j] <= last).astype(jnp.int32)
            order[5, t] = need

    for i in range(keys):
        k, kr, v, vr = spots[i // per]
        d = i % per * RUN
        r = order[0, i]
        k3[r] = kv_refs[k][kr + d : kr + d + RUN, :]
        v3[r] = kv_refs[v][vr + d : vr + d + RUN, :]
    for i in range(blocks):
        d = i % per * RUN
        q3[order[2, i]] = q_refs[i // per][d : d + RUN, :]
    for i in range(keys):
        k_s[i * RUN : (i + 1) * RUN, :] = k3[i]
        v_s[i * RUN : (i + 1) * RUN, :] = v3[i]
    for i in range(blocks):
        q_s[i * RUN : (i + 1) * RUN, :] = q3[i]

    col = lax.broadcasted_iota(jnp.int32, (1, keys * RUN), 1)
    kpos = lax.rem(col, RUN)
    for i in range(keys):
        kpos = kpos + jnp.where(lax.div(col, RUN) == i, order[1, i] * RUN, 0)
    row = lax.broadcasted_iota(jnp.int32, (tile, 1), 0)
    lane = lax.broadcasted_iota(jnp.int32, (RUN, HD), 1)

    def one_tile(t, carry):
        need = order[5, t]
        start = pl.multiple_of(t * tile, tile)
        qpos = lax.rem(row, RUN)
        for i in range(TILE):
            qpos = qpos + jnp.where(lax.div(row, RUN) == i, order[4, t * TILE + i] * RUN, 0)

        def put(a, num, lse):
            for i in range(TILE):
                g = order[3, t * TILE + i]
                o = num[i * RUN : (i + 1) * RUN]
                e = lse[i * RUN : (i + 1) * RUN]
                if prev:
                    pick = lane == head * 2 + a
                    before = jnp.max(jnp.where(pick, prev_lse[g], -3e38), -1, keepdims=True)
                    both = logsum([before, e])
                    o = o * jnp.exp2(e - both) + prev_o[g, :, a * 2 * HD : (a + 1) * 2 * HD].astype(f32) * jnp.exp2(before - both)
                    e = both
                o_ref[g, :, a * 2 * HD : (a + 1) * 2 * HD] = o.astype(bf16)
                lse_s[g] = jnp.where(lane == head * 2 + a, e, lse_s[g])

        for low, high in zip((0,) + spans[:-1], spans):

            @pl.when((need > low) & (need <= high))
            def _(span=high * RUN):
                allowed = kpos[:, :span] <= qpos
                ss = [
                    lax.dot_general(
                        q_s[pl.ds(start, tile), a * HD : (a + 1) * HD],
                        k_s[:span, a * HD : (a + 1) * HD],
                        (((1,), (1,)), ((), ())),
                        preferred_element_type=f32,
                    )
                    for a in range(2)
                ]
                ps = []
                for a in range(2):
                    s = jnp.where(allowed, ss[a], NEG)
                    m = jnp.maximum(jnp.max(s, -1, keepdims=True), FLOOR) * scale
                    p = jnp.exp2(s * scale - m)
                    ps.append((p.astype(bf16), m, jnp.sum(p, -1, keepdims=True)))
                for a in range(2):
                    p, m, total = ps[a]
                    num = jnp.dot(p, v_s[:span, :], preferred_element_type=f32)
                    some = total > 0.0
                    safe = jnp.where(some, total, 1.0)
                    put(a, num * (1.0 / safe), jnp.where(some, m + jnp.log2(safe), NEG))

        @pl.when(need == 0)
        def _():
            for a in range(2):
                put(a, jnp.zeros((tile, 2 * HD), f32), jnp.full((tile, 1), NEG, f32))

        return carry

    lax.fori_loop(0, tiles, one_tile, 0)

    @pl.when(head == pl.num_programs(0) - 1)
    def _():
        if prev:
            lse_ref[...] = jnp.transpose(lse_s[...].reshape(blocks * RUN, HD))[: lse_ref.shape[0], :]
        else:
            lse_ref[...] = lse_s[...]


def attend(q_parts, kv_parts, spots, spans, rows, heads, before=()):
    slots = len(q_parts)
    blocks = slots * rows // RUN
    keys = len(spots) * rows // RUN
    wide = jax.ShapeDtypeStruct((blocks, RUN, HD), f32)
    flat = jax.ShapeDtypeStruct((8, blocks * RUN), f32)
    lse = flat if before else wide
    out_block = pl.BlockSpec((blocks, RUN, 4 * HD), lambda h: (0, 0, h))
    ins = [pltpu.with_memory_space_constraint(x, pltpu.HBM) for x in [*q_parts, *kv_parts, *before]]
    return pl.pallas_call(
        lambda *r: attend_kernel(rows, spans, slots, spots, bool(before), *r),
        out_shape=[jax.ShapeDtypeStruct((blocks, RUN, heads * 4 * HD), bf16), lse],
        grid_spec=pltpu.PrefetchScalarGridSpec(
            num_scalar_prefetch=0,
            grid=(heads,),
            in_specs=[pl.BlockSpec((x.shape[0], 2 * HD), lambda h: (0, h)) for x in [*q_parts, *kv_parts]]
            + ([out_block, pl.BlockSpec(wide.shape, lambda h: (0, 0, 0))] if before else []),
            out_specs=[out_block, pl.BlockSpec(lse.shape, lambda h: (0,) * len(lse.shape))],
            scratch_shapes=[
                pltpu.VMEM((blocks, RUN, 2 * HD), bf16),
                pltpu.VMEM((keys, RUN, 2 * HD), bf16),
                pltpu.VMEM((keys, RUN, 2 * HD), bf16),
                pltpu.VMEM((blocks * RUN, 2 * HD), bf16),
                pltpu.VMEM((keys * RUN, 2 * HD), bf16),
                pltpu.VMEM((keys * RUN, 2 * HD), bf16),
                pltpu.VMEM((blocks, RUN, HD), f32),
                pltpu.SMEM((6, 128), jnp.int32),
            ],
        ),
        compiler_params=pltpu.CompilerParams(vmem_limit_bytes=36 << 20),
        cost_estimate=pl.CostEstimate(
            flops=heads * 2 * blocks * keys * RUN * RUN * 6 * HD * 8,
            bytes_accessed=(slots * 2 + len(spots) * 2) * rows * heads * 4 * HD,
            transcendentals=heads * 2 * blocks * keys * RUN * RUN,
        ),
        name="attend",
    )(*ins)


def logsum(parts):
    top = parts[0]
    for p in parts[1:]:
        top = jnp.maximum(top, p)
    total = jnp.exp2(parts[0] - top)
    for p in parts[1:]:
        total = total + jnp.exp2(p - top)
    return top + jnp.log2(total)


def reorder(x, rows, mask):
    slots = x.shape[1] // rows
    return jnp.concatenate([x[:, (s ^ mask) * rows : ((s ^ mask) + 1) * rows] for s in range(slots)], 1)


def merge_kernel(rows, a_ref, b_ref, o_ref):
    o_ref[...] = logsum([a_ref[...], reorder(b_ref[...], rows, 1)])


def merge(a, b, rows):
    vm = pl.BlockSpec(memory_space=pltpu.VMEM)
    return pl.pallas_call(
        lambda *r: merge_kernel(rows, *r),
        out_shape=jax.ShapeDtypeStruct(a.shape, a.dtype),
        in_specs=[vm, vm],
        out_specs=vm,
        compiler_params=pltpu.CompilerParams(vmem_limit_bytes=4 << 20),
        name="merge",
    )(a, b)


def weigh_kernel(heads, where, lam, lse_ref, *refs):
    all_refs, o_ref, out_ref, w_s = refs[:-3], refs[-3], refs[-2], refs[-1]
    j = pl.program_id(0)
    rows = out_ref.shape[2]

    @pl.when(j == 0)
    def _():
        whole = logsum([reorder(r[...], rows, 2 * i) for i, r in enumerate(all_refs)])
        w = jnp.exp2(lse_ref[...] - whole)
        w = jnp.concatenate([w, jnp.zeros((HD - w.shape[0], w.shape[1]), f32)], 0)
        w_s[...] = jnp.transpose(w)

    for d in range(2):
        w = w_s[pl.ds(pl.multiple_of((2 * j + d) * rows, rows), rows), :]
        o = o_ref[d * (rows // RUN) : (d + 1) * (rows // RUN)]
        place = where[0] ^ d
        for h in range(heads):
            w1 = w[:, 2 * h : 2 * h + 1]
            w2 = w[:, 2 * h + 1 : 2 * h + 2] * lam[h]
            o1 = o[:, :, h * 4 * HD : h * 4 * HD + 2 * HD].reshape(rows, 2 * HD).astype(f32)
            o2 = o[:, :, h * 4 * HD + 2 * HD : (h + 1) * 4 * HD].reshape(rows, 2 * HD).astype(f32)
            out_ref[place, 0, :, h * 2 * HD : (h + 1) * 2 * HD] = (w1 * o1 - w2 * o2).astype(bf16)


def weigh(where, lam, lse, lses, o, rows, heads):
    pairs = lse.shape[1] // rows // 2
    return pl.pallas_call(
        lambda *r: weigh_kernel(heads, *r),
        out_shape=jax.ShapeDtypeStruct((2, pairs, rows, heads * 2 * HD), bf16),
        grid_spec=pltpu.PrefetchScalarGridSpec(
            num_scalar_prefetch=2,
            grid=(pairs,),
            in_specs=[pl.BlockSpec(lse.shape, lambda j, *_: (0, 0))] * (1 + len(lses))
            + [pl.BlockSpec((2 * rows // RUN, RUN, heads * 4 * HD), lambda j, *_: (j, 0, 0))],
            out_specs=pl.BlockSpec(
                (2, 1, rows, heads * 2 * HD), lambda j, where, lam: (0, where[1] ^ j, 0, 0)
            ),
            scratch_shapes=[pltpu.VMEM((2 * pairs * rows, HD), f32)],
        ),
        compiler_params=pltpu.CompilerParams(vmem_limit_bytes=20 << 20),
        name="weigh",
    )(where, lam, lse, *lses, o)


def project_kernel(heads, cols, got_ref, gain_ref, w_ref, send_ref, keep_ref, n_s):
    i = pl.program_id(0)

    @pl.when(i == 0)
    def _():
        total = got_ref[0].astype(f32)
        for j in range(1, got_ref.shape[0]):
            total = total + got_ref[j].astype(f32)
        for h in range(heads):
            d = total[:, h * 2 * HD : (h + 1) * 2 * HD]
            mean_square = jnp.mean(d * d, -1, keepdims=True)
            g = gain_ref[0:1, h * 2 * HD : (h + 1) * 2 * HD]
            n_s[:, h * 2 * HD : (h + 1) * 2 * HD] = (out_factor * d / jnp.sqrt(mean_square + norm_eps) * g).astype(bf16)

    share = jnp.dot(n_s[...], w_ref[...], preferred_element_type=f32)

    @pl.when(i < 2)
    def _():
        send_ref[0] = share.astype(bf16)

    @pl.when(i >= 2)
    def _():
        keep_ref[0] = share


def project(cols, got, gain, weight, heads):
    rows = got.shape[1]
    width = weight.shape[1] // 4
    return pl.pallas_call(
        lambda *r: project_kernel(heads, *r),
        out_shape=[
            jax.ShapeDtypeStruct((2, rows, width), bf16),
            jax.ShapeDtypeStruct((2, rows, width), f32),
        ],
        grid_spec=pltpu.PrefetchScalarGridSpec(
            num_scalar_prefetch=1,
            grid=(4,),
            in_specs=[
                pl.BlockSpec(got.shape, lambda i, cols: (0, 0, 0)),
                pl.BlockSpec(gain.shape, lambda i, cols: (0, 0)),
                pl.BlockSpec((weight.shape[0], width), lambda i, cols: (0, cols[i])),
            ],
            out_specs=[
                pl.BlockSpec((1, rows, width), lambda i, cols: (jnp.minimum(i, 1), 0, 0)),
                pl.BlockSpec((1, rows, width), lambda i, cols: (jnp.maximum(i, 2) - 2, 0, 0)),
            ],
            scratch_shapes=[pltpu.VMEM((rows, got.shape[2]), bf16)],
        ),
        compiler_params=pltpu.CompilerParams(vmem_limit_bytes=24 << 20),
        name="project",
    )(cols, got, gain, pltpu.with_memory_space_constraint(weight, pltpu.HBM))


def shift(x, axis, size, step):
    return lax.ppermute(x, axis, [(i, (i + step) % size) for i in range(size)])


def swap(x, axis, size, mask):
    return lax.ppermute(x, axis, [(i, i ^ mask) for i in range(size)])


def per_device(sizes, queries, keys, values, positions, lambda_vecs, head_gain, out_weight, residual):
    nz, nh, ny, nl, nc = sizes
    rows, width = queries.shape
    heads = lambda_vecs.shape[1]
    block = ((positions[::RUN].astype(f32) + 0.5) * (1.0 / RUN)).astype(jnp.int32).astype(bf16)
    ids = jnp.broadcast_to(jnp.pad(block, (0, width - block.shape[0]))[None, :], (16, width))
    where = jnp.stack([lax.axis_index("h"), lax.axis_index("y")]).astype(jnp.int32)

    q_mine = jnp.concatenate([queries, ids], 0)
    kv_mine = jnp.concatenate([keys, values, ids], 0)
    up, down = shift(kv_mine, "z", nz, 1), shift(kv_mine, "z", nz, -1)
    q_pair = swap(q_mine, "h", nh, 1)
    q_near = [swap(q_mine, "y", ny, d) for d in range(1, ny)]
    kv_parts = [kv_mine, up, down]
    up, down, q_pair, q_near = lax.optimization_barrier((up, down, q_pair, q_near))
    up, down = shift(up, "z", nz, 1), shift(down, "z", nz, -1)
    q_far = [swap(q_pair, "y", ny, d) for d in range(1, ny)]
    kv_parts += [up, down]
    up, down, q_far, q_near = lax.optimization_barrier((up, down, q_far, q_near))
    up, down = shift(up, "z", nz, 1), shift(down, "z", nz, -1)
    kv_parts += [up, down]
    q_parts = [q_mine, q_pair]
    for d in range(ny - 1):
        q_parts += [q_near[d], q_far[d]]
    near = [(i, 0, i, rows) for i in range(5)]
    far = [(0, 0, 0, rows), (1, 0, 1, rows), (2, 0, 3, 0)]
    before = attend(q_parts, kv_parts[:5], near, (3, 6, 8, 10), rows, heads)
    up, down, before = lax.optimization_barrier((up, down, before))
    last = [up, down, shift(up[:rows], "z", nz, 1), shift(down[rows:], "z", nz, -1)]
    o, lse = attend(q_parts, last, far, (2, 4, 6), rows, heads, before)

    pair = merge(lse, swap(lse, "h", nh, 1), rows)
    others = [swap(pair, "y", ny, d) for d in range(1, ny)]

    lam = (
        jnp.exp(jnp.sum(lambda_vecs[0] * lambda_vecs[1], -1))
        - jnp.exp(jnp.sum(lambda_vecs[2] * lambda_vecs[3], -1))
        + lambda_init
    )
    parts = weigh(where, lam, lse, [pair] + others, o, rows, heads)

    parts = parts.reshape(nh * ny, rows, width)
    got = lax.all_to_all(parts, ("h", "y"), 0, 0, tiled=False)
    l, c = lax.axis_index("l"), lax.axis_index("c")
    cols = jnp.stack([l * nc + 1 - c, (1 - l) * nc + 1 - c, l * nc + c, (1 - l) * nc + c]).astype(jnp.int32)
    send, keep = project(cols, got, head_gain.reshape(1, width), out_weight, heads)
    near = swap(send, "c", nc, 1)
    far = swap((keep[1] + near[1].astype(f32)).astype(bf16), "l", nl, 1)
    return (keep[0] + near[0].astype(f32) + far.astype(f32) + residual.astype(f32)).astype(bf16)


def solution(mesh):
    sizes = (8, 2, 4, 2, 2)
    fine = Mesh(mesh.devices.reshape(sizes), ("z", "h", "y", "l", "c"))
    ctx, tp = ("z", "h", "y"), ("l", "c")
    placed = (
        P(ctx, tp),
        P(ctx, tp),
        P(ctx, tp),
        P(ctx),
        P(None, tp, None),
        P(tp),
        P(tp, None),
        P(ctx, tp),
    )
    return jax.shard_map(
        lambda *a: per_device(sizes, *a), mesh=fine, in_specs=placed, out_specs=P(ctx, tp), check_vma=False
    )
```

```python
import math

import jax
import jax.numpy as jnp
from jax import lax
from jax.experimental import pallas as pl
from jax.experimental.pallas import tpu as pltpu
from jax.sharding import Mesh, PartitionSpec as P

lambda_init = 0.2
out_factor = 0.8
norm_eps = 1e-05

HD = 128
RUN = 72
TILE = 4
NEG = -1e30
FLOOR = -1e29
f32 = jnp.float32
bf16 = jnp.bfloat16


def attend_kernel(rows, spans, slots, spots, *refs):
    q_refs = [refs[0].at[i // 2, i % 2] for i in range(slots)]
    kv_refs, refs = refs[1:-10], refs[-10:]
    o_ref, lse_ref, q3, k3, v3, q_s, k_s, v_s, lse_s, order = refs
    head = pl.program_id(0)
    per = rows // RUN
    blocks = slots * per
    keys = len(spots) * per
    tile = TILE * RUN
    tiles = blocks // TILE
    scale = math.log2(math.e) / math.sqrt(HD)

    @pl.when(head == 0)
    def _():
        lse_s[...] = jnp.zeros_like(lse_s)
        first = lax.broadcasted_iota(jnp.int32, (16, HD), 0) == 0
        lanes = lax.broadcasted_iota(jnp.int32, (16, HD), 1)

        def numbers(part):
            tail = part[part.shape[0] - 16 :, :HD].astype(f32)
            weight = jnp.where(first & (lanes < per), jnp.where(lanes == 0, float(HD), 1.0), 0.0)
            both = jnp.sum(tail * weight).astype(jnp.int32)
            return [lax.div(both, HD), lax.rem(both, HD)]

        kb = [v for k, kr, v, vr in spots for v in numbers(kv_refs[v])]
        qb = [v for p in q_refs for v in numbers(p)]
        for numbered, row in ((kb, 0), (qb, 2)):
            for i in range(len(numbered)):
                rank = jnp.int32(0)
                for j in range(len(numbered)):
                    rank = rank + (numbered[j] < numbered[i]).astype(jnp.int32)
                order[row, i] = rank
                if row == 0:
                    order[1, rank] = numbered[i]
                else:
                    order[3, rank] = i
                    order[4, rank] = numbered[i]
        for t in range(tiles):
            last = order[4, t * TILE + TILE - 1]
            need = jnp.int32(0)
            for j in range(keys):
                need = need + (kb[j] <= last).astype(jnp.int32)
            order[5, t] = need

    for i in range(keys):
        k, kr, v, vr = spots[i // per]
        d = i % per * RUN
        r = order[0, i]
        k3[r] = kv_refs[k][kr + d : kr + d + RUN, :]
        v3[r] = kv_refs[v][vr + d : vr + d + RUN, :]
    for i in range(blocks):
        d = i % per * RUN
        q3[order[2, i]] = q_refs[i // per][d : d + RUN, :]
    for i in range(keys):
        k_s[i * RUN : (i + 1) * RUN, :] = k3[i]
        v_s[i * RUN : (i + 1) * RUN, :] = v3[i]
    for i in range(blocks):
        q_s[i * RUN : (i + 1) * RUN, :] = q3[i]

    col = lax.broadcasted_iota(jnp.int32, (1, keys * RUN), 1)
    kpos = lax.rem(col, RUN)
    for i in range(keys):
        kpos = kpos + jnp.where(lax.div(col, RUN) == i, order[1, i] * RUN, 0)
    row = lax.broadcasted_iota(jnp.int32, (tile, 1), 0)
    lane = lax.broadcasted_iota(jnp.int32, (RUN, HD), 1)

    def one_tile(t, carry):
        need = order[5, t]
        start = pl.multiple_of(t * tile, tile)
        qpos = lax.rem(row, RUN)
        for i in range(TILE):
            qpos = qpos + jnp.where(lax.div(row, RUN) == i, order[4, t * TILE + i] * RUN, 0)

        def put(a, num, lse):
            for i in range(TILE):
                g = order[3, t * TILE + i]
                o = num[i * RUN : (i + 1) * RUN]
                e = lse[i * RUN : (i + 1) * RUN]
                o_ref[g, :, a * 2 * HD : (a + 1) * 2 * HD] = o.astype(bf16)
                lse_s[g] = jnp.where(lane == head * 2 + a, e, lse_s[g])

        for low, high in zip((0,) + spans[:-1], spans):

            @pl.when((need > low) & (need <= high))
            def _(span=high * RUN):
                allowed = kpos[:, :span] <= qpos
                ss = [
                    lax.dot_general(
                        q_s[pl.ds(start, tile), a * HD : (a + 1) * HD],
                        k_s[:span, a * HD : (a + 1) * HD],
                        (((1,), (1,)), ((), ())),
                        preferred_element_type=f32,
                    )
                    for a in range(2)
                ]
                ps = []
                for a in range(2):
                    s = jnp.where(allowed, ss[a], NEG)
                    m = jnp.maximum(jnp.max(s, -1, keepdims=True), FLOOR) * scale
                    p = jnp.exp2(s * scale - m)
                    ps.append((p.astype(bf16), m, jnp.sum(p, -1, keepdims=True)))
                for a in range(2):
                    p, m, total = ps[a]
                    num = jnp.dot(p, v_s[:span, :], preferred_element_type=f32)
                    some = total > 0.0
                    safe = jnp.where(some, total, 1.0)
                    put(a, num * (1.0 / safe), jnp.where(some, m + jnp.log2(safe), NEG))

        @pl.when(need == 0)
        def _():
            for a in range(2):
                put(a, jnp.zeros((tile, 2 * HD), f32), jnp.full((tile, 1), NEG, f32))

        return carry

    lax.fori_loop(0, tiles, one_tile, 0)

    @pl.when(head == pl.num_programs(0) - 1)
    def _():
        lse_ref[...] = jnp.transpose(lse_s[...].reshape(blocks * RUN, HD))[: lse_ref.shape[0], :]


def attend(q_pair, kv_parts, spots, spans, rows, heads):
    ny, _, pad, width = q_pair.shape
    slots = 2 * ny
    blocks = slots * rows // RUN
    keys = len(spots) * rows // RUN
    ins = [pltpu.with_memory_space_constraint(x, pltpu.HBM) for x in [q_pair, *kv_parts]]
    return pl.pallas_call(
        lambda *r: attend_kernel(rows, spans, slots, spots, *r),
        out_shape=[
            jax.ShapeDtypeStruct((blocks, RUN, heads * 4 * HD), bf16),
            jax.ShapeDtypeStruct((8, blocks * RUN), f32),
        ],
        grid_spec=pltpu.PrefetchScalarGridSpec(
            num_scalar_prefetch=0,
            grid=(heads,),
            in_specs=[pl.BlockSpec((ny, 2, pad, 2 * HD), lambda h: (0, 0, 0, h))]
            + [pl.BlockSpec((x.shape[0], 2 * HD), lambda h: (0, h)) for x in kv_parts],
            out_specs=[
                pl.BlockSpec((blocks, RUN, 4 * HD), lambda h: (0, 0, h)),
                pl.BlockSpec((8, blocks * RUN), lambda h: (0, 0)),
            ],
            scratch_shapes=[
                pltpu.VMEM((blocks, RUN, 2 * HD), bf16),
                pltpu.VMEM((keys, RUN, 2 * HD), bf16),
                pltpu.VMEM((keys, RUN, 2 * HD), bf16),
                pltpu.VMEM((blocks * RUN, 2 * HD), bf16),
                pltpu.VMEM((keys * RUN, 2 * HD), bf16),
                pltpu.VMEM((keys * RUN, 2 * HD), bf16),
                pltpu.VMEM((blocks, RUN, HD), f32),
                pltpu.SMEM((6, 128), jnp.int32),
            ],
        ),
        compiler_params=pltpu.CompilerParams(vmem_limit_bytes=36 << 20),
        cost_estimate=pl.CostEstimate(
            flops=heads * 2 * blocks * keys * RUN * RUN * 6 * HD * 8,
            bytes_accessed=(slots * 2 + len(spots) * 2) * rows * heads * 4 * HD,
            transcendentals=heads * 2 * blocks * keys * RUN * RUN,
        ),
        name="attend",
    )(*ins)


def logsum(parts):
    top = parts[0]
    for p in parts[1:]:
        top = jnp.maximum(top, p)
    total = jnp.exp2(parts[0] - top)
    for p in parts[1:]:
        total = total + jnp.exp2(p - top)
    return top + jnp.log2(total)


def reorder(x, rows, mask):
    slots = x.shape[1] // rows
    return jnp.concatenate([x[:, (s ^ mask) * rows : ((s ^ mask) + 1) * rows] for s in range(slots)], 1)


def merge_kernel(rows, a_ref, b_ref, o_ref):
    o_ref[...] = logsum([a_ref[...], reorder(b_ref[...], rows, 1)])


def merge(a, b, rows):
    vm = pl.BlockSpec(memory_space=pltpu.VMEM)
    return pl.pallas_call(
        lambda *r: merge_kernel(rows, *r),
        out_shape=jax.ShapeDtypeStruct(a.shape, a.dtype),
        in_specs=[vm, vm],
        out_specs=vm,
        compiler_params=pltpu.CompilerParams(vmem_limit_bytes=4 << 20),
        name="merge",
    )(a, b)


def weigh_kernel(heads, where, lam, lse_ref, *refs):
    all_refs, o_ref, out_ref, w_s = refs[:-3], refs[-3], refs[-2], refs[-1]
    j = pl.program_id(0)
    rows = out_ref.shape[2]

    @pl.when(j == 0)
    def _():
        whole = logsum([r[...] for r in all_refs])
        w = jnp.exp2(lse_ref[...] - whole)
        w = jnp.concatenate([w, jnp.zeros((HD - w.shape[0], w.shape[1]), f32)], 0)
        w_s[...] = jnp.transpose(w)

    for d in range(2):
        w = w_s[pl.ds(pl.multiple_of((2 * j + d) * rows, rows), rows), :]
        o = o_ref[d * (rows // RUN) : (d + 1) * (rows // RUN)]
        place = where[0] ^ d
        for h in range(heads):
            w1 = w[:, 2 * h : 2 * h + 1]
            w2 = w[:, 2 * h + 1 : 2 * h + 2] * lam[h]
            o1 = o[:, :, h * 4 * HD : h * 4 * HD + 2 * HD].reshape(rows, 2 * HD).astype(f32)
            o2 = o[:, :, h * 4 * HD + 2 * HD : (h + 1) * 4 * HD].reshape(rows, 2 * HD).astype(f32)
            out_ref[place, 0, :, h * 2 * HD : (h + 1) * 2 * HD] = (w1 * o1 - w2 * o2).astype(bf16)


def weigh(where, lam, lse, lses, o, rows, heads):
    pairs = lse.shape[1] // rows // 2
    return pl.pallas_call(
        lambda *r: weigh_kernel(heads, *r),
        out_shape=jax.ShapeDtypeStruct((2, pairs, rows, heads * 2 * HD), bf16),
        grid_spec=pltpu.PrefetchScalarGridSpec(
            num_scalar_prefetch=2,
            grid=(pairs,),
            in_specs=[pl.BlockSpec(lse.shape, lambda j, *_: (0, 0))] * (1 + len(lses))
            + [pl.BlockSpec((2 * rows // RUN, RUN, heads * 4 * HD), lambda j, *_: (j, 0, 0))],
            out_specs=pl.BlockSpec(
                (2, 1, rows, heads * 2 * HD), lambda j, where, lam: (0, j, 0, 0)
            ),
            scratch_shapes=[pltpu.VMEM((2 * pairs * rows, HD), f32)],
        ),
        compiler_params=pltpu.CompilerParams(vmem_limit_bytes=20 << 20),
        name="weigh",
    )(where, lam, lse, *lses, o)


def norm(got_ref, gain_ref, n_s, heads):
    total = got_ref[0].astype(f32)
    for j in range(1, got_ref.shape[0]):
        total = total + got_ref[j].astype(f32)
    for h in range(heads):
        d = total[:, h * 2 * HD : (h + 1) * 2 * HD]
        mean_square = jnp.mean(d * d, -1, keepdims=True)
        g = gain_ref[0:1, h * 2 * HD : (h + 1) * 2 * HD]
        n_s[:, h * 2 * HD : (h + 1) * 2 * HD] = (out_factor * d / jnp.sqrt(mean_square + norm_eps) * g).astype(bf16)


def project_kernel(heads, cols, *refs):
    i = pl.program_id(0)
    if heads:
        got_ref, gain_ref, w_ref, send_ref, keep_ref, n_ref = refs

        @pl.when(i == 0)
        def _():
            norm(got_ref, gain_ref, n_ref, heads)

    else:
        n_ref, w_ref, send_ref, keep_ref = refs
    share = jnp.dot(n_ref[...], w_ref[...], preferred_element_type=f32)

    @pl.when(i == 0)
    def _():
        send_ref[...] = share.astype(bf16)

    @pl.when(i == 1)
    def _():
        keep_ref[...] = share


def project(cols, ins, weight, rows, heads=0):
    depth = weight.shape[0]
    width = weight.shape[1] // 4
    zeros = lambda x: pl.BlockSpec(x.shape, lambda i, cols: (0,) * len(x.shape))
    outs = [
        jax.ShapeDtypeStruct((rows, width), bf16),
        jax.ShapeDtypeStruct((rows, width), f32),
    ] + [jax.ShapeDtypeStruct((rows, depth), bf16)] * bool(heads)
    return pl.pallas_call(
        lambda *r: project_kernel(heads, *r),
        out_shape=outs,
        grid_spec=pltpu.PrefetchScalarGridSpec(
            num_scalar_prefetch=1,
            grid=(2,),
            in_specs=[zeros(x) for x in ins] + [pl.BlockSpec((depth, width), lambda i, cols: (0, cols[i]))],
            out_specs=[zeros(x) for x in outs],
        ),
        compiler_params=pltpu.CompilerParams(vmem_limit_bytes=24 << 20),
        cost_estimate=pl.CostEstimate(flops=rows * depth * width * 32, bytes_accessed=depth * width * 4, transcendentals=0),
        name="project",
    )(cols, *ins, pltpu.with_memory_space_constraint(weight, pltpu.HBM))


def shift(x, axis, size, step):
    return lax.ppermute(x, axis, [(i, (i + step) % size) for i in range(size)])


def swap(x, axis, size, mask):
    return lax.ppermute(x, axis, [(i, i ^ mask) for i in range(size)])


def per_device(sizes, queries, keys, values, positions, lambda_vecs, head_gain, out_weight, residual):
    nz, nh, ny, nl, nc = sizes
    rows, width = queries.shape
    heads = lambda_vecs.shape[1]
    block = ((positions[::RUN].astype(f32) + 0.5) * (1.0 / RUN)).astype(jnp.int32).astype(bf16)
    ids = jnp.broadcast_to(jnp.pad(block, (0, width - block.shape[0]))[None, :], (16, width))
    where = lax.axis_index("h").astype(jnp.int32).reshape(1)

    q_mine = jnp.concatenate([queries, ids], 0)
    kv_mine = jnp.concatenate([keys, values, ids], 0)
    q_far = swap(q_mine, "h", nh, 1)
    up, down = shift(kv_mine, "z", nz, 1), shift(kv_mine, "z", nz, -1)
    kv_parts = [kv_mine, up, down]
    up, down, q_far = lax.optimization_barrier((up, down, q_far))
    q_pair = lax.all_gather(jnp.stack([q_mine, q_far]), "y", axis=0)
    for _ in range(2):
        up, down = shift(up, "z", nz, 1), shift(down, "z", nz, -1)
        kv_parts += [up, down]
    kv_parts += [shift(up[:rows], "z", nz, 1), shift(down[rows:], "z", nz, -1)]
    spots = [(i, 0, i, rows) for i in range(nz - 1)] + [(nz - 1, 0, nz, 0)]
    o, lse = attend(q_pair, kv_parts, spots, (4, 8, 12, 16), rows, heads)

    pair = merge(lse, swap(lse, "h", nh, 1), rows)
    others = [swap(pair, "y", ny, d) for d in range(1, ny)]

    lam = (
        jnp.exp(jnp.sum(lambda_vecs[0] * lambda_vecs[1], -1))
        - jnp.exp(jnp.sum(lambda_vecs[2] * lambda_vecs[3], -1))
        + lambda_init
    )
    parts = weigh(where, lam, lse, [pair] + others, o, rows, heads)

    parts = parts.reshape(nh * ny, rows, width)
    got = lax.all_to_all(parts, ("h", "y"), 0, 0, tiled=False)
    l, c = lax.axis_index("l"), lax.axis_index("c")
    cols = [jnp.stack([r * nc + 1 - c, r * nc + c]).astype(jnp.int32) for r in (1 - l, l)]
    send, keep, normed = project(cols[0], [got, head_gain.reshape(1, width)], out_weight, rows, heads)
    away = (keep + swap(send, "c", nc, 1).astype(f32)).astype(bf16)
    away, normed = lax.optimization_barrier((away, normed))
    far = swap(away, "l", nl, 1)
    send, keep = project(cols[1], [normed], out_weight, rows)
    rest = lax.optimization_barrier(far.astype(f32) + residual.astype(f32))
    return (rest + keep + swap(send, "c", nc, 1).astype(f32)).astype(bf16)


def solution(mesh):
    sizes = (8, 2, 4, 2, 2)
    fine = Mesh(mesh.devices.reshape(sizes), ("z", "h", "y", "l", "c"))
    ctx, tp = ("z", "h", "y"), ("l", "c")
    placed = (
        P(ctx, tp),
        P(ctx, tp),
        P(ctx, tp),
        P(ctx),
        P(None, tp, None),
        P(tp),
        P(tp, None),
        P(ctx, tp),
    )
    return jax.shard_map(
        lambda *a: per_device(sizes, *a), mesh=fine, in_specs=placed, out_specs=P(ctx, tp), check_vma=False
    )
```

```python
import math

import jax
import jax.numpy as jnp
from jax import lax
from jax.experimental import pallas as pl
from jax.experimental.pallas import tpu as pltpu
from jax.sharding import Mesh, PartitionSpec as P

lambda_init = 0.2
out_factor = 0.8
norm_eps = 1e-05

HD = 128
RUN = 72
TILE = 4
NEG = -1e30
FLOOR = -1e29
f32 = jnp.float32
bf16 = jnp.bfloat16


def attend_kernel(rows, spans, slots, spots, *refs):
    q_refs = [refs[0].at[i] for i in range(slots)]
    kv_refs, refs = refs[1:-10], refs[-10:]
    o_ref, lse_ref, q3, k3, v3, q_s, k_s, v_s, lse_s, order = refs
    head = pl.program_id(0)
    per = rows // RUN
    blocks = slots * per
    keys = len(spots) * per
    tile = TILE * RUN
    tiles = blocks // TILE
    scale = math.log2(math.e) / math.sqrt(HD)

    @pl.when(head == 0)
    def _():
        lse_s[...] = jnp.zeros_like(lse_s)
        first = lax.broadcasted_iota(jnp.int32, (16, HD), 0) == 0
        lanes = lax.broadcasted_iota(jnp.int32, (16, HD), 1)

        def numbers(part):
            tail = part[part.shape[0] - 16 :, :HD].astype(f32)
            weight = jnp.where(first & (lanes < per), jnp.where(lanes == 0, float(HD), 1.0), 0.0)
            both = jnp.sum(tail * weight).astype(jnp.int32)
            return [lax.div(both, HD), lax.rem(both, HD)]

        kb = [v for k, kr, v, vr in spots for v in numbers(kv_refs[v])]
        qb = [v for p in q_refs for v in numbers(p)]
        for numbered, row in ((kb, 0), (qb, 2)):
            for i in range(len(numbered)):
                rank = jnp.int32(0)
                for j in range(len(numbered)):
                    rank = rank + (numbered[j] < numbered[i]).astype(jnp.int32)
                order[row, i] = rank
                if row == 0:
                    order[1, rank] = numbered[i]
                else:
                    order[3, rank] = i
                    order[4, rank] = numbered[i]
        for t in range(tiles):
            last = order[4, t * TILE + TILE - 1]
            need = jnp.int32(0)
            for j in range(keys):
                need = need + (kb[j] <= last).astype(jnp.int32)
            order[5, t] = need

    for i in range(keys):
        k, kr, v, vr = spots[i // per]
        d = i % per * RUN
        r = order[0, i]
        k3[r] = kv_refs[k][kr + d : kr + d + RUN, :]
        v3[r] = kv_refs[v][vr + d : vr + d + RUN, :]
    for i in range(blocks):
        d = i % per * RUN
        q3[order[2, i]] = q_refs[i // per][d : d + RUN, :]
    for i in range(keys):
        k_s[i * RUN : (i + 1) * RUN, :] = k3[i]
        v_s[i * RUN : (i + 1) * RUN, :] = v3[i]
    for i in range(blocks):
        q_s[i * RUN : (i + 1) * RUN, :] = q3[i]

    col = lax.broadcasted_iota(jnp.int32, (1, keys * RUN), 1)
    kpos = lax.rem(col, RUN)
    for i in range(keys):
        kpos = kpos + jnp.where(lax.div(col, RUN) == i, order[1, i] * RUN, 0)
    row = lax.broadcasted_iota(jnp.int32, (tile, 1), 0)
    lane = lax.broadcasted_iota(jnp.int32, (RUN, HD), 1)

    def one_tile(t, carry):
        need = order[5, t]
        start = pl.multiple_of(t * tile, tile)
        qpos = lax.rem(row, RUN)
        for i in range(TILE):
            qpos = qpos + jnp.where(lax.div(row, RUN) == i, order[4, t * TILE + i] * RUN, 0)

        def put(a, num, lse):
            for i in range(TILE):
                g = order[3, t * TILE + i]
                o = num[i * RUN : (i + 1) * RUN]
                e = lse[i * RUN : (i + 1) * RUN]
                o_ref[g, :, a * 2 * HD : (a + 1) * 2 * HD] = o.astype(bf16)
                lse_s[g] = jnp.where(lane == head * 2 + a, e, lse_s[g])

        for low, high in zip((0,) + spans[:-1], spans):

            @pl.when((need > low) & (need <= high))
            def _(span=high * RUN):
                allowed = kpos[:, :span] <= qpos
                ss = [
                    lax.dot_general(
                        q_s[pl.ds(start, tile), a * HD : (a + 1) * HD],
                        k_s[:span, a * HD : (a + 1) * HD],
                        (((1,), (1,)), ((), ())),
                        preferred_element_type=f32,
                    )
                    for a in range(2)
                ]
                ps = []
                for a in range(2):
                    s = jnp.where(allowed, ss[a], NEG)
                    m = jnp.maximum(jnp.max(s, -1, keepdims=True), FLOOR) * scale
                    p = jnp.exp2(s * scale - m)
                    ps.append((p.astype(bf16), m, jnp.sum(p, -1, keepdims=True)))
                for a in range(2):
                    p, m, total = ps[a]
                    num = jnp.dot(p, v_s[:span, :], preferred_element_type=f32)
                    some = total > 0.0
                    safe = jnp.where(some, total, 1.0)
                    put(a, num * (1.0 / safe), jnp.where(some, m + jnp.log2(safe), NEG))

        @pl.when(need == 0)
        def _():
            for a in range(2):
                put(a, jnp.zeros((tile, 2 * HD), f32), jnp.full((tile, 1), NEG, f32))

        return carry

    lax.fori_loop(0, tiles, one_tile, 0)

    @pl.when(head == pl.num_programs(0) - 1)
    def _():
        lse_ref[...] = jnp.transpose(lse_s[...].reshape(blocks * RUN, HD))[: lse_ref.shape[0], :]


def attend(q_all, kv_parts, spots, spans, rows, heads):
    slots, pad, width = q_all.shape
    blocks = slots * rows // RUN
    keys = len(spots) * rows // RUN
    ins = [pltpu.with_memory_space_constraint(x, pltpu.HBM) for x in [q_all, *kv_parts]]
    return pl.pallas_call(
        lambda *r: attend_kernel(rows, spans, slots, spots, *r),
        out_shape=[
            jax.ShapeDtypeStruct((blocks, RUN, heads * 4 * HD), bf16),
            jax.ShapeDtypeStruct((8, blocks * RUN), f32),
        ],
        grid_spec=pltpu.PrefetchScalarGridSpec(
            num_scalar_prefetch=0,
            grid=(heads,),
            in_specs=[pl.BlockSpec((slots, pad, 2 * HD), lambda h: (0, 0, h))]
            + [pl.BlockSpec((x.shape[0], 2 * HD), lambda h: (0, h)) for x in kv_parts],
            out_specs=[
                pl.BlockSpec((blocks, RUN, 4 * HD), lambda h: (0, 0, h)),
                pl.BlockSpec((8, blocks * RUN), lambda h: (0, 0)),
            ],
            scratch_shapes=[
                pltpu.VMEM((blocks, RUN, 2 * HD), bf16),
                pltpu.VMEM((keys, RUN, 2 * HD), bf16),
                pltpu.VMEM((keys, RUN, 2 * HD), bf16),
                pltpu.VMEM((blocks * RUN, 2 * HD), bf16),
                pltpu.VMEM((keys * RUN, 2 * HD), bf16),
                pltpu.VMEM((keys * RUN, 2 * HD), bf16),
                pltpu.VMEM((blocks, RUN, HD), f32),
                pltpu.SMEM((6, 128), jnp.int32),
            ],
        ),
        compiler_params=pltpu.CompilerParams(vmem_limit_bytes=36 << 20),
        cost_estimate=pl.CostEstimate(
            flops=heads * 2 * blocks * keys * RUN * RUN * 6 * HD * 8,
            bytes_accessed=(slots * 2 + len(spots) * 2) * rows * heads * 4 * HD,
            transcendentals=heads * 2 * blocks * keys * RUN * RUN,
        ),
        name="attend",
    )(*ins)


def logsum(parts):
    top = parts[0]
    for p in parts[1:]:
        top = jnp.maximum(top, p)
    total = jnp.exp2(parts[0] - top)
    for p in parts[1:]:
        total = total + jnp.exp2(p - top)
    return top + jnp.log2(total)


def merge_kernel(a_ref, b_ref, o_ref):
    o_ref[...] = logsum([a_ref[...], b_ref[...]])


def merge(a, b):
    vm = pl.BlockSpec(memory_space=pltpu.VMEM)
    return pl.pallas_call(
        merge_kernel,
        out_shape=jax.ShapeDtypeStruct(a.shape, a.dtype),
        in_specs=[vm, vm],
        out_specs=vm,
        compiler_params=pltpu.CompilerParams(vmem_limit_bytes=4 << 20),
        name="merge",
    )(a, b)


def weigh_kernel(heads, lam, lse_ref, *refs):
    all_refs, o_ref, out_ref, w_s = refs[:-3], refs[-3], refs[-2], refs[-1]
    j = pl.program_id(0)
    slots, rows = out_ref.shape[:2]

    @pl.when(j == 0)
    def _():
        whole = logsum([r[...] for r in all_refs])
        w = jnp.exp2(lse_ref[...] - whole)
        w = jnp.concatenate([w, jnp.zeros((HD - w.shape[0], w.shape[1]), f32)], 0)
        w_s[...] = jnp.transpose(w)

    for d in range(slots):
        w = w_s[pl.ds(pl.multiple_of((slots * j + d) * rows, rows), rows), :]
        o = o_ref[d * (rows // RUN) : (d + 1) * (rows // RUN)]
        for h in range(heads):
            w1 = w[:, 2 * h : 2 * h + 1]
            w2 = w[:, 2 * h + 1 : 2 * h + 2] * lam[h]
            o1 = o[:, :, h * 4 * HD : h * 4 * HD + 2 * HD].reshape(rows, 2 * HD).astype(f32)
            o2 = o[:, :, h * 4 * HD + 2 * HD : (h + 1) * 4 * HD].reshape(rows, 2 * HD).astype(f32)
            out_ref[d, :, h * 2 * HD : (h + 1) * 2 * HD] = (w1 * o1 - w2 * o2).astype(bf16)


def weigh(lam, lse, lses, o, rows, heads):
    slots = lse.shape[1] // rows
    return pl.pallas_call(
        lambda *r: weigh_kernel(heads, *r),
        out_shape=jax.ShapeDtypeStruct((slots, rows, heads * 2 * HD), bf16),
        grid_spec=pltpu.PrefetchScalarGridSpec(
            num_scalar_prefetch=1,
            grid=(slots // 2,),
            in_specs=[pl.BlockSpec(lse.shape, lambda j, lam: (0, 0))] * (1 + len(lses))
            + [pl.BlockSpec((2 * rows // RUN, RUN, heads * 4 * HD), lambda j, lam: (j, 0, 0))],
            out_specs=pl.BlockSpec((2, rows, heads * 2 * HD), lambda j, lam: (j, 0, 0)),
            scratch_shapes=[pltpu.VMEM((slots * rows, HD), f32)],
        ),
        compiler_params=pltpu.CompilerParams(vmem_limit_bytes=20 << 20),
        name="weigh",
    )(lam, lse, *lses, o)


def norm(got_ref, gain_ref, n_s, heads):
    total = got_ref[0].astype(f32)
    for j in range(1, got_ref.shape[0]):
        total = total + got_ref[j].astype(f32)
    for h in range(heads):
        d = total[:, h * 2 * HD : (h + 1) * 2 * HD]
        mean_square = jnp.mean(d * d, -1, keepdims=True)
        g = gain_ref[0:1, h * 2 * HD : (h + 1) * 2 * HD]
        n_s[:, h * 2 * HD : (h + 1) * 2 * HD] = (out_factor * d / jnp.sqrt(mean_square + norm_eps) * g).astype(bf16)


def project_kernel(heads, cols, *refs):
    i = pl.program_id(0)
    if heads:
        got_ref, gain_ref, w_ref, send_ref, keep_ref, n_ref = refs

        @pl.when(i == 0)
        def _():
            norm(got_ref, gain_ref, n_ref, heads)

    else:
        n_ref, w_ref, send_ref, keep_ref = refs
    share = jnp.dot(n_ref[...], w_ref[...], preferred_element_type=f32)

    @pl.when(i == 0)
    def _():
        send_ref[...] = share.astype(bf16)

    @pl.when(i == 1)
    def _():
        keep_ref[...] = share


def project(cols, ins, weight, rows, heads=0):
    depth = weight.shape[0]
    width = weight.shape[1] // 4
    zeros = lambda x: pl.BlockSpec(x.shape, lambda i, cols: (0,) * len(x.shape))
    outs = [
        jax.ShapeDtypeStruct((rows, width), bf16),
        jax.ShapeDtypeStruct((rows, width), f32),
    ] + [jax.ShapeDtypeStruct((rows, depth), bf16)] * bool(heads)
    return pl.pallas_call(
        lambda *r: project_kernel(heads, *r),
        out_shape=outs,
        grid_spec=pltpu.PrefetchScalarGridSpec(
            num_scalar_prefetch=1,
            grid=(2,),
            in_specs=[zeros(x) for x in ins] + [pl.BlockSpec((depth, width), lambda i, cols: (0, cols[i]))],
            out_specs=[zeros(x) for x in outs],
        ),
        compiler_params=pltpu.CompilerParams(vmem_limit_bytes=24 << 20),
        cost_estimate=pl.CostEstimate(flops=rows * depth * width * 32, bytes_accessed=depth * width * 4, transcendentals=0),
        name="project",
    )(cols, *ins, pltpu.with_memory_space_constraint(weight, pltpu.HBM))


def shift(x, axis, size, step):
    return lax.ppermute(x, axis, [(i, (i + step) % size) for i in range(size)])


def swap(x, axis, size, mask):
    return lax.ppermute(x, axis, [(i, i ^ mask) for i in range(size)])


def per_device(sizes, queries, keys, values, positions, lambda_vecs, head_gain, out_weight, residual):
    nz, nh, ny, nl, nc = sizes
    rows, width = queries.shape
    heads = lambda_vecs.shape[1]
    block = ((positions[::RUN].astype(f32) + 0.5) * (1.0 / RUN)).astype(jnp.int32).astype(bf16)
    ids = jnp.broadcast_to(jnp.pad(block, (0, width - block.shape[0]))[None, :], (16, width))
    q_mine = jnp.concatenate([queries, ids], 0)
    q_all = lax.all_to_all(jnp.broadcast_to(q_mine[None], (nh * ny, *q_mine.shape)), ("h", "y"), 0, 0)
    kv_mine = jnp.concatenate([keys, values, ids], 0)
    up, down = shift(kv_mine, "z", nz, 1), shift(kv_mine, "z", nz, -1)
    kv_parts = [kv_mine, up, down]
    for _ in range(2):
        up, down = shift(up, "z", nz, 1), shift(down, "z", nz, -1)
        kv_parts += [up, down]
    kv_parts += [shift(up[:rows], "z", nz, 1), shift(down[rows:], "z", nz, -1)]
    spots = [(i, 0, i, rows) for i in range(nz - 1)] + [(nz - 1, 0, nz, 0)]
    o, lse = attend(q_all, kv_parts, spots, (4, 8, 12, 16), rows, heads)

    pair = merge(lse, swap(lse, "h", nh, 1))
    others = [swap(pair, "y", ny, d) for d in range(1, ny)]

    lam = (
        jnp.exp(jnp.sum(lambda_vecs[0] * lambda_vecs[1], -1))
        - jnp.exp(jnp.sum(lambda_vecs[2] * lambda_vecs[3], -1))
        + lambda_init
    )
    parts = weigh(lam, lse, [pair] + others, o, rows, heads)

    got = lax.all_to_all(parts, ("h", "y"), 0, 0, tiled=False)
    l, c = lax.axis_index("l"), lax.axis_index("c")
    cols = [jnp.stack([r * nc + 1 - c, r * nc + c]).astype(jnp.int32) for r in (1 - l, l)]
    send, keep, normed = project(cols[0], [got, head_gain.reshape(1, width)], out_weight, rows, heads)
    away = (keep + swap(send, "c", nc, 1).astype(f32)).astype(bf16)
    away, normed = lax.optimization_barrier((away, normed))
    far = swap(away, "l", nl, 1)
    send, keep = project(cols[1], [normed], out_weight, rows)
    rest = lax.optimization_barrier(far.astype(f32) + residual.astype(f32))
    return (rest + keep + swap(send, "c", nc, 1).astype(f32)).astype(bf16)


def solution(mesh):
    sizes = (8, 2, 4, 2, 2)
    fine = Mesh(mesh.devices.reshape(sizes), ("z", "h", "y", "l", "c"))
    ctx, tp = ("z", "h", "y"), ("l", "c")
    placed = (
        P(ctx, tp),
        P(ctx, tp),
        P(ctx, tp),
        P(ctx),
        P(None, tp, None),
        P(tp),
        P(tp, None),
        P(ctx, tp),
    )
    return jax.shard_map(
        lambda *a: per_device(sizes, *a), mesh=fine, in_specs=placed, out_specs=P(ctx, tp), check_vma=False
    )
```

```python
import math

import jax
import jax.numpy as jnp
from jax import lax
from jax.experimental import pallas as pl
from jax.experimental.pallas import tpu as pltpu
from jax.sharding import Mesh, PartitionSpec as P

lambda_init = 0.2
out_factor = 0.8
norm_eps = 1e-05

HD = 128
RUN = 72
TILE = 4
NEG = -1e30
FLOOR = -1e29
f32 = jnp.float32
bf16 = jnp.bfloat16


def attend_kernel(rows, spans, slots, spots, *refs):
    q_refs = [refs[0].at[i] for i in range(slots)]
    kv_refs, refs = refs[1:-10], refs[-10:]
    o_ref, lse_ref, q3, k3, v3, q_s, k_s, v_s, lse_s, order = refs
    head = pl.program_id(0)
    per = rows // RUN
    blocks = slots * per
    keys = len(spots) * per
    tile = TILE * RUN
    tiles = blocks // TILE
    scale = math.log2(math.e) / math.sqrt(HD)

    @pl.when(head == 0)
    def _():
        lse_s[...] = jnp.zeros_like(lse_s)
        first = lax.broadcasted_iota(jnp.int32, (16, HD), 0) == 0
        lanes = lax.broadcasted_iota(jnp.int32, (16, HD), 1)

        def numbers(part):
            tail = part[part.shape[0] - 16 :, :HD].astype(f32)
            weight = jnp.where(first & (lanes < per), jnp.where(lanes == 0, float(HD), 1.0), 0.0)
            both = jnp.sum(tail * weight).astype(jnp.int32)
            return [lax.div(both, HD), lax.rem(both, HD)]

        kb = [v for k, kr, v, vr in spots for v in numbers(kv_refs[v])]
        qb = [v for p in q_refs for v in numbers(p)]
        for numbered, row in ((kb, 0), (qb, 2)):
            for i in range(len(numbered)):
                rank = jnp.int32(0)
                for j in range(len(numbered)):
                    rank = rank + (numbered[j] < numbered[i]).astype(jnp.int32)
                order[row, i] = rank
                if row == 0:
                    order[1, rank] = numbered[i]
                else:
                    order[3, rank] = i
                    order[4, rank] = numbered[i]
        for t in range(tiles):
            last = order[4, t * TILE + TILE - 1]
            need = jnp.int32(0)
            for j in range(keys):
                need = need + (kb[j] <= last).astype(jnp.int32)
            order[5, t] = need

    for i in range(keys):
        k, kr, v, vr = spots[i // per]
        d = i % per * RUN
        r = order[0, i]
        k3[r] = kv_refs[k][kr + d : kr + d + RUN, :]
        v3[r] = kv_refs[v][vr + d : vr + d + RUN, :]
    for i in range(blocks):
        d = i % per * RUN
        q3[order[2, i]] = q_refs[i // per][d : d + RUN, :]
    for i in range(keys):
        k_s[i * RUN : (i + 1) * RUN, :] = k3[i]
        v_s[i * RUN : (i + 1) * RUN, :] = v3[i]
    for i in range(blocks):
        q_s[i * RUN : (i + 1) * RUN, :] = q3[i]

    col = lax.broadcasted_iota(jnp.int32, (1, keys * RUN), 1)
    kpos = lax.rem(col, RUN)
    for i in range(keys):
        kpos = kpos + jnp.where(lax.div(col, RUN) == i, order[1, i] * RUN, 0)
    row = lax.broadcasted_iota(jnp.int32, (tile, 1), 0)
    lane = lax.broadcasted_iota(jnp.int32, (RUN, HD), 1)

    def one_tile(t, carry):
        need = order[5, t]
        start = pl.multiple_of(t * tile, tile)
        qpos = lax.rem(row, RUN)
        for i in range(TILE):
            qpos = qpos + jnp.where(lax.div(row, RUN) == i, order[4, t * TILE + i] * RUN, 0)

        def put(a, num, lse):
            for i in range(TILE):
                g = order[3, t * TILE + i]
                o = num[i * RUN : (i + 1) * RUN]
                e = lse[i * RUN : (i + 1) * RUN]
                o_ref[g, :, a * 2 * HD : (a + 1) * 2 * HD] = o.astype(bf16)
                lse_s[g] = jnp.where(lane == head * 2 + a, e, lse_s[g])

        for low, high in zip((0,) + spans[:-1], spans):

            @pl.when((need > low) & (need <= high))
            def _(span=high * RUN):
                allowed = kpos[:, :span] <= qpos
                ss = [
                    lax.dot_general(
                        q_s[pl.ds(start, tile), a * HD : (a + 1) * HD],
                        k_s[:span, a * HD : (a + 1) * HD],
                        (((1,), (1,)), ((), ())),
                        preferred_element_type=f32,
                    )
                    for a in range(2)
                ]
                ps = []
                for a in range(2):
                    s = jnp.where(allowed, ss[a], NEG)
                    m = jnp.maximum(jnp.max(s, -1, keepdims=True), FLOOR) * scale
                    p = jnp.exp2(s * scale - m)
                    ps.append((p.astype(bf16), m, jnp.sum(p, -1, keepdims=True)))
                for a in range(2):
                    p, m, total = ps[a]
                    num = jnp.dot(p, v_s[:span, :], preferred_element_type=f32)
                    some = total > 0.0
                    safe = jnp.where(some, total, 1.0)
                    put(a, num * (1.0 / safe), jnp.where(some, m + jnp.log2(safe), NEG))

        @pl.when(need == 0)
        def _():
            for a in range(2):
                put(a, jnp.zeros((tile, 2 * HD), f32), jnp.full((tile, 1), NEG, f32))

        return carry

    lax.fori_loop(0, tiles, one_tile, 0)

    @pl.when(head == pl.num_programs(0) - 1)
    def _():
        lse_ref[...] = jnp.transpose(lse_s[...].reshape(blocks * RUN, HD))[: lse_ref.shape[0], :]


def attend(q_all, kv_parts, spots, spans, rows, heads):
    slots, pad, width = q_all.shape
    blocks = slots * rows // RUN
    keys = len(spots) * rows // RUN
    ins = [pltpu.with_memory_space_constraint(x, pltpu.HBM) for x in kv_parts]
    return pl.pallas_call(
        lambda *r: attend_kernel(rows, spans, slots, spots, *r),
        out_shape=[
            jax.ShapeDtypeStruct((blocks, RUN, heads * 4 * HD), bf16),
            jax.ShapeDtypeStruct((8, blocks * RUN), f32),
        ],
        grid_spec=pltpu.PrefetchScalarGridSpec(
            num_scalar_prefetch=0,
            grid=(heads,),
            in_specs=[pl.BlockSpec((slots, pad, 2 * HD), lambda h: (0, 0, h))]
            + [pl.BlockSpec((x.shape[0], 2 * HD), lambda h: (0, h)) for x in kv_parts],
            out_specs=[
                pl.BlockSpec((blocks, RUN, 4 * HD), lambda h: (0, 0, h)),
                pl.BlockSpec((8, blocks * RUN), lambda h: (0, 0)),
            ],
            scratch_shapes=[
                pltpu.VMEM((blocks, RUN, 2 * HD), bf16),
                pltpu.VMEM((keys, RUN, 2 * HD), bf16),
                pltpu.VMEM((keys, RUN, 2 * HD), bf16),
                pltpu.VMEM((blocks * RUN, 2 * HD), bf16),
                pltpu.VMEM((keys * RUN, 2 * HD), bf16),
                pltpu.VMEM((keys * RUN, 2 * HD), bf16),
                pltpu.VMEM((blocks, RUN, HD), f32),
                pltpu.SMEM((6, 128), jnp.int32),
            ],
        ),
        compiler_params=pltpu.CompilerParams(vmem_limit_bytes=36 << 20),
        cost_estimate=pl.CostEstimate(
            flops=heads * 2 * blocks * keys * RUN * RUN * 6 * HD * 8,
            bytes_accessed=(slots * 2 + len(spots) * 2) * rows * heads * 4 * HD,
            transcendentals=heads * 2 * blocks * keys * RUN * RUN,
        ),
        name="attend",
    )(q_all, *ins)


def logsum(parts):
    top = parts[0]
    for p in parts[1:]:
        top = jnp.maximum(top, p)
    total = jnp.exp2(parts[0] - top)
    for p in parts[1:]:
        total = total + jnp.exp2(p - top)
    return top + jnp.log2(total)


def merge_kernel(a_ref, b_ref, o_ref):
    o_ref[...] = logsum([a_ref[...], b_ref[...]])


def merge(a, b):
    vm = pl.BlockSpec(memory_space=pltpu.VMEM)
    return pl.pallas_call(
        merge_kernel,
        out_shape=jax.ShapeDtypeStruct(a.shape, a.dtype),
        in_specs=[vm, vm],
        out_specs=vm,
        compiler_params=pltpu.CompilerParams(vmem_limit_bytes=4 << 20),
        name="merge",
    )(a, b)


def weigh_kernel(heads, lam, lse_ref, *refs):
    all_refs, o_ref, out_ref, w_s = refs[:-3], refs[-3], refs[-2], refs[-1]
    j = pl.program_id(0)
    slots, rows = out_ref.shape[:2]

    @pl.when(j == 0)
    def _():
        whole = logsum([r[...] for r in all_refs])
        w = jnp.exp2(lse_ref[...] - whole)
        w = jnp.concatenate([w, jnp.zeros((HD - w.shape[0], w.shape[1]), f32)], 0)
        w_s[...] = jnp.transpose(w)

    for d in range(slots):
        w = w_s[pl.ds(pl.multiple_of((slots * j + d) * rows, rows), rows), :]
        o = o_ref[d * (rows // RUN) : (d + 1) * (rows // RUN)]
        for h in range(heads):
            w1 = w[:, 2 * h : 2 * h + 1]
            w2 = w[:, 2 * h + 1 : 2 * h + 2] * lam[h]
            o1 = o[:, :, h * 4 * HD : h * 4 * HD + 2 * HD].reshape(rows, 2 * HD).astype(f32)
            o2 = o[:, :, h * 4 * HD + 2 * HD : (h + 1) * 4 * HD].reshape(rows, 2 * HD).astype(f32)
            out_ref[d, :, h * 2 * HD : (h + 1) * 2 * HD] = (w1 * o1 - w2 * o2).astype(bf16)


def weigh(lam, lse, lses, o, rows, heads):
    slots = lse.shape[1] // rows
    return pl.pallas_call(
        lambda *r: weigh_kernel(heads, *r),
        out_shape=jax.ShapeDtypeStruct((slots, rows, heads * 2 * HD), bf16),
        grid_spec=pltpu.PrefetchScalarGridSpec(
            num_scalar_prefetch=1,
            grid=(slots // 2,),
            in_specs=[pl.BlockSpec(lse.shape, lambda j, lam: (0, 0))] * (1 + len(lses))
            + [pl.BlockSpec((2 * rows // RUN, RUN, heads * 4 * HD), lambda j, lam: (j, 0, 0))],
            out_specs=pl.BlockSpec((2, rows, heads * 2 * HD), lambda j, lam: (j, 0, 0)),
            scratch_shapes=[pltpu.VMEM((slots * rows, HD), f32)],
        ),
        compiler_params=pltpu.CompilerParams(vmem_limit_bytes=20 << 20),
        name="weigh",
    )(lam, lse, *lses, o)


def norm(got_ref, gain_ref, n_s, heads):
    total = got_ref[0].astype(f32)
    for j in range(1, got_ref.shape[0]):
        total = total + got_ref[j].astype(f32)
    for h in range(heads):
        d = total[:, h * 2 * HD : (h + 1) * 2 * HD]
        mean_square = jnp.mean(d * d, -1, keepdims=True)
        g = gain_ref[0:1, h * 2 * HD : (h + 1) * 2 * HD]
        n_s[:, h * 2 * HD : (h + 1) * 2 * HD] = (out_factor * d / jnp.sqrt(mean_square + norm_eps) * g).astype(bf16)


def project_kernel(heads, cols, *refs):
    i = pl.program_id(0)
    if heads:
        got_ref, gain_ref, w_ref, send_ref, keep_ref, n_ref = refs

        @pl.when(i == 0)
        def _():
            norm(got_ref, gain_ref, n_ref, heads)

    else:
        n_ref, w_ref, send_ref, keep_ref = refs
    share = jnp.dot(n_ref[...], w_ref[...], preferred_element_type=f32)

    @pl.when(i == 0)
    def _():
        send_ref[...] = share.astype(bf16)

    @pl.when(i == 1)
    def _():
        keep_ref[...] = share


def project(cols, ins, weight, rows, heads=0):
    depth = weight.shape[0]
    width = weight.shape[1] // 4
    zeros = lambda x: pl.BlockSpec(x.shape, lambda i, cols: (0,) * len(x.shape))
    outs = [
        jax.ShapeDtypeStruct((rows, width), bf16),
        jax.ShapeDtypeStruct((rows, width), f32),
    ] + [jax.ShapeDtypeStruct((rows, depth), bf16)] * bool(heads)
    return pl.pallas_call(
        lambda *r: project_kernel(heads, *r),
        out_shape=outs,
        grid_spec=pltpu.PrefetchScalarGridSpec(
            num_scalar_prefetch=1,
            grid=(2,),
            in_specs=[zeros(x) for x in ins] + [pl.BlockSpec((depth, width), lambda i, cols: (0, cols[i]))],
            out_specs=[zeros(x) for x in outs],
        ),
        compiler_params=pltpu.CompilerParams(vmem_limit_bytes=24 << 20),
        cost_estimate=pl.CostEstimate(flops=rows * depth * width * 32, bytes_accessed=depth * width * 4, transcendentals=0),
        name="project",
    )(cols, *ins, pltpu.with_memory_space_constraint(weight, pltpu.HBM))


def repeat_kernel(x_ref, ids_ref, o_ref):
    rows = x_ref.shape[0]
    for i in range(o_ref.shape[0]):
        o_ref[i, :rows] = x_ref[...]
        o_ref[i, rows:] = ids_ref[...]


def repeat(x, ids, count):
    rows, width = x.shape
    vm = pl.BlockSpec(memory_space=pltpu.VMEM)
    return pl.pallas_call(
        repeat_kernel,
        out_shape=jax.ShapeDtypeStruct((count, rows + ids.shape[0], width), x.dtype),
        in_specs=[vm, vm],
        out_specs=vm,
        name="repeat",
    )(x, ids)


def lambda_kernel(x_ref, o_ref):
    first = jnp.sum(x_ref[0] * x_ref[1], -1, keepdims=True)
    second = jnp.sum(x_ref[2] * x_ref[3], -1, keepdims=True)
    o_ref[...] = jnp.broadcast_to(jnp.exp(first) - jnp.exp(second) + lambda_init, o_ref.shape)


def lambdas(x):
    vm = pl.BlockSpec(memory_space=pltpu.VMEM)
    return pl.pallas_call(
        lambda_kernel,
        out_shape=jax.ShapeDtypeStruct(x.shape[1:], f32),
        in_specs=[vm],
        out_specs=vm,
        cost_estimate=pl.CostEstimate(flops=10**11, bytes_accessed=4 * 10**4, transcendentals=0),
        name="lambdas",
    )(x)


def shift(x, axis, size, step):
    return lax.ppermute(x, axis, [(i, (i + step) % size) for i in range(size)])


def swap(x, axis, size, mask):
    return lax.ppermute(x, axis, [(i, i ^ mask) for i in range(size)])


def per_device(sizes, queries, keys, values, positions, lambda_vecs, head_gain, out_weight, residual):
    nz, nh, ny, nl, nc = sizes
    rows, width = queries.shape
    heads = lambda_vecs.shape[1]
    block = ((positions[::RUN].astype(f32) + 0.5) * (1.0 / RUN)).astype(jnp.int32).astype(bf16)
    ids = jnp.broadcast_to(jnp.pad(block, (0, width - block.shape[0]))[None, :], (16, width))
    kv_mine = jnp.concatenate([keys, values, ids], 0)
    kv_mine, queries = lax.optimization_barrier((kv_mine, queries))
    q_all = lax.all_to_all(repeat(queries, ids, nh * ny), ("h", "y"), 0, 0)
    up, down = shift(kv_mine, "z", nz, 1), shift(kv_mine, "z", nz, -1)
    kv_parts = [kv_mine, up, down]
    up, down, lam = lax.optimization_barrier((up, down, lambdas(lambda_vecs)))
    for _ in range(2):
        up, down = shift(up, "z", nz, 1), shift(down, "z", nz, -1)
        kv_parts += [up, down]
    kv_parts += [shift(up[:rows], "z", nz, 1), shift(down[rows:], "z", nz, -1)]
    spots = [(i, 0, i, rows) for i in range(nz - 1)] + [(nz - 1, 0, nz, 0)]
    o, lse = attend(q_all, kv_parts, spots, (3, 6, 9, 12, 16), rows, heads)

    pair = merge(lse, swap(lse, "h", nh, 1))
    others = [swap(pair, "y", ny, d) for d in range(1, ny)]

    parts = weigh(lam[:, 0], lse, [pair] + others, o, rows, heads)

    got = lax.all_to_all(parts, ("h", "y"), 0, 0, tiled=False)
    l, c = lax.axis_index("l"), lax.axis_index("c")
    cols = [jnp.stack([r * nc + 1 - c, r * nc + c]).astype(jnp.int32) for r in (1 - l, l)]
    send, keep, normed = project(cols[0], [got, head_gain.reshape(1, width)], out_weight, rows, heads)
    away = (keep + swap(send, "c", nc, 1).astype(f32)).astype(bf16)
    away, normed = lax.optimization_barrier((away, normed))
    far = swap(away, "l", nl, 1)
    send, keep = project(cols[1], [normed], out_weight, rows)
    rest = lax.optimization_barrier(far.astype(f32) + residual.astype(f32))
    return (rest + keep + swap(send, "c", nc, 1).astype(f32)).astype(bf16)


def solution(mesh):
    sizes = (8, 2, 4, 2, 2)
    fine = Mesh(mesh.devices.reshape(sizes), ("z", "h", "y", "l", "c"))
    ctx, tp = ("z", "h", "y"), ("l", "c")
    placed = (
        P(ctx, tp),
        P(ctx, tp),
        P(ctx, tp),
        P(ctx),
        P(None, tp, None),
        P(tp),
        P(tp, None),
        P(ctx, tp),
    )
    return jax.shard_map(
        lambda *a: per_device(sizes, *a), mesh=fine, in_specs=placed, out_specs=P(ctx, tp), check_vma=False
    )
```

```python
import math

import jax
import jax.numpy as jnp
from jax import lax
from jax.experimental import pallas as pl
from jax.experimental.pallas import tpu as pltpu
from jax.sharding import Mesh, PartitionSpec as P

lambda_init = 0.2
out_factor = 0.8
norm_eps = 1e-05

HD = 128
RUN = 72
TILE = 4
NEG = -1e30
FLOOR = -1e29
f32 = jnp.float32
bf16 = jnp.bfloat16


def attend_kernel(rows, spans, slots, spots, *refs):
    q_refs = [refs[0].at[i] for i in range(slots)]
    kv_refs, refs = refs[1:-10], refs[-10:]
    o_ref, lse_ref, q3, k3, v3, q_s, k_s, v_s, lse_s, order = refs
    head = pl.program_id(0)
    per = rows // RUN
    blocks = slots * per
    keys = len(spots) * per
    tile = TILE * RUN
    tiles = blocks // TILE
    scale = math.log2(math.e) / math.sqrt(HD)

    @pl.when(head == 0)
    def _():
        lse_s[...] = jnp.zeros_like(lse_s)
        first = lax.broadcasted_iota(jnp.int32, (16, HD), 0) == 0
        lanes = lax.broadcasted_iota(jnp.int32, (16, HD), 1)

        def numbers(part):
            tail = part[part.shape[0] - 16 :, :HD].astype(f32)
            weight = jnp.where(first & (lanes == 0), float(HD), jnp.where(first & (lanes == RUN), 1.0, 0.0))
            both = jnp.sum(tail * weight).astype(jnp.int32)
            return [lax.div(both, HD), lax.rem(both, HD)]

        kb = [v for k, kr, v, vr in spots for v in numbers(kv_refs[v])]
        qb = [v for p in q_refs for v in numbers(p)]
        for numbered, row in ((kb, 0), (qb, 2)):
            for i in range(len(numbered)):
                rank = jnp.int32(0)
                for j in range(len(numbered)):
                    rank = rank + (numbered[j] < numbered[i]).astype(jnp.int32)
                order[row, i] = rank
                if row == 0:
                    order[1, rank] = numbered[i]
                else:
                    order[3, rank] = i
                    order[4, rank] = numbered[i]
        for t in range(tiles):
            last = order[4, t * TILE + TILE - 1]
            need = jnp.int32(0)
            for j in range(keys):
                need = need + (kb[j] <= last).astype(jnp.int32)
            order[5, t] = need

    for i in range(keys):
        k, kr, v, vr = spots[i // per]
        d = i % per * RUN
        r = order[0, i]
        k3[r] = kv_refs[k][kr + d : kr + d + RUN, :]
        v3[r] = kv_refs[v][vr + d : vr + d + RUN, :]
    for i in range(blocks):
        d = i % per * RUN
        q3[order[2, i]] = q_refs[i // per][d : d + RUN, :]
    for i in range(keys):
        k_s[i * RUN : (i + 1) * RUN, :] = k3[i]
        v_s[i * RUN : (i + 1) * RUN, :] = v3[i]
    for i in range(blocks):
        q_s[i * RUN : (i + 1) * RUN, :] = q3[i]

    col = lax.broadcasted_iota(jnp.int32, (1, keys * RUN), 1)
    kpos = lax.rem(col, RUN)
    for i in range(keys):
        kpos = kpos + jnp.where(lax.div(col, RUN) == i, order[1, i] * RUN, 0)
    row = lax.broadcasted_iota(jnp.int32, (tile, 1), 0)
    lane = lax.broadcasted_iota(jnp.int32, (RUN, HD), 1)

    def one_tile(t, carry):
        need = order[5, t]
        start = pl.multiple_of(t * tile, tile)
        qpos = lax.rem(row, RUN)
        for i in range(TILE):
            qpos = qpos + jnp.where(lax.div(row, RUN) == i, order[4, t * TILE + i] * RUN, 0)

        def put(a, num, lse):
            for i in range(TILE):
                g = order[3, t * TILE + i]
                o = num[i * RUN : (i + 1) * RUN]
                e = lse[i * RUN : (i + 1) * RUN]
                o_ref[g, :, a * 2 * HD : (a + 1) * 2 * HD] = o.astype(bf16)
                lse_s[g] = jnp.where(lane == head * 2 + a, e, lse_s[g])

        for low, high in zip((0,) + spans[:-1], spans):

            @pl.when((need > low) & (need <= high))
            def _(span=high * RUN):
                allowed = kpos[:, :span] <= qpos
                ss = [
                    lax.dot_general(
                        q_s[pl.ds(start, tile), a * HD : (a + 1) * HD],
                        k_s[:span, a * HD : (a + 1) * HD],
                        (((1,), (1,)), ((), ())),
                        preferred_element_type=f32,
                    )
                    for a in range(2)
                ]
                ps = []
                for a in range(2):
                    s = jnp.where(allowed, ss[a], NEG)
                    m = jnp.maximum(jnp.max(s, -1, keepdims=True), FLOOR) * scale
                    p = jnp.exp2(s * scale - m)
                    ps.append((p.astype(bf16), m, jnp.sum(p, -1, keepdims=True)))
                for a in range(2):
                    p, m, total = ps[a]
                    num = jnp.dot(p, v_s[:span, :], preferred_element_type=f32)
                    some = total > 0.0
                    safe = jnp.where(some, total, 1.0)
                    put(a, num * (1.0 / safe), jnp.where(some, m + jnp.log2(safe), NEG))

        @pl.when(need == 0)
        def _():
            for a in range(2):
                put(a, jnp.zeros((tile, 2 * HD), f32), jnp.full((tile, 1), NEG, f32))

        return carry

    lax.fori_loop(0, tiles, one_tile, 0)

    @pl.when(head == pl.num_programs(0) - 1)
    def _():
        lse_ref[...] = jnp.transpose(lse_s[...].reshape(blocks * RUN, HD))[: lse_ref.shape[0], :]


def attend(q_all, kv_parts, spots, spans, rows, heads):
    slots, pad, width = q_all.shape
    blocks = slots * rows // RUN
    keys = len(spots) * rows // RUN
    ins = [pltpu.with_memory_space_constraint(x, pltpu.HBM) for x in kv_parts[:-2]]
    return pl.pallas_call(
        lambda *r: attend_kernel(rows, spans, slots, spots, *r),
        out_shape=[
            jax.ShapeDtypeStruct((blocks, RUN, heads * 4 * HD), bf16),
            jax.ShapeDtypeStruct((8, blocks * RUN), f32),
        ],
        grid_spec=pltpu.PrefetchScalarGridSpec(
            num_scalar_prefetch=0,
            grid=(heads,),
            in_specs=[pl.BlockSpec((slots, pad, 2 * HD), lambda h: (0, 0, h))]
            + [pl.BlockSpec((x.shape[0], 2 * HD), lambda h: (0, h)) for x in kv_parts],
            out_specs=[
                pl.BlockSpec((blocks, RUN, 4 * HD), lambda h: (0, 0, h)),
                pl.BlockSpec((8, blocks * RUN), lambda h: (0, 0)),
            ],
            scratch_shapes=[
                pltpu.VMEM((blocks, RUN, 2 * HD), bf16),
                pltpu.VMEM((keys, RUN, 2 * HD), bf16),
                pltpu.VMEM((keys, RUN, 2 * HD), bf16),
                pltpu.VMEM((blocks * RUN, 2 * HD), bf16),
                pltpu.VMEM((keys * RUN, 2 * HD), bf16),
                pltpu.VMEM((keys * RUN, 2 * HD), bf16),
                pltpu.VMEM((blocks, RUN, HD), f32),
                pltpu.SMEM((6, 128), jnp.int32),
            ],
        ),
        compiler_params=pltpu.CompilerParams(vmem_limit_bytes=36 << 20),
        cost_estimate=pl.CostEstimate(
            flops=heads * 2 * blocks * keys * RUN * RUN * 6 * HD * 8,
            bytes_accessed=(slots * 2 + len(spots) * 2) * rows * heads * 4 * HD,
            transcendentals=heads * 2 * blocks * keys * RUN * RUN,
        ),
        name="attend",
    )(q_all, *ins, *kv_parts[-2:])


def logsum(parts):
    top = parts[0]
    for p in parts[1:]:
        top = jnp.maximum(top, p)
    total = jnp.exp2(parts[0] - top)
    for p in parts[1:]:
        total = total + jnp.exp2(p - top)
    return top + jnp.log2(total)


def merge_kernel(a_ref, b_ref, o_ref):
    o_ref[...] = logsum([a_ref[...], b_ref[...]])


def merge(a, b):
    vm = pl.BlockSpec(memory_space=pltpu.VMEM)
    return pl.pallas_call(
        merge_kernel,
        out_shape=jax.ShapeDtypeStruct(a.shape, a.dtype),
        in_specs=[vm, vm],
        out_specs=vm,
        compiler_params=pltpu.CompilerParams(vmem_limit_bytes=4 << 20),
        name="merge",
    )(a, b)


def weigh_kernel(heads, lam, lse_ref, *refs):
    all_refs, o_ref, out_ref, w_s = refs[:-3], refs[-3], refs[-2], refs[-1]
    j = pl.program_id(0)
    slots, rows = out_ref.shape[:2]

    @pl.when(j == 0)
    def _():
        whole = logsum([r[...] for r in all_refs])
        w = jnp.exp2(lse_ref[...] - whole)
        w = jnp.concatenate([w, jnp.zeros((HD - w.shape[0], w.shape[1]), f32)], 0)
        w_s[...] = jnp.transpose(w)

    for d in range(slots):
        w = w_s[pl.ds(pl.multiple_of((slots * j + d) * rows, rows), rows), :]
        o = o_ref[d * (rows // RUN) : (d + 1) * (rows // RUN)]
        for h in range(heads):
            w1 = w[:, 2 * h : 2 * h + 1]
            w2 = w[:, 2 * h + 1 : 2 * h + 2] * lam[h]
            o1 = o[:, :, h * 4 * HD : h * 4 * HD + 2 * HD].reshape(rows, 2 * HD).astype(f32)
            o2 = o[:, :, h * 4 * HD + 2 * HD : (h + 1) * 4 * HD].reshape(rows, 2 * HD).astype(f32)
            out_ref[d, :, h * 2 * HD : (h + 1) * 2 * HD] = (w1 * o1 - w2 * o2).astype(bf16)


def weigh(lam, lse, lses, o, rows, heads):
    slots = lse.shape[1] // rows
    return pl.pallas_call(
        lambda *r: weigh_kernel(heads, *r),
        out_shape=jax.ShapeDtypeStruct((slots, rows, heads * 2 * HD), bf16),
        grid_spec=pltpu.PrefetchScalarGridSpec(
            num_scalar_prefetch=1,
            grid=(slots // 2,),
            in_specs=[pl.BlockSpec(lse.shape, lambda j, lam: (0, 0))] * (1 + len(lses))
            + [pl.BlockSpec((2 * rows // RUN, RUN, heads * 4 * HD), lambda j, lam: (j, 0, 0))],
            out_specs=pl.BlockSpec((2, rows, heads * 2 * HD), lambda j, lam: (j, 0, 0)),
            scratch_shapes=[pltpu.VMEM((slots * rows, HD), f32)],
        ),
        compiler_params=pltpu.CompilerParams(vmem_limit_bytes=20 << 20),
        name="weigh",
    )(lam, lse, *lses, o)


def norm(got_ref, gain_ref, n_s, heads):
    total = got_ref[0].astype(f32)
    for j in range(1, got_ref.shape[0]):
        total = total + got_ref[j].astype(f32)
    for h in range(heads):
        d = total[:, h * 2 * HD : (h + 1) * 2 * HD]
        mean_square = jnp.mean(d * d, -1, keepdims=True)
        g = gain_ref[0:1, h * 2 * HD : (h + 1) * 2 * HD]
        n_s[:, h * 2 * HD : (h + 1) * 2 * HD] = (out_factor * d / jnp.sqrt(mean_square + norm_eps) * g).astype(bf16)


def project_kernel(heads, cols, *refs):
    i = pl.program_id(0)
    if heads:
        got_ref, gain_ref, w_ref, send_ref, keep_ref, n_ref = refs

        @pl.when(i == 0)
        def _():
            norm(got_ref, gain_ref, n_ref, heads)

    else:
        n_ref, w_ref, send_ref, keep_ref = refs
    share = jnp.dot(n_ref[...], w_ref[...], preferred_element_type=f32)

    @pl.when(i == 0)
    def _():
        send_ref[...] = share.astype(bf16)

    @pl.when(i == 1)
    def _():
        keep_ref[...] = share


def project(cols, ins, weight, rows, heads=0):
    depth = weight.shape[0]
    width = weight.shape[1] // 4
    zeros = lambda x: pl.BlockSpec(x.shape, lambda i, cols: (0,) * len(x.shape))
    outs = [
        jax.ShapeDtypeStruct((rows, width), bf16),
        jax.ShapeDtypeStruct((rows, width), f32),
    ] + [jax.ShapeDtypeStruct((rows, depth), bf16)] * bool(heads)
    return pl.pallas_call(
        lambda *r: project_kernel(heads, *r),
        out_shape=outs,
        grid_spec=pltpu.PrefetchScalarGridSpec(
            num_scalar_prefetch=1,
            grid=(2,),
            in_specs=[zeros(x) for x in ins] + [pl.BlockSpec((depth, width), lambda i, cols: (0, cols[i]))],
            out_specs=[zeros(x) for x in outs],
        ),
        compiler_params=pltpu.CompilerParams(vmem_limit_bytes=24 << 20),
        cost_estimate=pl.CostEstimate(flops=rows * depth * width * 32, bytes_accessed=depth * width * 4, transcendentals=0),
        name="project",
    )(cols, *ins, pltpu.with_memory_space_constraint(weight, pltpu.HBM))


def repeat_kernel(x_ref, ids_ref, o_ref, one, sems):
    rows = x_ref.shape[0]
    one[:rows] = x_ref[...]
    one[rows:] = ids_ref[...]
    copies = [pltpu.make_async_copy(one, o_ref.at[i], sems.at[i]) for i in range(o_ref.shape[0])]
    for c in copies:
        c.start()
    for c in copies:
        c.wait()


def repeat(x, ids, count):
    rows, width = x.shape
    shape = (rows + ids.shape[0], width)
    vm = pl.BlockSpec(memory_space=pltpu.VMEM)
    return pl.pallas_call(
        repeat_kernel,
        out_shape=jax.ShapeDtypeStruct((count, *shape), x.dtype),
        in_specs=[vm, vm],
        out_specs=pl.BlockSpec(memory_space=pl.ANY),
        scratch_shapes=[pltpu.VMEM(shape, x.dtype), pltpu.SemaphoreType.DMA((count,))],
        compiler_params=pltpu.CompilerParams(vmem_limit_bytes=2 << 20),
        name="repeat",
    )(x, ids)


def lambda_kernel(x_ref, o_ref):
    first = jnp.sum(x_ref[:, 0] * x_ref[:, 1], -1, keepdims=True)
    second = jnp.sum(x_ref[:, 2] * x_ref[:, 3], -1, keepdims=True)
    o_ref[...] = jnp.broadcast_to(jnp.exp(first) - jnp.exp(second) + lambda_init, o_ref.shape)


def lambdas(x):
    vm = pl.BlockSpec(memory_space=pltpu.VMEM)
    return pl.pallas_call(
        lambda_kernel,
        out_shape=jax.ShapeDtypeStruct((x.shape[0], x.shape[2]), f32),
        in_specs=[vm],
        out_specs=vm,
        cost_estimate=pl.CostEstimate(flops=10**11, bytes_accessed=4 * 10**4, transcendentals=0),
        name="lambdas",
    )(x)


def shift(x, axis, size, step):
    return lax.ppermute(x, axis, [(i, (i + step) % size) for i in range(size)])


def swap(x, axis, size, mask):
    return lax.ppermute(x, axis, [(i, i ^ mask) for i in range(size)])


def per_device(sizes, queries, keys, values, positions, lambda_vecs, head_gain, out_weight, residual):
    nz, nh, ny, nl, nc = sizes
    rows, width = queries.shape
    heads = lambda_vecs.shape[1]
    block = ((positions.astype(f32) + 0.5) * (1.0 / RUN)).astype(jnp.int32).astype(bf16)
    ids = jnp.broadcast_to(jnp.pad(block, (0, width - block.shape[0]))[None, :], (16, width))
    kv_mine = jnp.concatenate([keys, values, ids], 0)
    kv_mine, queries = lax.optimization_barrier((kv_mine, queries))
    q_all = lax.all_to_all(repeat(queries, ids, nh * ny), ("h", "y"), 0, 0)
    up, down = shift(kv_mine, "z", nz, 1), shift(kv_mine, "z", nz, -1)
    kv_parts = [kv_mine, up, down]
    up, down, lam = lax.optimization_barrier((up, down, lambdas(jnp.transpose(lambda_vecs, (1, 0, 2)))))
    for _ in range(2):
        up, down = shift(up, "z", nz, 1), shift(down, "z", nz, -1)
        kv_parts += [up, down]
    kv_parts += [shift(up[:rows], "z", nz, 1), shift(down[rows:], "z", nz, -1)]
    spots = [(i, 0, i, rows) for i in range(nz - 1)] + [(nz - 1, 0, nz, 0)]
    o, lse = attend(q_all, kv_parts, spots, (3, 6, 9, 12, 16), rows, heads)

    pair = merge(lse, swap(lse, "h", nh, 1))
    others = [swap(pair, "y", ny, d) for d in range(1, ny)]

    parts = weigh(lam[:, 0], lse, [pair] + others, o, rows, heads)

    got = lax.all_to_all(parts, ("h", "y"), 0, 0, tiled=False)
    l, c = lax.axis_index("l"), lax.axis_index("c")
    cols = [jnp.stack([r * nc + 1 - c, r * nc + c]).astype(jnp.int32) for r in (1 - l, l)]
    send, keep, normed = project(cols[0], [got, head_gain.reshape(1, width)], out_weight, rows, heads)
    away = (keep + swap(send, "c", nc, 1).astype(f32)).astype(bf16)
    away, normed = lax.optimization_barrier((away, normed))
    far = swap(away, "l", nl, 1)
    send, keep = project(cols[1], [normed], out_weight, rows)
    rest = lax.optimization_barrier(far.astype(f32) + residual.astype(f32))
    return (rest + keep + swap(send, "c", nc, 1).astype(f32)).astype(bf16)


def solution(mesh):
    sizes = (8, 2, 4, 2, 2)
    fine = Mesh(mesh.devices.reshape(sizes), ("z", "h", "y", "l", "c"))
    ctx, tp = ("z", "h", "y"), ("l", "c")
    placed = (
        P(ctx, tp),
        P(ctx, tp),
        P(ctx, tp),
        P(ctx),
        P(None, tp, None),
        P(tp),
        P(tp, None),
        P(ctx, tp),
    )
    return jax.shard_map(
        lambda *a: per_device(sizes, *a), mesh=fine, in_specs=placed, out_specs=P(ctx, tp), check_vma=False
    )
```

```python
import math

import jax
import jax.numpy as jnp
from jax import lax
from jax.experimental import pallas as pl
from jax.experimental.pallas import tpu as pltpu
from jax.sharding import Mesh, PartitionSpec as P

lambda_init = 0.2
out_factor = 0.8
norm_eps = 1e-05

HD = 128
RUN = 72
TILE = 8
NEG = -1e30
FLOOR = -1e29
f32 = jnp.float32
bf16 = jnp.bfloat16


def attend_kernel(rows, spans, slots, spots, *refs):
    q_refs = [refs[0].at[i] for i in range(slots)]
    kv_refs, refs = refs[1:-10], refs[-10:]
    o_ref, lse_ref, q3, k3, v3, q_s, k_s, v_s, lse_s, order = refs
    head = pl.program_id(0)
    per = rows // RUN
    blocks = slots * per
    keys = len(spots) * per
    tile = TILE * RUN
    tiles = blocks // TILE
    scale = math.log2(math.e) / math.sqrt(HD)

    @pl.when(head == 0)
    def _():
        lse_s[...] = jnp.zeros_like(lse_s)
        first = lax.broadcasted_iota(jnp.int32, (16, HD), 0) == 0
        lanes = lax.broadcasted_iota(jnp.int32, (16, HD), 1)

        def numbers(part):
            tail = part[part.shape[0] - 16 :, :HD].astype(f32)
            weight = jnp.where(first & (lanes == 0), float(HD), jnp.where(first & (lanes == RUN), 1.0, 0.0))
            both = jnp.sum(tail * weight).astype(jnp.int32)
            return [lax.div(both, HD), lax.rem(both, HD)]

        kb = [v for k, kr, v, vr in spots for v in numbers(kv_refs[v])]
        qb = [v for p in q_refs for v in numbers(p)]
        for numbered, row in ((kb, 0), (qb, 2)):
            for i in range(len(numbered)):
                rank = jnp.int32(0)
                for j in range(len(numbered)):
                    rank = rank + (numbered[j] < numbered[i]).astype(jnp.int32)
                order[row, i] = rank
                if row == 0:
                    order[1, rank] = numbered[i]
                else:
                    order[3, rank] = i
                    order[4, rank] = numbered[i]
        for t in range(tiles):
            last = order[4, t * TILE + TILE - 1]
            need = jnp.int32(0)
            for j in range(keys):
                need = need + (kb[j] <= last).astype(jnp.int32)
            order[5, t] = need

    for i in range(keys):
        k, kr, v, vr = spots[i // per]
        d = i % per * RUN
        r = order[0, i]
        k3[r] = kv_refs[k][kr + d : kr + d + RUN, :]
        v3[r] = kv_refs[v][vr + d : vr + d + RUN, :]
    for i in range(blocks):
        d = i % per * RUN
        q3[order[2, i]] = q_refs[i // per][d : d + RUN, :]
    for i in range(keys):
        k_s[i * RUN : (i + 1) * RUN, :] = k3[i]
        v_s[i * RUN : (i + 1) * RUN, :] = v3[i]
    for i in range(blocks):
        q_s[i * RUN : (i + 1) * RUN, :] = q3[i]

    col = lax.broadcasted_iota(jnp.int32, (1, keys * RUN), 1)
    kpos = lax.rem(col, RUN)
    for i in range(keys):
        kpos = kpos + jnp.where(lax.div(col, RUN) == i, order[1, i] * RUN, 0)
    row = lax.broadcasted_iota(jnp.int32, (tile, 1), 0)
    lane = lax.broadcasted_iota(jnp.int32, (RUN, HD), 1)

    def one_tile(t, carry):
        need = order[5, t]
        start = pl.multiple_of(t * tile, tile)
        qpos = lax.rem(row, RUN)
        for i in range(TILE):
            qpos = qpos + jnp.where(lax.div(row, RUN) == i, order[4, t * TILE + i] * RUN, 0)

        def put(a, num, lse):
            for i in range(TILE):
                g = order[3, t * TILE + i]
                o = num[i * RUN : (i + 1) * RUN]
                e = lse[i * RUN : (i + 1) * RUN]
                o_ref[g, :, a * 2 * HD : (a + 1) * 2 * HD] = o.astype(bf16)
                lse_s[g] = jnp.where(lane == head * 2 + a, e, lse_s[g])

        clear = order[4, t * TILE] > order[1, keys - 1]
        cases = [(low, high, False) for low, high in zip((0,) + spans[:-1], spans)] + [(spans[-2], spans[-1], True)]
        for low, high, whole in cases:
            here = (need > low) & (need <= high)
            if high == spans[-1]:
                here = here & (clear if whole else jnp.logical_not(clear))

            @pl.when(here)
            def _(span=high * RUN, whole=whole):
                ss = [
                    lax.dot_general(
                        q_s[pl.ds(start, tile), a * HD : (a + 1) * HD],
                        k_s[:span, a * HD : (a + 1) * HD],
                        (((1,), (1,)), ((), ())),
                        preferred_element_type=f32,
                    )
                    for a in range(2)
                ]
                ps = []
                for a in range(2):
                    s = ss[a] if whole else jnp.where(kpos[:, :span] <= qpos, ss[a], NEG)
                    m = jnp.maximum(jnp.max(s, -1, keepdims=True), FLOOR) * scale
                    p = jnp.exp2(s * scale - m)
                    ps.append((p.astype(bf16), m, jnp.sum(p, -1, keepdims=True)))
                for a in range(2):
                    p, m, total = ps[a]
                    num = jnp.dot(p, v_s[:span, :], preferred_element_type=f32)
                    some = total > 0.0
                    safe = jnp.where(some, total, 1.0)
                    put(a, num * (1.0 / safe), jnp.where(some, m + jnp.log2(safe), NEG))

        @pl.when(need == 0)
        def _():
            for a in range(2):
                put(a, jnp.zeros((tile, 2 * HD), f32), jnp.full((tile, 1), NEG, f32))

        return carry

    lax.fori_loop(0, tiles, one_tile, 0)

    @pl.when(head == pl.num_programs(0) - 1)
    def _():
        lse_ref[...] = jnp.transpose(lse_s[...].reshape(blocks * RUN, HD))[: lse_ref.shape[0], :]


def attend(q_all, kv_parts, spots, spans, rows, heads):
    slots, pad, width = q_all.shape
    blocks = slots * rows // RUN
    keys = len(spots) * rows // RUN
    ins = [pltpu.with_memory_space_constraint(x, pltpu.HBM) for x in kv_parts[:-2]]
    return pl.pallas_call(
        lambda *r: attend_kernel(rows, spans, slots, spots, *r),
        out_shape=[
            jax.ShapeDtypeStruct((blocks, RUN, heads * 4 * HD), bf16),
            jax.ShapeDtypeStruct((8, blocks * RUN), f32),
        ],
        grid_spec=pltpu.PrefetchScalarGridSpec(
            num_scalar_prefetch=0,
            grid=(heads,),
            in_specs=[pl.BlockSpec((slots, pad, 2 * HD), lambda h: (0, 0, h))]
            + [pl.BlockSpec((x.shape[0], 2 * HD), lambda h: (0, h)) for x in kv_parts],
            out_specs=[
                pl.BlockSpec((blocks, RUN, 4 * HD), lambda h: (0, 0, h)),
                pl.BlockSpec((8, blocks * RUN), lambda h: (0, 0)),
            ],
            scratch_shapes=[
                pltpu.VMEM((blocks, RUN, 2 * HD), bf16),
                pltpu.VMEM((keys, RUN, 2 * HD), bf16),
                pltpu.VMEM((keys, RUN, 2 * HD), bf16),
                pltpu.VMEM((blocks * RUN, 2 * HD), bf16),
                pltpu.VMEM((keys * RUN, 2 * HD), bf16),
                pltpu.VMEM((keys * RUN, 2 * HD), bf16),
                pltpu.VMEM((blocks, RUN, HD), f32),
                pltpu.SMEM((6, 128), jnp.int32),
            ],
        ),
        compiler_params=pltpu.CompilerParams(vmem_limit_bytes=36 << 20),
        cost_estimate=pl.CostEstimate(
            flops=heads * 2 * blocks * keys * RUN * RUN * 6 * HD * 8,
            bytes_accessed=(slots * 2 + len(spots) * 2) * rows * heads * 4 * HD,
            transcendentals=heads * 2 * blocks * keys * RUN * RUN,
        ),
        name="attend",
    )(q_all, *ins, *kv_parts[-2:])


def logsum(parts):
    top = parts[0]
    for p in parts[1:]:
        top = jnp.maximum(top, p)
    total = jnp.exp2(parts[0] - top)
    for p in parts[1:]:
        total = total + jnp.exp2(p - top)
    return top + jnp.log2(total)


def merge_kernel(a_ref, b_ref, o_ref):
    o_ref[...] = logsum([a_ref[...], b_ref[...]])


def merge(a, b):
    vm = pl.BlockSpec(memory_space=pltpu.VMEM)
    return pl.pallas_call(
        merge_kernel,
        out_shape=jax.ShapeDtypeStruct(a.shape, a.dtype),
        in_specs=[vm, vm],
        out_specs=vm,
        compiler_params=pltpu.CompilerParams(vmem_limit_bytes=4 << 20),
        name="merge",
    )(a, b)


def weigh_kernel(heads, lam, lse_ref, *refs):
    all_refs, o_ref, out_ref, w_s = refs[:-3], refs[-3], refs[-2], refs[-1]
    j = pl.program_id(0)
    slots, rows = out_ref.shape[:2]

    @pl.when(j == 0)
    def _():
        whole = logsum([r[...] for r in all_refs])
        w = jnp.exp2(lse_ref[...] - whole)
        w = jnp.concatenate([w, jnp.zeros((HD - w.shape[0], w.shape[1]), f32)], 0)
        w_s[...] = jnp.transpose(w)

    for d in range(slots):
        w = w_s[pl.ds(pl.multiple_of((slots * j + d) * rows, rows), rows), :]
        o = o_ref[d * (rows // RUN) : (d + 1) * (rows // RUN)]
        for h in range(heads):
            w1 = w[:, 2 * h : 2 * h + 1]
            w2 = w[:, 2 * h + 1 : 2 * h + 2] * lam[h]
            o1 = o[:, :, h * 4 * HD : h * 4 * HD + 2 * HD].reshape(rows, 2 * HD).astype(f32)
            o2 = o[:, :, h * 4 * HD + 2 * HD : (h + 1) * 4 * HD].reshape(rows, 2 * HD).astype(f32)
            out_ref[d, :, h * 2 * HD : (h + 1) * 2 * HD] = (w1 * o1 - w2 * o2).astype(bf16)


def weigh(lam, lse, lses, o, rows, heads):
    slots = lse.shape[1] // rows
    return pl.pallas_call(
        lambda *r: weigh_kernel(heads, *r),
        out_shape=jax.ShapeDtypeStruct((slots, rows, heads * 2 * HD), bf16),
        grid_spec=pltpu.PrefetchScalarGridSpec(
            num_scalar_prefetch=1,
            grid=(slots // 2,),
            in_specs=[pl.BlockSpec(lse.shape, lambda j, lam: (0, 0))] * (1 + len(lses))
            + [pl.BlockSpec((2 * rows // RUN, RUN, heads * 4 * HD), lambda j, lam: (j, 0, 0))],
            out_specs=pl.BlockSpec((2, rows, heads * 2 * HD), lambda j, lam: (j, 0, 0)),
            scratch_shapes=[pltpu.VMEM((slots * rows, HD), f32)],
        ),
        compiler_params=pltpu.CompilerParams(vmem_limit_bytes=20 << 20),
        name="weigh",
    )(lam, lse, *lses, o)


def norm(got_ref, gain_ref, n_s, heads):
    total = got_ref[0].astype(f32)
    for j in range(1, got_ref.shape[0]):
        total = total + got_ref[j].astype(f32)
    for h in range(heads):
        d = total[:, h * 2 * HD : (h + 1) * 2 * HD]
        mean_square = jnp.mean(d * d, -1, keepdims=True)
        g = gain_ref[0:1, h * 2 * HD : (h + 1) * 2 * HD]
        n_s[:, h * 2 * HD : (h + 1) * 2 * HD] = (out_factor * d / jnp.sqrt(mean_square + norm_eps) * g).astype(bf16)


def project_kernel(heads, kinds, cols, *refs):
    i = pl.program_id(0)
    if heads:
        got_ref, gain_ref, w_ref, *outs, n_ref = refs

        @pl.when(i == 0)
        def _():
            norm(got_ref, gain_ref, n_ref, heads)

    else:
        n_ref, w_ref, *outs = refs
    share = jnp.dot(n_ref[...], w_ref[...], preferred_element_type=f32)
    for j, kind in enumerate(kinds):

        @pl.when(i == j)
        def _(j=j, kind=kind):
            outs[j][...] = share.astype(kind)


def project(cols, ins, weight, rows, kinds, heads=0):
    depth = weight.shape[0]
    width = weight.shape[1] // 4
    whole = lambda x: pl.BlockSpec(x.shape, lambda i, cols: (0,) * len(x.shape))
    outs = [jax.ShapeDtypeStruct((rows, width), kind) for kind in kinds]
    outs += [jax.ShapeDtypeStruct((rows, depth), bf16)] * bool(heads)
    return pl.pallas_call(
        lambda *r: project_kernel(heads, kinds, *r),
        out_shape=outs,
        grid_spec=pltpu.PrefetchScalarGridSpec(
            num_scalar_prefetch=1,
            grid=(len(kinds),),
            in_specs=[whole(x) for x in ins] + [pl.BlockSpec((depth, width), lambda i, cols: (0, cols[i]))],
            out_specs=[whole(x) for x in outs],
        ),
        compiler_params=pltpu.CompilerParams(vmem_limit_bytes=24 << 20),
        cost_estimate=pl.CostEstimate(
            flops=rows * depth * width * 16 * len(kinds), bytes_accessed=depth * width * 2 * len(kinds), transcendentals=0
        ),
        name="project",
    )(cols, *ins, pltpu.with_memory_space_constraint(weight, pltpu.HBM))


def repeat_kernel(x_ref, ids_ref, o_ref, one, sems):
    rows = x_ref.shape[0]
    one[:rows] = x_ref[...]
    one[rows:] = ids_ref[...]
    copies = [pltpu.make_async_copy(one, o_ref.at[i], sems.at[i]) for i in range(o_ref.shape[0])]
    for c in copies:
        c.start()
    for c in copies:
        c.wait()


def repeat(x, ids, count):
    rows, width = x.shape
    shape = (rows + ids.shape[0], width)
    vm = pl.BlockSpec(memory_space=pltpu.VMEM)
    return pl.pallas_call(
        repeat_kernel,
        out_shape=jax.ShapeDtypeStruct((count, *shape), x.dtype),
        in_specs=[vm, vm],
        out_specs=pl.BlockSpec(memory_space=pl.ANY),
        scratch_shapes=[pltpu.VMEM(shape, x.dtype), pltpu.SemaphoreType.DMA((count,))],
        compiler_params=pltpu.CompilerParams(vmem_limit_bytes=2 << 20),
        name="repeat",
    )(x, ids)


def lambda_kernel(x_ref, o_ref):
    first = jnp.sum(x_ref[:, 0] * x_ref[:, 1], -1, keepdims=True)
    second = jnp.sum(x_ref[:, 2] * x_ref[:, 3], -1, keepdims=True)
    o_ref[...] = jnp.broadcast_to(jnp.exp(first) - jnp.exp(second) + lambda_init, o_ref.shape)


def lambdas(x):
    vm = pl.BlockSpec(memory_space=pltpu.VMEM)
    return pl.pallas_call(
        lambda_kernel,
        out_shape=jax.ShapeDtypeStruct((x.shape[0], x.shape[2]), f32),
        in_specs=[vm],
        out_specs=vm,
        cost_estimate=pl.CostEstimate(flops=10**11, bytes_accessed=4 * 10**4, transcendentals=0),
        name="lambdas",
    )(x)


def shift(x, axis, size, step):
    return lax.ppermute(x, axis, [(i, (i + step) % size) for i in range(size)])


def swap(x, axis, size, mask):
    return lax.ppermute(x, axis, [(i, i ^ mask) for i in range(size)])


def per_device(sizes, queries, keys, values, positions, lambda_vecs, head_gain, out_weight, residual):
    nz, nh, ny, nl, nc = sizes
    rows, width = queries.shape
    heads = lambda_vecs.shape[1]
    block = ((positions.astype(f32) + 0.5) * (1.0 / RUN)).astype(jnp.int32).astype(bf16)
    ids = jnp.broadcast_to(jnp.pad(block, (0, width - block.shape[0]))[None, :], (16, width))
    kv_mine = jnp.concatenate([keys, values, ids], 0)
    kv_mine, queries = lax.optimization_barrier((kv_mine, queries))
    q_all = lax.all_to_all(repeat(queries, ids, nh * ny), ("h", "y"), 0, 0)
    up, down = shift(kv_mine, "z", nz, 1), shift(kv_mine, "z", nz, -1)
    kv_parts = [kv_mine, up, down]
    up, down, lam = lax.optimization_barrier((up, down, lambdas(jnp.transpose(lambda_vecs, (1, 0, 2)))))
    for _ in range(2):
        up, down = shift(up, "z", nz, 1), shift(down, "z", nz, -1)
        kv_parts += [up, down]
    kv_parts += [shift(up[:rows], "z", nz, 1), shift(down[rows:], "z", nz, -1)]
    spots = [(i, 0, i, rows) for i in range(nz - 1)] + [(nz - 1, 0, nz, 0)]
    o, lse = attend(q_all, kv_parts, spots, (4, 8, 12, 16), rows, heads)

    pair = merge(lse, swap(lse, "h", nh, 1))
    others = [swap(pair, "y", ny, d) for d in range(1, ny)]

    parts = weigh(lam[:, 0], lse, [pair] + others, o, rows, heads)

    got = lax.all_to_all(parts, ("h", "y"), 0, 0, tiled=False)
    l, c = lax.axis_index("l"), lax.axis_index("c")
    cols = [(r * nc + d).astype(jnp.int32).reshape(1) for r in (1 - l, l) for d in (1 - c, c)]
    send, normed = project(cols[0], [got, head_gain.reshape(1, width)], out_weight, rows, [bf16], heads)
    (keep,) = project(cols[1], [normed], out_weight, rows, [f32])
    away = (keep + swap(send, "c", nc, 1).astype(f32)).astype(bf16)
    away, normed = lax.optimization_barrier((away, normed))
    far = swap(away, "l", nl, 1)
    send, keep = project(jnp.concatenate(cols[2:]), [normed], out_weight, rows, [bf16, f32])
    rest = lax.optimization_barrier(far.astype(f32) + residual.astype(f32))
    return (rest + keep + swap(send, "c", nc, 1).astype(f32)).astype(bf16)


def solution(mesh):
    sizes = (8, 2, 4, 2, 2)
    fine = Mesh(mesh.devices.reshape(sizes), ("z", "h", "y", "l", "c"))
    ctx, tp = ("z", "h", "y"), ("l", "c")
    placed = (
        P(ctx, tp),
        P(ctx, tp),
        P(ctx, tp),
        P(ctx),
        P(None, tp, None),
        P(tp),
        P(tp, None),
        P(ctx, tp),
    )
    return jax.shard_map(
        lambda *a: per_device(sizes, *a), mesh=fine, in_specs=placed, out_specs=P(ctx, tp), check_vma=False
    )
```

```python
import math

import jax
import jax.numpy as jnp
from jax import lax
from jax.experimental import pallas as pl
from jax.experimental.pallas import tpu as pltpu
from jax.sharding import Mesh, PartitionSpec as P

lambda_init = 0.2
out_factor = 0.8
norm_eps = 1e-05

HD = 128
RUN = 72
TILE = 4
NEG = -1e30
FLOOR = -1e29
f32 = jnp.float32
bf16 = jnp.bfloat16


def attend_kernel(rows, spans, slots, spots, *refs):
    q_refs = [refs[0].at[i] for i in range(slots)]
    kv_refs, refs = refs[1:-10], refs[-10:]
    o_ref, lse_ref, q3, k3, v3, q_s, k_s, v_s, lse_s, order = refs
    head = pl.program_id(0)
    per = rows // RUN
    blocks = slots * per
    keys = len(spots) * per
    tile = TILE * RUN
    tiles = blocks // TILE
    scale = math.log2(math.e) / math.sqrt(HD)

    @pl.when(head == 0)
    def _():
        lse_s[...] = jnp.zeros_like(lse_s)
        first = lax.broadcasted_iota(jnp.int32, (16, HD), 0) == 0
        lanes = lax.broadcasted_iota(jnp.int32, (16, HD), 1)

        def numbers(part):
            tail = part[part.shape[0] - 16 :, :HD].astype(f32)
            weight = jnp.where(first & (lanes == 0), float(HD), jnp.where(first & (lanes == RUN), 1.0, 0.0))
            both = jnp.sum(tail * weight).astype(jnp.int32)
            return [lax.div(both, HD), lax.rem(both, HD)]

        kb = [v for k, kr, v, vr in spots for v in numbers(kv_refs[v])]
        qb = [v for p in q_refs for v in numbers(p)]
        for numbered, row in ((kb, 0), (qb, 2)):
            for i in range(len(numbered)):
                rank = jnp.int32(0)
                for j in range(len(numbered)):
                    rank = rank + (numbered[j] < numbered[i]).astype(jnp.int32)
                order[row, i] = rank
                if row == 0:
                    order[1, rank] = numbered[i]
                else:
                    order[3, rank] = i
                    order[4, rank] = numbered[i]
        for t in range(tiles):
            last = order[4, t * TILE + TILE - 1]
            need = jnp.int32(0)
            for j in range(keys):
                need = need + (kb[j] <= last).astype(jnp.int32)
            order[5, t] = need

    for i in range(keys):
        k, kr, v, vr = spots[i // per]
        d = i % per * RUN
        r = order[0, i]
        k3[r] = kv_refs[k][kr + d : kr + d + RUN, :]
        v3[r] = kv_refs[v][vr + d : vr + d + RUN, :]
    for i in range(blocks):
        d = i % per * RUN
        q3[order[2, i]] = q_refs[i // per][d : d + RUN, :]
    for i in range(keys):
        k_s[i * RUN : (i + 1) * RUN, :] = k3[i]
        v_s[i * RUN : (i + 1) * RUN, :] = v3[i]
    for i in range(blocks):
        q_s[i * RUN : (i + 1) * RUN, :] = q3[i]

    col = lax.broadcasted_iota(jnp.int32, (1, keys * RUN), 1)
    kpos = lax.rem(col, RUN)
    for i in range(keys):
        kpos = kpos + jnp.where(lax.div(col, RUN) == i, order[1, i] * RUN, 0)
    row = lax.broadcasted_iota(jnp.int32, (tile, 1), 0)
    lane = lax.broadcasted_iota(jnp.int32, (RUN, HD), 1)

    def one_tile(t, carry):
        need = order[5, t]
        start = pl.multiple_of(t * tile, tile)
        qpos = lax.rem(row, RUN)
        for i in range(TILE):
            qpos = qpos + jnp.where(lax.div(row, RUN) == i, order[4, t * TILE + i] * RUN, 0)

        def put(a, num, lse):
            for i in range(TILE):
                g = order[3, t * TILE + i]
                o = num[i * RUN : (i + 1) * RUN]
                e = lse[i * RUN : (i + 1) * RUN]
                o_ref[g, :, a * 2 * HD : (a + 1) * 2 * HD] = o.astype(bf16)
                lse_s[g] = jnp.where(lane == head * 2 + a, e, lse_s[g])

        clear = order[4, t * TILE] > order[1, keys - 1]
        cases = [(low, high, False) for low, high in zip((0,) + spans[:-1], spans)] + [(spans[-2], spans[-1], True)]
        for low, high, whole in cases:
            here = (need > low) & (need <= high)
            if high == spans[-1]:
                here = here & (clear if whole else jnp.logical_not(clear))

            @pl.when(here)
            def _(span=high * RUN, whole=whole):
                ss = [
                    lax.dot_general(
                        q_s[pl.ds(start, tile), a * HD : (a + 1) * HD],
                        k_s[:span, a * HD : (a + 1) * HD],
                        (((1,), (1,)), ((), ())),
                        preferred_element_type=f32,
                    )
                    for a in range(2)
                ]
                ps = []
                for a in range(2):
                    s = ss[a] if whole else jnp.where(kpos[:, :span] <= qpos, ss[a], NEG)
                    m = jnp.maximum(jnp.max(s, -1, keepdims=True), FLOOR) * scale
                    p = jnp.exp2(s * scale - m)
                    ps.append((p.astype(bf16), m, jnp.sum(p, -1, keepdims=True)))
                for a in range(2):
                    p, m, total = ps[a]
                    num = jnp.dot(p, v_s[:span, :], preferred_element_type=f32)
                    some = total > 0.0
                    safe = jnp.where(some, total, 1.0)
                    put(a, num * (1.0 / safe), jnp.where(some, m + jnp.log2(safe), NEG))

        @pl.when(need == 0)
        def _():
            for a in range(2):
                put(a, jnp.zeros((tile, 2 * HD), f32), jnp.full((tile, 1), NEG, f32))

        return carry

    lax.fori_loop(0, tiles, one_tile, 0)

    @pl.when(head == pl.num_programs(0) - 1)
    def _():
        lse_ref[...] = jnp.transpose(lse_s[...].reshape(blocks * RUN, HD))[: lse_ref.shape[0], :]


def attend(q_all, kv_parts, spots, spans, rows, heads):
    slots, pad, width = q_all.shape
    blocks = slots * rows // RUN
    keys = len(spots) * rows // RUN
    ins = [pltpu.with_memory_space_constraint(x, pltpu.HBM) for x in kv_parts[:-2]]
    return pl.pallas_call(
        lambda *r: attend_kernel(rows, spans, slots, spots, *r),
        out_shape=[
            jax.ShapeDtypeStruct((blocks, RUN, heads * 4 * HD), bf16),
            jax.ShapeDtypeStruct((8, blocks * RUN), f32),
        ],
        grid_spec=pltpu.PrefetchScalarGridSpec(
            num_scalar_prefetch=0,
            grid=(heads,),
            in_specs=[pl.BlockSpec((slots, pad, 2 * HD), lambda h: (0, 0, h))]
            + [pl.BlockSpec((x.shape[0], 2 * HD), lambda h: (0, h)) for x in kv_parts],
            out_specs=[
                pl.BlockSpec((blocks, RUN, 4 * HD), lambda h: (0, 0, h)),
                pl.BlockSpec((8, blocks * RUN), lambda h: (0, 0)),
            ],
            scratch_shapes=[
                pltpu.VMEM((blocks, RUN, 2 * HD), bf16),
                pltpu.VMEM((keys, RUN, 2 * HD), bf16),
                pltpu.VMEM((keys, RUN, 2 * HD), bf16),
                pltpu.VMEM((blocks * RUN, 2 * HD), bf16),
                pltpu.VMEM((keys * RUN, 2 * HD), bf16),
                pltpu.VMEM((keys * RUN, 2 * HD), bf16),
                pltpu.VMEM((blocks, RUN, HD), f32),
                pltpu.SMEM((6, 128), jnp.int32),
            ],
        ),
        compiler_params=pltpu.CompilerParams(vmem_limit_bytes=36 << 20),
        cost_estimate=pl.CostEstimate(
            flops=heads * 2 * blocks * keys * RUN * RUN * 6 * HD * 8,
            bytes_accessed=(slots * 2 + len(spots) * 2) * rows * heads * 4 * HD,
            transcendentals=heads * 2 * blocks * keys * RUN * RUN,
        ),
        name="attend",
    )(q_all, *ins, *kv_parts[-2:])


def logsum(parts):
    top = parts[0]
    for p in parts[1:]:
        top = jnp.maximum(top, p)
    total = jnp.exp2(parts[0] - top)
    for p in parts[1:]:
        total = total + jnp.exp2(p - top)
    return top + jnp.log2(total)


def merge_kernel(a_ref, b_ref, o_ref):
    o_ref[...] = logsum([a_ref[...], b_ref[...]])


def merge(a, b):
    vm = pl.BlockSpec(memory_space=pltpu.VMEM)
    return pl.pallas_call(
        merge_kernel,
        out_shape=jax.ShapeDtypeStruct(a.shape, a.dtype),
        in_specs=[vm, vm],
        out_specs=vm,
        compiler_params=pltpu.CompilerParams(vmem_limit_bytes=4 << 20),
        name="merge",
    )(a, b)


def weigh_kernel(heads, lam, lse_ref, *refs):
    all_refs, o_ref, out_ref, w_s = refs[:-3], refs[-3], refs[-2], refs[-1]
    j = pl.program_id(0)
    slots, rows = out_ref.shape[:2]

    @pl.when(j == 0)
    def _():
        whole = logsum([r[...] for r in all_refs])
        w = jnp.exp2(lse_ref[...] - whole)
        w = jnp.concatenate([w, jnp.zeros((HD - w.shape[0], w.shape[1]), f32)], 0)
        w_s[...] = jnp.transpose(w)

    for d in range(slots):
        w = w_s[pl.ds(pl.multiple_of((slots * j + d) * rows, rows), rows), :]
        o = o_ref[d * (rows // RUN) : (d + 1) * (rows // RUN)]
        for h in range(heads):
            w1 = w[:, 2 * h : 2 * h + 1]
            w2 = w[:, 2 * h + 1 : 2 * h + 2] * lam[h]
            o1 = o[:, :, h * 4 * HD : h * 4 * HD + 2 * HD].reshape(rows, 2 * HD).astype(f32)
            o2 = o[:, :, h * 4 * HD + 2 * HD : (h + 1) * 4 * HD].reshape(rows, 2 * HD).astype(f32)
            out_ref[d, :, h * 2 * HD : (h + 1) * 2 * HD] = (w1 * o1 - w2 * o2).astype(bf16)


def weigh(lam, lse, lses, o, rows, heads):
    slots = lse.shape[1] // rows
    return pl.pallas_call(
        lambda *r: weigh_kernel(heads, *r),
        out_shape=jax.ShapeDtypeStruct((slots, rows, heads * 2 * HD), bf16),
        grid_spec=pltpu.PrefetchScalarGridSpec(
            num_scalar_prefetch=1,
            grid=(slots // 2,),
            in_specs=[pl.BlockSpec(lse.shape, lambda j, lam: (0, 0))] * (1 + len(lses))
            + [pl.BlockSpec((2 * rows // RUN, RUN, heads * 4 * HD), lambda j, lam: (j, 0, 0))],
            out_specs=pl.BlockSpec((2, rows, heads * 2 * HD), lambda j, lam: (j, 0, 0)),
            scratch_shapes=[pltpu.VMEM((slots * rows, HD), f32)],
        ),
        compiler_params=pltpu.CompilerParams(vmem_limit_bytes=20 << 20),
        name="weigh",
    )(lam, lse, *lses, o)


def norm(got_ref, gain_ref, n_s, heads):
    total = got_ref[0].astype(f32)
    for j in range(1, got_ref.shape[0]):
        total = total + got_ref[j].astype(f32)
    for h in range(heads):
        d = total[:, h * 2 * HD : (h + 1) * 2 * HD]
        mean_square = jnp.mean(d * d, -1, keepdims=True)
        g = gain_ref[0:1, h * 2 * HD : (h + 1) * 2 * HD]
        n_s[:, h * 2 * HD : (h + 1) * 2 * HD] = (out_factor * d / jnp.sqrt(mean_square + norm_eps) * g).astype(bf16)


def project_kernel(heads, kinds, cols, *refs):
    i = pl.program_id(0)
    if heads:
        got_ref, gain_ref, w_ref, *outs, n_ref = refs

        @pl.when(i == 0)
        def _():
            norm(got_ref, gain_ref, n_ref, heads)

    else:
        n_ref, w_ref, *outs = refs
    share = jnp.dot(n_ref[...], w_ref[...], preferred_element_type=f32)
    for j, kind in enumerate(kinds):

        @pl.when(i == j)
        def _(j=j, kind=kind):
            outs[j][...] = share.astype(kind)


def project(cols, ins, weight, rows, kinds, heads=0):
    depth = weight.shape[0]
    width = weight.shape[1] // 4
    whole = lambda x: pl.BlockSpec(x.shape, lambda i, cols: (0,) * len(x.shape))
    outs = [jax.ShapeDtypeStruct((rows, width), kind) for kind in kinds]
    outs += [jax.ShapeDtypeStruct((rows, depth), bf16)] * bool(heads)
    return pl.pallas_call(
        lambda *r: project_kernel(heads, kinds, *r),
        out_shape=outs,
        grid_spec=pltpu.PrefetchScalarGridSpec(
            num_scalar_prefetch=1,
            grid=(len(kinds),),
            in_specs=[whole(x) for x in ins] + [pl.BlockSpec((depth, width), lambda i, cols: (0, cols[i]))],
            out_specs=[whole(x) for x in outs],
        ),
        compiler_params=pltpu.CompilerParams(vmem_limit_bytes=24 << 20),
        cost_estimate=pl.CostEstimate(
            flops=rows * depth * width * 16 * len(kinds), bytes_accessed=depth * width * 2 * len(kinds), transcendentals=0
        ),
        name="project",
    )(cols, *ins, pltpu.with_memory_space_constraint(weight, pltpu.HBM))


def repeat_kernel(x_ref, ids_ref, o_ref, one, sems):
    rows = x_ref.shape[0]
    one[:rows] = x_ref[...]
    one[rows:] = ids_ref[...]
    copies = [pltpu.make_async_copy(one, o_ref.at[i], sems.at[i]) for i in range(o_ref.shape[0])]
    for c in copies:
        c.start()
    for c in copies:
        c.wait()


def repeat(x, ids, count):
    rows, width = x.shape
    shape = (rows + ids.shape[0], width)
    vm = pl.BlockSpec(memory_space=pltpu.VMEM)
    return pl.pallas_call(
        repeat_kernel,
        out_shape=jax.ShapeDtypeStruct((count, *shape), x.dtype),
        in_specs=[vm, vm],
        out_specs=pl.BlockSpec(memory_space=pl.ANY),
        scratch_shapes=[pltpu.VMEM(shape, x.dtype), pltpu.SemaphoreType.DMA((count,))],
        compiler_params=pltpu.CompilerParams(vmem_limit_bytes=2 << 20),
        name="repeat",
    )(x, ids)


def lambda_kernel(x_ref, o_ref):
    first = jnp.sum(x_ref[:, 0] * x_ref[:, 1], -1, keepdims=True)
    second = jnp.sum(x_ref[:, 2] * x_ref[:, 3], -1, keepdims=True)
    o_ref[...] = jnp.broadcast_to(jnp.exp(first) - jnp.exp(second) + lambda_init, o_ref.shape)


def lambdas(x):
    vm = pl.BlockSpec(memory_space=pltpu.VMEM)
    return pl.pallas_call(
        lambda_kernel,
        out_shape=jax.ShapeDtypeStruct((x.shape[0], x.shape[2]), f32),
        in_specs=[vm],
        out_specs=vm,
        cost_estimate=pl.CostEstimate(flops=10**11, bytes_accessed=4 * 10**4, transcendentals=0),
        name="lambdas",
    )(x)


def shift(x, axis, size, step):
    return lax.ppermute(x, axis, [(i, (i + step) % size) for i in range(size)])


def swap(x, axis, size, mask):
    return lax.ppermute(x, axis, [(i, i ^ mask) for i in range(size)])


def per_device(sizes, queries, keys, values, positions, lambda_vecs, head_gain, out_weight, residual):
    nz, nh, ny, nl, nc = sizes
    rows, width = queries.shape
    heads = lambda_vecs.shape[1]
    block = ((positions.astype(f32) + 0.5) * (1.0 / RUN)).astype(jnp.int32).astype(bf16)
    ids = jnp.broadcast_to(jnp.pad(block, (0, width - block.shape[0]))[None, :], (16, width))
    kv_mine = jnp.concatenate([keys, values, ids], 0)
    kv_mine, queries = lax.optimization_barrier((kv_mine, queries))
    q_all = lax.all_to_all(repeat(queries, ids, nh * ny), ("h", "y"), 0, 0)
    up, down = shift(kv_mine, "z", nz, 1), shift(kv_mine, "z", nz, -1)
    kv_parts = [kv_mine, up, down]
    up, down, lam = lax.optimization_barrier((up, down, lambdas(jnp.transpose(lambda_vecs, (1, 0, 2)))))
    for _ in range(2):
        up, down = shift(up, "z", nz, 1), shift(down, "z", nz, -1)
        kv_parts += [up, down]
    kv_parts += [shift(up[:rows], "z", nz, 1), shift(down[rows:], "z", nz, -1)]
    spots = [(i, 0, i, rows) for i in range(nz - 1)] + [(nz - 1, 0, nz, 0)]
    o, lse = attend(q_all, kv_parts, spots, (3, 6, 9, 12, 16), rows, heads)

    pair = merge(lse, swap(lse, "h", nh, 1))
    others = [swap(pair, "y", ny, d) for d in range(1, ny)]

    parts = weigh(lam[:, 0], lse, [pair] + others, o, rows, heads)

    got = lax.all_to_all(parts, ("h", "y"), 0, 0, tiled=False)
    l, c = lax.axis_index("l"), lax.axis_index("c")
    cols = [(r * nc + d).astype(jnp.int32).reshape(1) for r in (1 - l, l) for d in (1 - c, c)]
    send, normed = project(cols[0], [got, head_gain.reshape(1, width)], out_weight, rows, [bf16], heads)
    (keep,) = project(cols[1], [normed], out_weight, rows, [f32])
    away = (keep + swap(send, "c", nc, 1).astype(f32)).astype(bf16)
    away, normed = lax.optimization_barrier((away, normed))
    far = swap(away, "l", nl, 1)
    send, keep = project(jnp.concatenate(cols[2:]), [normed], out_weight, rows, [bf16, f32])
    rest = lax.optimization_barrier(far.astype(f32) + residual.astype(f32))
    return (rest + keep + swap(send, "c", nc, 1).astype(f32)).astype(bf16)


def solution(mesh):
    sizes = (8, 2, 4, 2, 2)
    fine = Mesh(mesh.devices.reshape(sizes), ("z", "h", "y", "l", "c"))
    ctx, tp = ("z", "h", "y"), ("l", "c")
    placed = (
        P(ctx, tp),
        P(ctx, tp),
        P(ctx, tp),
        P(ctx),
        P(None, tp, None),
        P(tp),
        P(tp, None),
        P(ctx, tp),
    )
    return jax.shard_map(
        lambda *a: per_device(sizes, *a), mesh=fine, in_specs=placed, out_specs=P(ctx, tp), check_vma=False
    )
```

```python
import math

import jax
import jax.numpy as jnp
from jax import lax
from jax.experimental import pallas as pl
from jax.experimental.pallas import tpu as pltpu
from jax.sharding import Mesh, PartitionSpec as P

lambda_init = 0.2
out_factor = 0.8
norm_eps = 1e-05

HD = 128
RUN = 72
TILE = 4
NEG = -1e30
FLOOR = -1e29
f32 = jnp.float32
bf16 = jnp.bfloat16


def attend_kernel(rows, spans, slots, spots, *refs):
    q_refs = [refs[0].at[i] for i in range(slots)]
    kv_refs, refs = refs[1:-10], refs[-10:]
    o_ref, lse_ref, q3, k3, v3, q_s, k_s, v_s, lse_s, order = refs
    head = pl.program_id(0)
    per = rows // RUN
    blocks = slots * per
    keys = len(spots) * per
    tile = TILE * RUN
    tiles = blocks // TILE
    scale = math.log2(math.e) / math.sqrt(HD)

    @pl.when(head == 0)
    def _():
        lse_s[...] = jnp.zeros_like(lse_s)
        first = lax.broadcasted_iota(jnp.int32, (16, HD), 0) == 0
        lanes = lax.broadcasted_iota(jnp.int32, (16, HD), 1)

        def numbers(part):
            tail = part[part.shape[0] - 16 :, :HD].astype(f32)
            weight = jnp.where(first & (lanes == 0), float(HD), jnp.where(first & (lanes == RUN), 1.0, 0.0))
            both = jnp.sum(tail * weight).astype(jnp.int32)
            return [lax.div(both, HD), lax.rem(both, HD)]

        kb = [v for k, kr, v, vr in spots for v in numbers(kv_refs[v])]
        qb = [v for p in q_refs for v in numbers(p)]
        for numbered, row in ((kb, 0), (qb, 2)):
            for i in range(len(numbered)):
                rank = jnp.int32(0)
                for j in range(len(numbered)):
                    rank = rank + (numbered[j] < numbered[i]).astype(jnp.int32)
                order[row, i] = rank
                if row == 0:
                    order[1, rank] = numbered[i]
                else:
                    order[3, rank] = i
                    order[4, rank] = numbered[i]
        for t in range(tiles):
            last = order[4, t * TILE + TILE - 1]
            need = jnp.int32(0)
            for j in range(keys):
                need = need + (kb[j] <= last).astype(jnp.int32)
            order[5, t] = need

    for i in range(keys):
        k, kr, v, vr = spots[i // per]
        d = i % per * RUN
        r = order[0, i]
        k3[r] = kv_refs[k][kr + d : kr + d + RUN, :]
        v3[r] = kv_refs[v][vr + d : vr + d + RUN, :]
    for i in range(blocks):
        d = i % per * RUN
        q3[order[2, i]] = q_refs[i // per][d : d + RUN, :]
    for i in range(keys):
        k_s[i * RUN : (i + 1) * RUN, :] = k3[i]
        v_s[i * RUN : (i + 1) * RUN, :] = v3[i]
    for i in range(blocks):
        q_s[i * RUN : (i + 1) * RUN, :] = q3[i]

    col = lax.broadcasted_iota(jnp.int32, (1, keys * RUN), 1)
    kpos = lax.rem(col, RUN)
    for i in range(keys):
        kpos = kpos + jnp.where(lax.div(col, RUN) == i, order[1, i] * RUN, 0)
    row = lax.broadcasted_iota(jnp.int32, (tile, 1), 0)
    lane = lax.broadcasted_iota(jnp.int32, (RUN, HD), 1)

    def one_tile(t, carry):
        need = order[5, t]
        start = pl.multiple_of(t * tile, tile)
        qpos = lax.rem(row, RUN)
        for i in range(TILE):
            qpos = qpos + jnp.where(lax.div(row, RUN) == i, order[4, t * TILE + i] * RUN, 0)

        def put(a, num, lse):
            for i in range(TILE):
                g = order[3, t * TILE + i]
                o = num[i * RUN : (i + 1) * RUN]
                e = lse[i * RUN : (i + 1) * RUN]
                o_ref[g, :, a * 2 * HD : (a + 1) * 2 * HD] = o.astype(bf16)
                lse_s[g] = jnp.where(lane == head * 2 + a, e, lse_s[g])

        clear = order[4, t * TILE] > order[1, keys - 1]
        cases = [(low, high, False) for low, high in zip((0,) + spans[:-1], spans)] + [(spans[-2], spans[-1], True)]
        for low, high, whole in cases:
            here = (need > low) & (need <= high)
            if high == spans[-1]:
                here = here & (clear if whole else jnp.logical_not(clear))

            @pl.when(here)
            def _(span=high * RUN, whole=whole):
                ss = [
                    lax.dot_general(
                        q_s[pl.ds(start, tile), a * HD : (a + 1) * HD],
                        k_s[:span, a * HD : (a + 1) * HD],
                        (((1,), (1,)), ((), ())),
                        preferred_element_type=f32,
                    )
                    for a in range(2)
                ]
                ps = []
                for a in range(2):
                    s = ss[a] if whole else jnp.where(kpos[:, :span] <= qpos, ss[a], NEG)
                    m = jnp.maximum(jnp.max(s, -1, keepdims=True), FLOOR) * scale
                    p = jnp.exp2(s * scale - m)
                    ps.append((p.astype(bf16), m, jnp.sum(p, -1, keepdims=True)))
                for a in range(2):
                    p, m, total = ps[a]
                    num = jnp.dot(p, v_s[:span, :], preferred_element_type=f32)
                    some = total > 0.0
                    safe = jnp.where(some, total, 1.0)
                    put(a, num * (1.0 / safe), jnp.where(some, m + jnp.log2(safe), NEG))

        @pl.when(need == 0)
        def _():
            for a in range(2):
                put(a, jnp.zeros((tile, 2 * HD), f32), jnp.full((tile, 1), NEG, f32))

        return carry

    lax.fori_loop(0, tiles, one_tile, 0)

    @pl.when(head == pl.num_programs(0) - 1)
    def _():
        lse_ref[...] = jnp.transpose(lse_s[...].reshape(blocks * RUN, HD))[: lse_ref.shape[0], :]


def attend(q_all, kv_parts, spots, spans, rows, heads):
    slots, pad, width = q_all.shape
    blocks = slots * rows // RUN
    keys = len(spots) * rows // RUN
    ins = [pltpu.with_memory_space_constraint(x, pltpu.HBM) for x in kv_parts[:-2]]
    return pl.pallas_call(
        lambda *r: attend_kernel(rows, spans, slots, spots, *r),
        out_shape=[
            jax.ShapeDtypeStruct((blocks, RUN, heads * 4 * HD), bf16),
            jax.ShapeDtypeStruct((8, blocks * RUN), f32),
        ],
        grid_spec=pltpu.PrefetchScalarGridSpec(
            num_scalar_prefetch=0,
            grid=(heads,),
            in_specs=[pl.BlockSpec((slots, pad, 2 * HD), lambda h: (0, 0, h))]
            + [pl.BlockSpec((x.shape[0], 2 * HD), lambda h: (0, h)) for x in kv_parts],
            out_specs=[
                pl.BlockSpec((blocks, RUN, 4 * HD), lambda h: (0, 0, h)),
                pl.BlockSpec((8, blocks * RUN), lambda h: (0, 0)),
            ],
            scratch_shapes=[
                pltpu.VMEM((blocks, RUN, 2 * HD), bf16),
                pltpu.VMEM((keys, RUN, 2 * HD), bf16),
                pltpu.VMEM((keys, RUN, 2 * HD), bf16),
                pltpu.VMEM((blocks * RUN, 2 * HD), bf16),
                pltpu.VMEM((keys * RUN, 2 * HD), bf16),
                pltpu.VMEM((keys * RUN, 2 * HD), bf16),
                pltpu.VMEM((blocks, RUN, HD), f32),
                pltpu.SMEM((6, 128), jnp.int32),
            ],
        ),
        compiler_params=pltpu.CompilerParams(vmem_limit_bytes=36 << 20),
        cost_estimate=pl.CostEstimate(
            flops=heads * 2 * blocks * keys * RUN * RUN * 6 * HD * 8,
            bytes_accessed=(slots * 2 + len(spots) * 2) * rows * heads * 4 * HD,
            transcendentals=heads * 2 * blocks * keys * RUN * RUN,
        ),
        name="attend",
    )(q_all, *ins, *kv_parts[-2:])


def logsum(parts):
    top = parts[0]
    for p in parts[1:]:
        top = jnp.maximum(top, p)
    total = jnp.exp2(parts[0] - top)
    for p in parts[1:]:
        total = total + jnp.exp2(p - top)
    return top + jnp.log2(total)


def merge_kernel(a_ref, b_ref, o_ref):
    o_ref[...] = logsum([a_ref[...], b_ref[...]])


def merge(a, b):
    vm = pl.BlockSpec(memory_space=pltpu.VMEM)
    return pl.pallas_call(
        merge_kernel,
        out_shape=jax.ShapeDtypeStruct(a.shape, a.dtype),
        in_specs=[vm, vm],
        out_specs=vm,
        compiler_params=pltpu.CompilerParams(vmem_limit_bytes=4 << 20),
        name="merge",
    )(a, b)


def weigh_kernel(heads, lam, lse_ref, *refs):
    all_refs, o_ref, out_ref, w_s = refs[:-3], refs[-3], refs[-2], refs[-1]
    j = pl.program_id(0)
    slots, rows = out_ref.shape[:2]

    @pl.when(j == 0)
    def _():
        whole = logsum([r[...] for r in all_refs])
        w = jnp.exp2(lse_ref[...] - whole)
        w = jnp.concatenate([w, jnp.zeros((HD - w.shape[0], w.shape[1]), f32)], 0)
        w_s[...] = jnp.transpose(w)

    for d in range(slots):
        w = w_s[pl.ds(pl.multiple_of((slots * j + d) * rows, rows), rows), :]
        o = o_ref[d * (rows // RUN) : (d + 1) * (rows // RUN)]
        for h in range(heads):
            w1 = w[:, 2 * h : 2 * h + 1]
            w2 = w[:, 2 * h + 1 : 2 * h + 2] * lam[h]
            o1 = o[:, :, h * 4 * HD : h * 4 * HD + 2 * HD].reshape(rows, 2 * HD).astype(f32)
            o2 = o[:, :, h * 4 * HD + 2 * HD : (h + 1) * 4 * HD].reshape(rows, 2 * HD).astype(f32)
            out_ref[d, :, h * 2 * HD : (h + 1) * 2 * HD] = (w1 * o1 - w2 * o2).astype(bf16)


def weigh(lam, lse, lses, o, rows, heads):
    slots = lse.shape[1] // rows
    return pl.pallas_call(
        lambda *r: weigh_kernel(heads, *r),
        out_shape=jax.ShapeDtypeStruct((slots, rows, heads * 2 * HD), bf16),
        grid_spec=pltpu.PrefetchScalarGridSpec(
            num_scalar_prefetch=1,
            grid=(slots // 4,),
            in_specs=[pl.BlockSpec(lse.shape, lambda j, lam: (0, 0))] * (1 + len(lses))
            + [pl.BlockSpec((4 * rows // RUN, RUN, heads * 4 * HD), lambda j, lam: (j, 0, 0))],
            out_specs=pl.BlockSpec((4, rows, heads * 2 * HD), lambda j, lam: (j, 0, 0)),
            scratch_shapes=[pltpu.VMEM((slots * rows, HD), f32)],
        ),
        compiler_params=pltpu.CompilerParams(vmem_limit_bytes=20 << 20),
        name="weigh",
    )(lam, lse, *lses, o)


def norm(got_ref, gain_ref, n_s, heads):
    total = got_ref[0].astype(f32)
    for j in range(1, got_ref.shape[0]):
        total = total + got_ref[j].astype(f32)
    for h in range(heads):
        d = total[:, h * 2 * HD : (h + 1) * 2 * HD]
        mean_square = jnp.mean(d * d, -1, keepdims=True)
        g = gain_ref[0:1, h * 2 * HD : (h + 1) * 2 * HD]
        n_s[:, h * 2 * HD : (h + 1) * 2 * HD] = (out_factor * d / jnp.sqrt(mean_square + norm_eps) * g).astype(bf16)


def project_kernel(heads, kinds, cols, *refs):
    i = pl.program_id(0)
    if heads:
        got_ref, gain_ref, w_ref, *outs, n_ref = refs

        @pl.when(i == 0)
        def _():
            norm(got_ref, gain_ref, n_ref, heads)

    else:
        n_ref, w_ref, *outs = refs
    share = jnp.dot(n_ref[...], w_ref[...], preferred_element_type=f32)
    for j, kind in enumerate(kinds):

        @pl.when(i == j)
        def _(j=j, kind=kind):
            outs[j][...] = share.astype(kind)


def project(cols, ins, weight, rows, kinds, heads=0):
    depth = weight.shape[0]
    width = weight.shape[1] // 4
    whole = lambda x: pl.BlockSpec(x.shape, lambda i, cols: (0,) * len(x.shape))
    outs = [jax.ShapeDtypeStruct((rows, width), kind) for kind in kinds]
    outs += [jax.ShapeDtypeStruct((rows, depth), bf16)] * bool(heads)
    return pl.pallas_call(
        lambda *r: project_kernel(heads, kinds, *r),
        out_shape=outs,
        grid_spec=pltpu.PrefetchScalarGridSpec(
            num_scalar_prefetch=1,
            grid=(len(kinds),),
            in_specs=[whole(x) for x in ins] + [pl.BlockSpec((depth, width), lambda i, cols: (0, cols[i]))],
            out_specs=[whole(x) for x in outs],
        ),
        compiler_params=pltpu.CompilerParams(vmem_limit_bytes=24 << 20),
        cost_estimate=pl.CostEstimate(
            flops=rows * depth * width * 16 * len(kinds), bytes_accessed=depth * width * 2 * len(kinds), transcendentals=0
        ),
        name="project",
    )(cols, *ins, pltpu.with_memory_space_constraint(weight, pltpu.HBM))


def repeat_kernel(x_ref, ids_ref, o_ref, one, sems):
    rows = x_ref.shape[0]
    one[:rows] = x_ref[...]
    one[rows:] = ids_ref[...]
    copies = [pltpu.make_async_copy(one, o_ref.at[i], sems.at[i]) for i in range(o_ref.shape[0])]
    for c in copies:
        c.start()
    for c in copies:
        c.wait()


def repeat(x, ids, count):
    rows, width = x.shape
    shape = (rows + ids.shape[0], width)
    vm = pl.BlockSpec(memory_space=pltpu.VMEM)
    return pl.pallas_call(
        repeat_kernel,
        out_shape=jax.ShapeDtypeStruct((count, *shape), x.dtype),
        in_specs=[vm, vm],
        out_specs=pl.BlockSpec(memory_space=pl.ANY),
        scratch_shapes=[pltpu.VMEM(shape, x.dtype), pltpu.SemaphoreType.DMA((count,))],
        compiler_params=pltpu.CompilerParams(vmem_limit_bytes=2 << 20),
        name="repeat",
    )(x, ids)


def lambda_kernel(x_ref, o_ref):
    first = jnp.sum(x_ref[:, 0] * x_ref[:, 1], -1, keepdims=True)
    second = jnp.sum(x_ref[:, 2] * x_ref[:, 3], -1, keepdims=True)
    o_ref[...] = jnp.broadcast_to(jnp.exp(first) - jnp.exp(second) + lambda_init, o_ref.shape)


def lambdas(x):
    vm = pl.BlockSpec(memory_space=pltpu.VMEM)
    return pl.pallas_call(
        lambda_kernel,
        out_shape=jax.ShapeDtypeStruct((x.shape[0], x.shape[2]), f32),
        in_specs=[vm],
        out_specs=vm,
        cost_estimate=pl.CostEstimate(flops=10**11, bytes_accessed=4 * 10**4, transcendentals=0),
        name="lambdas",
    )(x)


def shift(x, axis, size, step):
    return lax.ppermute(x, axis, [(i, (i + step) % size) for i in range(size)])


def swap(x, axis, size, mask):
    return lax.ppermute(x, axis, [(i, i ^ mask) for i in range(size)])


def per_device(sizes, queries, keys, values, positions, lambda_vecs, head_gain, out_weight, residual):
    nz, nh, ny, nl, nc = sizes
    rows, width = queries.shape
    heads = lambda_vecs.shape[1]
    block = ((positions.astype(f32) + 0.5) * (1.0 / RUN)).astype(jnp.int32).astype(bf16)
    ids = jnp.broadcast_to(jnp.pad(block, (0, width - block.shape[0]))[None, :], (16, width))
    kv_mine = jnp.concatenate([keys, values, ids], 0)
    kv_mine, queries = lax.optimization_barrier((kv_mine, queries))
    q_all = lax.all_to_all(repeat(queries, ids, nh * ny), ("h", "y"), 0, 0)
    up, down = shift(kv_mine, "z", nz, 1), shift(kv_mine, "z", nz, -1)
    kv_parts = [kv_mine, up, down]
    up, down, lam = lax.optimization_barrier((up, down, lambdas(jnp.transpose(lambda_vecs, (1, 0, 2)))))
    for _ in range(2):
        up, down = shift(up, "z", nz, 1), shift(down, "z", nz, -1)
        kv_parts += [up, down]
    kv_parts += [shift(up[:rows], "z", nz, 1), shift(down[rows:], "z", nz, -1)]
    spots = [(i, 0, i, rows) for i in range(nz - 1)] + [(nz - 1, 0, nz, 0)]
    o, lse = attend(q_all, kv_parts, spots, (3, 6, 9, 12, 16), rows, heads)

    pair = merge(lse, swap(lse, "h", nh, 1))
    others = [swap(pair, "y", ny, d) for d in range(1, ny)]

    parts = weigh(lam[:, 0], lse, [pair] + others, o, rows, heads)

    got = lax.all_to_all(parts, ("h", "y"), 0, 0, tiled=False)
    l, c = lax.axis_index("l"), lax.axis_index("c")
    cols = [(r * nc + d).astype(jnp.int32).reshape(1) for r in (1 - l, l) for d in (1 - c, c)]
    send, normed = project(cols[0], [got, head_gain.reshape(1, width)], out_weight, rows, [bf16], heads)
    (keep,) = project(cols[1], [normed], out_weight, rows, [f32])
    away = (keep + swap(send, "c", nc, 1).astype(f32)).astype(bf16)
    away, normed = lax.optimization_barrier((away, normed))
    far = swap(away, "l", nl, 1)
    send, keep = project(jnp.concatenate(cols[2:]), [normed], out_weight, rows, [bf16, f32])
    rest = lax.optimization_barrier(far.astype(f32) + residual.astype(f32))
    return (rest + keep + swap(send, "c", nc, 1).astype(f32)).astype(bf16)


def solution(mesh):
    sizes = (8, 2, 4, 2, 2)
    fine = Mesh(mesh.devices.reshape(sizes), ("z", "h", "y", "l", "c"))
    ctx, tp = ("z", "h", "y"), ("l", "c")
    placed = (
        P(ctx, tp),
        P(ctx, tp),
        P(ctx, tp),
        P(ctx),
        P(None, tp, None),
        P(tp),
        P(tp, None),
        P(ctx, tp),
    )
    return jax.shard_map(
        lambda *a: per_device(sizes, *a), mesh=fine, in_specs=placed, out_specs=P(ctx, tp), check_vma=False
    )
```
